32 devices in a mesh: shot: 2 (over core), gy: 4 (over y, x), gx: 4 (over z).
Axes of the slice: x: 2, y: 2, z: 4, core: 2. Of those that a mesh axis runs over, the one named last changes fastest.
Arguments:
- fwd_prev: float32 [2, 4, 1024, 512], P('shot', None, 'gy', 'gx'), may hold values from -6 to 6
- fwd_cur: float32 [2, 4, 1024, 512], P('shot', None, 'gy', 'gx'), may hold values from -6 to 6
- adj_late: float32 [2, 4, 1024, 512], P('shot', None, 'gy', 'gx'), may hold values from -6 to 6
- adj_now: float32 [2, 4, 1024, 512], P('shot', None, 'gy', 'gx'), may hold values from -6 to 6
- courant: float32 [4, 1024, 512], P(None, 'gy', 'gx'), may hold values from 0.02 to 0.19
- wavelet: float32 [2, 2], P('shot'), may hold values from -16 to 16
- boxes: int32 [2, 4], P('shot'), may hold values from 0 to 1024, as said below
- sources: int32 [2, 3], P('shot'), may hold values from 0 to 1023, as said below
- slab_top: int32 [1], replicated, may hold values from 0 to 508
Outputs:
- gradient: float32 [2, 512, 256], P(None, 'gy', 'gx')
The draws below stay inside these ranges and needn't reach their ends.
Inputs may be any that keep to these rules, and one draw needn't show every extreme that they name: `boxes`: shot s's box is y0 <= y < y1, x0 <= x < x1 with y0 < y1 <= 1024, x0 < x1 <= 512, every bound a multiple of 16. `sources`: each shot's source cell (z, y, x) lies in the slab and inside that shot's box.
All inputs are finite; a program needn't handle non-finite values.
Results may differ from the reference program's by a relative error of at most 0.0003.
Values sent between devices are 32-bit elements; how exact they have to be, the bound alone decides.
A program may use at most 128 MiB of HBM per device.

```python
import math
import jax
import jax.numpy as jnp
from jax import lax

BLK = 16
DEPTH = 512
SHOTS = 2
NZ = 4
NY = 1024
NX = 512


def boxes_and_sources(key):
    base_key = jax.random.fold_in(key, 7)
    sub_keys = jax.random.split(base_key, 8)
    blocks_y = NY // BLK
    blocks_x = NX // BLK
    length_y = jax.random.randint(sub_keys[0], (SHOTS,), max(1, blocks_y // 4), blocks_y + 1)
    length_x = jax.random.randint(sub_keys[1], (SHOTS,), max(1, blocks_x // 4), blocks_x + 1)
    widest = jax.random.randint(sub_keys[2], (), 0, SHOTS)
    is_widest = jnp.arange(SHOTS) == widest
    length_y = jnp.where(is_widest, blocks_y, length_y)
    length_x = jnp.where(is_widest, blocks_x, length_x)
    start_y = jax.random.randint(sub_keys[3], (SHOTS,), 0, 1 << 20) % (blocks_y - length_y + 1)
    start_x = jax.random.randint(sub_keys[4], (SHOTS,), 0, 1 << 20) % (blocks_x - length_x + 1)
    low_y = start_y * BLK
    high_y = (start_y + length_y) * BLK
    low_x = start_x * BLK
    high_x = (start_x + length_x) * BLK
    source_y = low_y + jax.random.randint(sub_keys[5], (SHOTS,), 0, 1 << 20) % (high_y - low_y)
    source_x = low_x + jax.random.randint(sub_keys[6], (SHOTS,), 0, 1 << 20) % (high_x - low_x)
    source_z = jax.random.randint(sub_keys[7], (SHOTS,), 0, NZ)
    source_y = jnp.where(is_widest, NY - 1, source_y)
    source_x = jnp.where(is_widest, NX - 1, source_x)
    source_z = jnp.where(is_widest, 0, source_z)
    box_table = jnp.stack([low_y, high_y, low_x, high_x], axis=1).astype(jnp.int32)
    source_table = jnp.stack([source_z, source_y, source_x], axis=1).astype(jnp.int32)
    return (box_table, source_table)


def draw_boxes(key, part):
    return boxes_and_sources(key)[0]


def draw_sources(key, part):
    return boxes_and_sources(key)[1]


def wave_field(key, tag):
    shape = (SHOTS, NZ, NY, NX)
    rough_key = jax.random.fold_in(key, tag)
    return jnp.clip(jax.random.normal(rough_key, shape, jnp.float32), -6.0, 6.0)


def draw_fwd_prev(key, part):
    return wave_field(key, 11)


def draw_fwd_cur(key, part):
    return wave_field(key, 12)


def draw_adj_late(key, part):
    return wave_field(key, 13)


def draw_adj_now(key, part):
    return wave_field(key, 14)


def block_levels(own_key, dims, shards, least, largest):
    factor_of = 1.0
    for axis_at, shards_of in shards:
        draws = jax.random.uniform(jax.random.fold_in(jax.random.fold_in(own_key, 6), axis_at), (shards_of,), jnp.float32, least / len(shards), largest / len(shards))
        factor_of = factor_of * jnp.repeat(jnp.exp(draws), dims[axis_at] // shards_of).reshape((-1,) + (1,) * (len(dims) - 1 - axis_at))
    return factor_of


def noise(key, dims, width, most, cuts=(), held_as=jnp.bfloat16):
    entries = jax.random.normal(key, dims, jnp.float32) * width
    if len(cuts) > 0:
        entries = block_levels(key, dims, cuts, -0.22, 0.18) * entries
    return jnp.clip(entries, min=-most, max=most).astype(held_as)


def setup_inputs(seed: int = 0) -> dict:
    key_of = jax.random.split(jax.random.key(seed), 10)
    return {
        "fwd_prev": draw_fwd_prev(jax.random.fold_in(key_of[9], 71), 0),
        "fwd_cur": draw_fwd_cur(jax.random.fold_in(key_of[9], 71), 0),
        "adj_late": draw_adj_late(jax.random.fold_in(key_of[9], 71), 0),
        "adj_now": draw_adj_now(jax.random.fold_in(key_of[9], 71), 0),
        "courant": jnp.clip(jnp.exp(math.log(0.19) - 2.2512918 * jax.random.uniform(key_of[4], (NZ, NY, NX), jnp.float32) ** block_levels(key_of[4], (NZ, NY, NX), ((1, 4), (2, 4)), -0.2, 0.2)), 0.02, 0.19),
        "wavelet": noise(key_of[5], (SHOTS, 2), 4.0, 16.0, ((0, 2),), jnp.float32),
        "boxes": draw_boxes(jax.random.fold_in(key_of[9], 71), 0),
        "sources": draw_sources(jax.random.fold_in(key_of[9], 71), 0),
        "slab_top": jax.random.randint(key_of[8], (1,), 0, DEPTH - NZ + 1).astype(jnp.int32),
    }


COEFFS = (-205.0 / 72.0, 8.0 / 5.0, -1.0 / 5.0, 8.0 / 315.0, -1.0 / 560.0)


def laplace(field):
    padded = jnp.pad(field, 4)
    depth_count, span_y, span_x = field.shape
    summed = 3.0 * COEFFS[0] * field
    for offset in range(1, 5):
        neighbours = padded[4 + offset:4 + offset + depth_count, 4:4 + span_y, 4:4 + span_x]
        neighbours = neighbours + padded[4 - offset:4 - offset + depth_count, 4:4 + span_y, 4:4 + span_x]
        neighbours = neighbours + padded[4:4 + depth_count, 4 + offset:4 + offset + span_y, 4:4 + span_x]
        neighbours = neighbours + padded[4:4 + depth_count, 4 - offset:4 - offset + span_y, 4:4 + span_x]
        neighbours = neighbours + padded[4:4 + depth_count, 4:4 + span_y, 4 + offset:4 + offset + span_x]
        neighbours = neighbours + padded[4:4 + depth_count, 4:4 + span_y, 4 - offset:4 - offset + span_x]
        summed = summed + COEFFS[offset] * neighbours
    return summed


def reference(fwd_prev, fwd_cur, adj_late, adj_now, courant, wavelet, boxes, sources, slab_top):
    cells_y = jnp.arange(NY).astype(jnp.int32)
    cells_x = jnp.arange(NX).astype(jnp.int32)
    cells_z = jnp.arange(NZ).astype(jnp.int32)

    def one_shot(shot_index):
        shot_box = boxes[shot_index]
        shot_source = sources[shot_index]
        inside_y = ((cells_y >= shot_box[0]) & (cells_y < shot_box[1])).astype(jnp.float32)
        inside_x = ((cells_x >= shot_box[2]) & (cells_x < shot_box[3])).astype(jnp.float32)
        box_mask = (inside_y[:, None] * inside_x[None, :])[None, :, :]
        spike_field = ((cells_z == shot_source[0])[:, None, None] & (cells_y == shot_source[1])[None, :, None]
                       & (cells_x == shot_source[2])[None, None, :]).astype(jnp.float32)
        field_zero = fwd_prev[shot_index]
        field_one = fwd_cur[shot_index]
        field_two = box_mask * (2.0 * field_one - field_zero + courant * laplace(field_one)
                                + wavelet[shot_index, 0] * spike_field)
        field_three = box_mask * (2.0 * field_two - field_one + courant * laplace(field_two)
                                  + wavelet[shot_index, 1] * spike_field)
        adj_three = adj_late[shot_index]
        adj_two = adj_now[shot_index]
        adj_one = box_mask * (2.0 * adj_two - adj_three + courant * laplace(adj_two))
        adj_zero = box_mask * (2.0 * adj_one - adj_two + courant * laplace(adj_one))
        image_cell = (adj_zero * (field_two - 2.0 * field_one + field_zero)
                      + adj_one * (field_three - 2.0 * field_two + field_one))
        return image_cell.reshape(NZ // 2, 2, NY // 2, 2, NX // 2, 2).mean(axis=(1, 3, 5))

    coarse_all = lax.map(one_shot, jnp.arange(SHOTS).astype(jnp.int32))
    summed = jnp.sum(coarse_all, axis=0)
    depth_index = slab_top[0].astype(jnp.float32) + 2.0 * jnp.arange(NZ // 2).astype(jnp.float32) + 1.0
    return summed * (0.25 + depth_index / 128.0)[:, None, None]
```

```python
import functools

import jax
import jax.numpy as jnp
from jax import lax
from jax.experimental import pallas as pl
from jax.experimental.pallas import tpu as pltpu
from jax.sharding import PartitionSpec as P

COEFFS = (-205.0 / 72.0, 8.0 / 5.0, -1.0 / 5.0, 8.0 / 315.0, -1.0 / 560.0)
LEAD = COEFFS[1]
RATIO = (3.0 * COEFFS[0] / LEAD, 1.0, COEFFS[2] / LEAD, COEFFS[3] / LEAD, COEFFS[4] / LEAD)
MESH = pl.DeviceIdType.MESH
PAD = 8
LANES = 128
ROWS = 16
SUB = 8


def kernel(
    shots, counts, wave_hbm, box_hbm, src_hbm, top_hbm, f0_hbm, f1_hbm, a3_hbm, a2_hbm, c_hbm, out_ref,
    wave, box, src, top, now, mid, old, speed, image, yin, yext, own, far, across, xs_out, xs_in,
    corner_out, corner_in, corner_ext, along, joined_x, w_main, w_pack, w_own, w_join, coarse, arrived,
    small_sem, load_sem, ysend, yrecv, xsend, xrecv, csend, crecv, shot_send, shot_recv,
):
    county, countx = counts
    nz, ny = speed.shape[0], speed.shape[1]
    planes = 2 * nz
    half = ny // 2
    groups = ny // ROWS
    gy, gx, shot = lax.axis_index("gy"), lax.axis_index("gx"), lax.axis_index("shot")
    has_up, has_down = gy > 0, gy < county - 1
    has_left, has_right = gx > 0, gx < countx - 1

    loads = []
    for i, (hbm, ref) in enumerate(
        (
            (f1_hbm.at[0], now.at[pl.ds(0, nz)]),
            (a2_hbm.at[0], now.at[pl.ds(nz, nz)]),
            (f0_hbm.at[0], old.at[pl.ds(0, nz)]),
            (a3_hbm.at[0], old.at[pl.ds(nz, nz)]),
            (c_hbm, speed),
        )
    ):
        loads.append(pltpu.make_async_copy(hbm, ref, load_sem.at[i]))
    smalls = []
    for i, (hbm, ref) in enumerate(((wave_hbm, wave), (box_hbm, box), (src_hbm, src), (top_hbm, top))):
        smalls.append(pltpu.make_async_copy(hbm, ref, small_sem.at[i]))
    for copy in loads + smalls:
        copy.start()

    barrier = pltpu.get_barrier_semaphore()
    y_sides = [(has_up, {"gy": gy - 1}), (has_down, {"gy": gy + 1})]
    x_sides = [(has_left, {"gx": gx - 1}), (has_right, {"gx": gx + 1})]
    diagonal = [
        (v & h, {"gy": gy + dy, "gx": gx + dx})
        for v, dy in ((has_up, -1), (has_down, 1))
        for h, dx in ((has_left, -1), (has_right, 1))
    ]
    expected = shots - 1
    for there, device in y_sides + x_sides + diagonal:
        expected = expected + there.astype(jnp.int32)

        @pl.when(there)
        def _(device=device):
            pl.semaphore_signal(barrier, inc=1, device_id=device, device_id_type=MESH)
    for step in range(1, shots):
        pl.semaphore_signal(
            barrier, inc=1, device_id={"shot": lax.rem(shot + step, shots)}, device_id_type=MESH
        )

    for side, (there, _) in enumerate(y_sides):
        @pl.when(jnp.logical_not(there))
        def _(side=side):
            yin[side] = jnp.zeros(yin.shape[1:], jnp.float32)
    for side, (there, _) in enumerate(x_sides):
        @pl.when(jnp.logical_not(there))
        def _(side=side):
            xs_in[side] = jnp.zeros(xs_in.shape[1:], jnp.float32)
    for i, (there, _) in enumerate(diagonal):
        @pl.when(jnp.logical_not(there))
        def _(i=i):
            corner_in[i] = jnp.zeros((SUB, LANES), jnp.float32)

    lane = lax.broadcasted_iota(jnp.int32, (SUB, LANES), 1)
    group = lane >> 3
    spot = lane & 7
    low = spot < 4

    def table(distance, keep):
        weights = jnp.zeros((LANES, LANES), jnp.float32)
        for k in range(1, 5):
            weights = jnp.where(keep & (distance == k), RATIO[k], weights)
        return weights.astype(jnp.bfloat16)

    ri = lax.broadcasted_iota(jnp.int32, (LANES, LANES), 0)
    ci = lax.broadcasted_iota(jnp.int32, (LANES, LANES), 1)
    rj, cj = ri & 7, ci & 7
    rg, cg = ri >> 3, ci >> 3
    always = ri >= 0
    inner_r = jnp.where(rj < 4, rj + (LANES - 4), rj - 4)
    inner_c = jnp.where(cj < 4, cj + (LANES - 4), cj - 4)
    outer_r = jnp.where(rj < 4, rj - 4, rj + (LANES - 4))
    outer_c = jnp.where(cj < 4, cj - 4, cj + (LANES - 4))
    deep_r = jnp.where(rj < 4, rj + 4, rj + (LANES - 12))
    last = groups - 1
    deep_g = jnp.where(rj < 4, rg - 1, rg + 1) & last
    tables = (
        (w_join, 0, table(jnp.abs(outer_r - inner_c), rg == cg)),
        (w_main, 0, table(jnp.abs(ri - ci), always)),
        (w_main, 1, table(jnp.abs(outer_r - ci), always)),
        (w_pack, 0, table(jnp.abs(inner_r - inner_c), rg == cg)),
        (w_pack, 1, table(jnp.abs(deep_r - inner_c), deep_g == cg)),
        (w_own, 0, table(jnp.abs(inner_r - outer_c), rg == cg)),
    )
    for ref, part, weights in tables:
        ref[pl.ds(part * 2 * LANES, LANES)] = weights
        ref[pl.ds(part * 2 * LANES + LANES, LANES)] = weights

    def split(x):
        high = x.astype(jnp.bfloat16)
        return high, (x - high.astype(jnp.float32)).astype(jnp.bfloat16)

    def dot(pieces, weights):
        return jnp.dot(jnp.concatenate(pieces, 1), weights, preferred_element_type=jnp.float32)

    def parts(x):
        return [x[p * ROWS : (p + 1) * ROWS] for p in range(planes)]

    def pack(ref, store, first, count):
        fill = jnp.where(low, group - 1, group + 1) & last

        def body(i, carry):
            p = first + i
            for t in range(2):
                near = jnp.zeros((SUB, LANES), jnp.float32)
                deep = near
                for g in range(groups):
                    moved = pltpu.roll(ref[p, pl.ds(g * ROWS + t * SUB, SUB), :], (8 * g + 4) % LANES, 1)
                    near = jnp.where(group == g, moved, near)
                    if store is not None:
                        deep = jnp.where(fill == g, moved, deep)
                if store is not None:
                    own[p, pl.ds((t + 1) * SUB, SUB), :] = near
                    far[p, pl.ds(t * SUB, SUB), :] = deep
                else:
                    across[p, pl.ds(t * SUB, SUB), :] = near
            return carry

        lax.fori_loop(0, count, body, 0)

    def dense(p, first, second):
        xs_out[1, p] = jnp.where(low, first, pltpu.roll(second, 4, 1))
        xs_out[0, p] = jnp.where(low, pltpu.roll(second, LANES - 4, 1), first)

    def y_copies(side):
        there, device = y_sides[side]
        rows = pl.ds(0, SUB) if side == 0 else pl.ds(ny - SUB, SUB)
        sources = (f1_hbm.at[0], a2_hbm.at[0], f0_hbm.at[0], a3_hbm.at[0], c_hbm)
        return [
            pltpu.make_async_remote_copy(
                src_ref=source.at[:, rows, :], dst_ref=yin.at[1 - side, pl.ds(nz * i, nz)],
                send_sem=ysend.at[side, i], recv_sem=yrecv.at[1 - side, i],
                device_id=device, device_id_type=MESH,
            )
            for i, source in enumerate(sources)
        ]

    def x_copy(side, part):
        device = x_sides[side][1]
        rows = pl.ds(0, planes) if part == 0 else pl.ds(planes, planes + nz)
        return pltpu.make_async_remote_copy(
            src_ref=xs_out.at[side, rows], dst_ref=xs_in.at[1 - side, rows],
            send_sem=xsend.at[side, part], recv_sem=xrecv.at[1 - side, part],
            device_id=device, device_id_type=MESH,
        )

    def corner_copy(i):
        return pltpu.make_async_remote_copy(
            src_ref=corner_out.at[i // 2], dst_ref=corner_in.at[3 - i],
            send_sem=csend.at[i], recv_sem=crecv.at[3 - i],
            device_id=diagonal[i][1], device_id_type=MESH,
        )

    loads[0].wait()
    pack(now, True, 0, nz)
    loads[1].wait()
    pack(now, True, nz, nz)
    upper = jnp.zeros((SUB, LANES), jnp.float32)
    lower = upper
    for p in range(planes):
        t0, t1 = own[p, pl.ds(SUB, SUB), :], own[p, pl.ds(2 * SUB, SUB), :]
        dense(p, t0, t1)
        own[p, pl.ds(0, SUB), :] = jnp.where(group == 0, 0.0, pltpu.roll(t1, 8, 1))
        own[p, pl.ds(3 * SUB, SUB), :] = jnp.where(group == last, 0.0, pltpu.roll(t0, LANES - 8, 1))
        upper = jnp.where(group == p, pltpu.roll(t0, 8 * p, 1) if p else t0, upper)
        lower = jnp.where(group == p, pltpu.roll(t1, 8 * p + 8, 1), lower)
    corner_out[0] = upper
    corner_out[1] = lower

    pl.semaphore_wait(barrier, expected)
    for side in range(2):
        @pl.when(x_sides[side][0])
        def _(side=side):
            x_copy(side, 0).start()
    for side in range(2):
        @pl.when(y_sides[side][0])
        def _(side=side):
            for copy in y_copies(side):
                copy.start()
    for i in range(4):
        @pl.when(diagonal[i][0])
        def _(i=i):
            corner_copy(i).start()

    for copy in smalls:
        copy.wait()
    y0, y1, x0, x1 = box[0, 0], box[0, 1], box[0, 2], box[0, 3]
    sz, sy, sx = src[0, 0], src[0, 1], src[0, 2]

    def inside_of(cell_y, cell_x):
        inside = (cell_x >= x0) & (cell_x < x1) & (cell_y >= y0) & (cell_y < y1)
        return inside, (cell_x == sx) & (cell_y == sy)

    def place(at, rows):
        cell_y = gy * ny + at + lax.broadcasted_iota(jnp.int32, (rows, LANES), 0)
        cell_x = gx * LANES + lax.broadcasted_iota(jnp.int32, (rows, LANES), 1)
        return inside_of(cell_y, cell_x)

    def amplitude(step, z):
        return jnp.where(sz == z, wave[0, step], 0.0)

    def vertical(values, p, total):
        z = p % nz
        for k in range(1, 5):
            s = None
            for d in (z + k, z - k):
                if 0 <= d < nz:
                    s = values[p - z + d] if s is None else s + values[p - z + d]
            if s is not None:
                total[k] = s if total[k] is None else total[k] + s
        return total

    def combine(cells, centre, along_x):
        result = []
        for p in range(planes):
            sums = vertical(centre, p, [None] * 5)
            total = along_x[p] + RATIO[0] * centre[p]
            for k in range(1, 5):
                s = cells(p, k) + cells(p, -k)
                if sums[k] is not None:
                    s = s + sums[k]
                total = total + (s if k == 1 else RATIO[k] * s)
            result.append(total)
        return result

    for load in loads[2:]:
        load.wait()
    pack(old, None, 0, planes)

    def pack_speed(z, carry):
        for t in range(2):
            near = jnp.zeros((SUB, LANES), jnp.float32)
            for g in range(groups):
                moved = pltpu.roll(speed[z, pl.ds(g * ROWS + t * SUB, SUB), :], (8 * g + 4) % LANES, 1)
                near = jnp.where(group == g, moved, near)
            across[planes + z, pl.ds(t * SUB, SUB), :] = near
        return carry

    lax.fori_loop(0, nz, pack_speed, 0)

    lane16 = lax.broadcasted_iota(jnp.int32, (ROWS, LANES), 1)
    row16 = lax.broadcasted_iota(jnp.int32, (ROWS, LANES), 0)
    spot16 = lane16 & 7
    inside_p, source_p = inside_of(
        gy * ny + (lane16 >> 3) * ROWS + row16,
        gx * LANES + jnp.where(spot16 < 4, spot16 + (LANES - 4), spot16 - 4),
    )
    centre = [own[p, pl.ds(SUB, ROWS), :] for p in range(planes)]
    high, rest = split(jnp.concatenate(centre, 0))
    deep_high, deep_rest = split(jnp.concatenate([far[p] for p in range(planes)], 0))
    lap = combine(
        lambda p, k: own[p, pl.ds(SUB + k, ROWS), :], centre,
        parts(dot([high, rest, deep_high, deep_rest], w_pack[...])),
    )
    scaled = [jnp.where(inside_p, LEAD * across[planes + z], 0.0) for z in range(nz)]
    for p in range(planes):
        value = jnp.where(inside_p, 2.0 * centre[p] - across[p], 0.0) + scaled[p % nz] * lap[p]
        if p < nz:
            value = value + jnp.where(source_p, amplitude(0, p), 0.0)
        dense(planes + p, value[:SUB], value[SUB:])
    for z in range(nz):
        dense(2 * planes + z, scaled[z][:SUB], scaled[z][SUB:])
        across[planes + z] = scaled[z]
    for side in range(2):
        @pl.when(x_sides[side][0])
        def _(side=side):
            x_copy(side, 1).start()
    reach = dot([high, rest], w_own[...])
    for p in range(planes):
        across[p] = reach[p * ROWS : (p + 1) * ROWS]

    def sweep(ref, start):
        for p in range(planes):
            along[p] = dot(split(ref[p, pl.ds(start, ny), :]), w_main[pl.ds(0, 2 * LANES)])

    def swept(here):
        return [along[p, here, :] for p in range(planes)]

    def advance(cells, before, courant, along_x, at, first):
        inside, source = place(at, ROWS)
        centre = [cells(p, 0) for p in range(planes)]
        lap = combine(cells, centre, along_x(centre))
        scale = [LEAD * courant(z) for z in range(nz)]
        for p in range(planes):
            new = 2.0 * centre[p] - before(p) + scale[p % nz] * lap[p]
            if p < nz:
                new = new + jnp.where(source, amplitude(0, p), 0.0)
            mid[p, pl.ds(first, ROWS), :] = jnp.where(inside, new, 0.0)

    def first_step(i, carry):
        at = pl.multiple_of(i * ROWS, ROWS) + SUB
        here = pl.ds(at, ROWS)
        advance(
            lambda p, k: now[p, pl.ds(at + k, ROWS), :],
            lambda p: old[p, here, :], lambda z: speed[z, here, :], lambda _: swept(here), at, at + PAD,
        )
        return carry

    sweep(now, 0)
    lax.fori_loop(0, groups - 1, first_step, 0)

    for side, (there, _) in enumerate(x_sides):
        @pl.when(there)
        def _(side=side):
            x_copy(1 - side, 0).wait_recv()

    def spread(p):
        left, right = xs_in[0, p], xs_in[1, p]
        return jnp.concatenate(
            [
                jnp.where(low, left, right),
                jnp.where(low, pltpu.roll(left, LANES - 4, 1), pltpu.roll(right, 4, 1)),
            ],
            0,
        )

    def join(values):
        return parts(dot(split(jnp.concatenate(values, 0)), w_join[...]))

    for p, lack in enumerate(join([spread(p) for p in range(planes)])):
        joined_x[p] = across[planes + p % nz] * lack

    for side, (there, _) in enumerate(y_sides):
        @pl.when(there)
        def _(side=side):
            for copy in y_copies(1 - side):
                copy.wait_recv()
    for p in range(planes):
        yext[0, p, pl.ds(SUB, SUB), :] = yin[0, p]
        yext[0, p, pl.ds(2 * SUB, ROWS), :] = now[p, pl.ds(0, ROWS), :]
        yext[1, p, pl.ds(0, ROWS), :] = now[p, pl.ds(ny - ROWS, ROWS), :]
        yext[1, p, pl.ds(ROWS, SUB), :] = yin[1, p]
    for side in range(2):
        def joined(i, inner, side=side):
            pair = [yin[side, i], inner]
            return jnp.concatenate(pair if side == 0 else pair[::-1], 0)

        edge = pl.ds(0, SUB) if side == 0 else pl.ds(ny - SUB, SUB)
        advance(
            lambda p, k: yext[side, p, pl.ds(SUB + k, ROWS), :],
            lambda p: joined(planes + p, old[p, edge, :]),
            lambda z: joined(2 * planes + z, speed[z, edge, :]),
            lambda centre: parts(dot(split(jnp.concatenate(centre, 0)), w_main[pl.ds(0, 2 * LANES)])),
            -SUB if side == 0 else ny - SUB, 0 if side == 0 else ny,
        )

    edge = (lane < 4) | (lane >= LANES - 4)

    def cross(p, carry):
        for t in range(2):
            packed = joined_x[p, pl.ds(t * SUB, SUB), :]
            for g in range(groups):
                here = pl.ds(g * ROWS + t * SUB + PAD, SUB)
                moved = pltpu.roll(packed, (LANES - 8 * g - 4) % LANES, 1)
                mid[p, here, :] = mid[p, here, :] + jnp.where(edge, moved, 0.0)
        return carry

    lax.fori_loop(0, planes, cross, 0)

    for i in range(4):
        @pl.when(diagonal[i][0])
        def _(i=i):
            corner_copy(3 - i).wait_recv()
    halves = [jnp.where(low, corner_in[2 * v], corner_in[2 * v + 1]) for v in range(2)]
    pieces = [
        jnp.where(group == p, halves[v], 0.0) for v in range(2) for p in range(planes)
    ]
    lack = dot(split(jnp.concatenate(pieces, 0)), w_main[pl.ds(2 * LANES, 2 * LANES)])
    for v in range(2):
        inside, _ = place(-SUB if v == 0 else ny, SUB)
        here = pl.ds(0 if v == 0 else PAD + ny, SUB)
        scale = [jnp.where(inside, LEAD * yin[v, 2 * planes + z], 0.0) for z in range(nz)]
        for p in range(planes):
            at = (v * planes + p) * SUB
            mid[p, here, :] = mid[p, here, :] + scale[p % nz] * lack[at : at + SUB]
    nothing = jnp.zeros((SUB, LANES), jnp.float32)
    corner_ext[0, pl.ds(0, SUB)] = halves[0]
    corner_ext[0, pl.ds(SUB, SUB)] = nothing
    corner_ext[1, pl.ds(0, SUB)] = nothing
    corner_ext[1, pl.ds(SUB, SUB)] = halves[1]
    above, below = None, None
    for k in range(1, 5):
        a = RATIO[k] * corner_ext[0, pl.ds(SUB - k, SUB), :]
        b = RATIO[k] * corner_ext[1, pl.ds(k, SUB), :]
        above, below = (a, b) if k == 1 else (above + a, below + b)

    for side, (there, _) in enumerate(x_sides):
        @pl.when(there)
        def _(side=side):
            x_copy(1 - side, 1).wait_recv()
    scale = [spread(2 * planes + z) for z in range(nz)]
    beyond = []
    for p in range(planes):
        first = jnp.where(group == 0, pltpu.roll(above, (LANES - 8 * p) % LANES, 1) if p else above, 0.0)
        second = jnp.where(group == last, pltpu.roll(below, LANES - 8 - 8 * p, 1) if p < last else below, 0.0)
        reach_p = across[p] + jnp.concatenate([first, second], 0)
        beyond.append(spread(planes + p) + scale[p % nz] * reach_p)
    for p, value in enumerate(join(beyond)):
        joined_x[p] = value
    sweep(mid, PAD)

    edge16 = (lane16 < 4) | (lane16 >= LANES - 4)

    def second_step(g, carry):
        at = pl.multiple_of(g * ROWS, ROWS)
        here, padded = pl.ds(at, ROWS), pl.ds(at + PAD, ROWS)
        inside, source = place(at, ROWS)
        centre = [mid[p, padded, :] for p in range(planes)]
        along_x = [
            x + jnp.where(edge16, pltpu.roll(joined_x[p], LANES - 4 - 8 * g, 1), 0.0)
            for p, x in enumerate(swept(here))
        ]
        lap = combine(lambda p, k: mid[p, pl.ds(at + PAD + k, ROWS), :], centre, along_x)
        total = None
        for z in range(nz):
            c = LEAD * speed[z, here, :]
            f0, f1, a2 = old[z, here, :], now[z, here, :], now[nz + z, here, :]
            f2, a1 = centre[z], centre[nz + z]
            f3 = 2.0 * f2 - f1 + c * lap[z] + jnp.where(source, amplitude(1, z), 0.0)
            f3 = jnp.where(inside, f3, 0.0)
            a0 = jnp.where(inside, 2.0 * a1 - a2 + c * lap[nz + z], 0.0)
            part = a0 * (f2 - 2.0 * f1 + f0) + a1 * (f3 - 2.0 * f2 + f1)
            total = part if z % 2 == 0 else total + part
            if z % 2 == 1:
                image[z // 2, here, :] = total
        return carry

    lax.fori_loop(0, groups, second_step, 0)

    pair = lax.broadcasted_iota(jnp.int32, (LANES, LANES), 0) // 2
    column = lax.broadcasted_iota(jnp.int32, (LANES, LANES), 1)
    total = None
    for k in range(nz // 2):
        rows = image[k, pl.ds(0, half, stride=2), :] + image[k, pl.ds(1, half, stride=2), :]
        pick = (column == pair + 64 * k).astype(jnp.bfloat16)
        left, part = rows, None
        for _ in range(3):
            piece = left.astype(jnp.bfloat16)
            left = left - piece.astype(jnp.float32)
            term = lax.dot_general(
                pick, piece, (((0,), (1,)), ((), ())), preferred_element_type=jnp.float32
            )
            part = term if part is None else part + term
        total = part if total is None else total + part
    coarse[...] = total
    sends = []
    for step in range(1, shots):
        copy = pltpu.make_async_remote_copy(
            src_ref=coarse, dst_ref=arrived.at[step - 1],
            send_sem=shot_send.at[step - 1], recv_sem=shot_recv.at[step - 1],
            device_id={"shot": lax.rem(shot + step, shots)}, device_id_type=MESH,
        )
        copy.start()
        sends.append(copy)
    for side in range(2):
        @pl.when(y_sides[side][0])
        def _(side=side):
            for copy in y_copies(side):
                copy.wait_send()

        @pl.when(x_sides[side][0])
        def _(side=side):
            for part in range(2):
                x_copy(side, part).wait_send()
    for i in range(4):
        @pl.when(diagonal[i][0])
        def _(i=i):
            corner_copy(i).wait_send()
    for step, copy in enumerate(sends):
        copy.wait_recv()
        total = total + arrived[step]
    depth = top[0].astype(jnp.float32)
    for k in range(nz // 2):
        factor = (0.25 + (depth + (2.0 * k + 1.0)) / 128.0) * 0.125
        out_ref[k] = total[64 * k : 64 * k + 64] * factor
    for copy in sends:
        copy.wait_send()


def per_device(shots, counts, fwd_prev, fwd_cur, adj_late, adj_now, courant, wavelet, boxes, sources, slab_top):
    nz, ny, nx = courant.shape
    f32, b16 = jnp.float32, jnp.bfloat16
    planes = 2 * nz
    others = max(shots - 1, 1)
    hbm = pl.BlockSpec(memory_space=pltpu.HBM)
    dma = pltpu.SemaphoreType.DMA
    out = pl.pallas_call(
        functools.partial(kernel, shots, counts),
        out_shape=jax.ShapeDtypeStruct((nz // 2, nx // 2, ny // 2), f32),
        in_specs=[hbm] * 9,
        out_specs=pl.BlockSpec(memory_space=pltpu.VMEM),
        scratch_shapes=[
            pltpu.SMEM((1, 2), f32),
            pltpu.SMEM((1, 4), jnp.int32),
            pltpu.SMEM((1, 3), jnp.int32),
            pltpu.SMEM((1,), jnp.int32),
            pltpu.VMEM((planes, ny, nx), f32),
            pltpu.VMEM((planes, ny + 2 * PAD, nx), f32),
            pltpu.VMEM((planes, ny, nx), f32),
            pltpu.VMEM((nz, ny, nx), f32),
            pltpu.VMEM((nz // 2, ny, nx), f32),
            pltpu.VMEM((2, 2 * planes + nz, SUB, nx), f32),
            pltpu.VMEM((2, planes, 4 * SUB, nx), f32),
            pltpu.VMEM((planes, 4 * SUB, nx), f32),
            pltpu.VMEM((planes, ROWS, nx), f32),
            pltpu.VMEM((planes + nz, ROWS, nx), f32),
            pltpu.VMEM((2, 2 * planes + nz, SUB, nx), f32),
            pltpu.VMEM((2, 2 * planes + nz, SUB, nx), f32),
            pltpu.VMEM((2, SUB, nx), f32),
            pltpu.VMEM((4, SUB, nx), f32),
            pltpu.VMEM((2, ROWS, nx), f32),
            pltpu.VMEM((planes, ny, nx), f32),
            pltpu.VMEM((planes, ROWS, nx), f32),
            pltpu.VMEM((4 * nx, nx), b16),
            pltpu.VMEM((4 * nx, nx), b16),
            pltpu.VMEM((2 * nx, nx), b16),
            pltpu.VMEM((2 * nx, nx), b16),
            pltpu.VMEM((nx, ny // 2), f32),
            pltpu.VMEM((others, nx, ny // 2), f32),
            dma((4,)),
            dma((5,)),
            dma((2, 5)),
            dma((2, 5)),
            dma((2, 2)),
            dma((2, 2)),
            dma((4,)),
            dma((4,)),
            dma((others,)),
            dma((others,)),
        ],
        compiler_params=pltpu.CompilerParams(
            collective_id=0, has_side_effects=True, vmem_limit_bytes=54912 * 1024
        ),
    )(wavelet, boxes, sources, slab_top, fwd_prev, fwd_cur, adj_late, adj_now, courant)
    return jnp.swapaxes(out, 1, 2)


def solution(mesh):
    shots = mesh.shape["shot"]
    counts = (mesh.shape["gy"], mesh.shape["gx"])
    return jax.shard_map(
        functools.partial(per_device, shots, counts),
        mesh=mesh,
        in_specs=(
            P("shot", None, "gy", "gx"),
            P("shot", None, "gy", "gx"),
            P("shot", None, "gy", "gx"),
            P("shot", None, "gy", "gx"),
            P(None, "gy", "gx"),
            P("shot", None),
            P("shot", None),
            P("shot", None),
            P(),
        ),
        out_specs=P(None, "gy", "gx"),
        check_vma=False,
    )
```

```python
import functools

import jax
import jax.numpy as jnp
from jax import lax
from jax.experimental import pallas as pl
from jax.experimental.pallas import tpu as pltpu
from jax.sharding import PartitionSpec as P

COEFFS = (-205.0 / 72.0, 8.0 / 5.0, -1.0 / 5.0, 8.0 / 315.0, -1.0 / 560.0)
LEAD = COEFFS[1]
RATIO = (3.0 * COEFFS[0] / LEAD, 1.0, COEFFS[2] / LEAD, COEFFS[3] / LEAD, COEFFS[4] / LEAD)
MESH = pl.DeviceIdType.MESH
PAD = 8
LANES = 128
ROWS = 16
SUB = 8


def kernel(
    shots, counts, wave_hbm, box_hbm, src_hbm, top_hbm, f0_hbm, f1_hbm, a3_hbm, a2_hbm, c_hbm, out_ref,
    wave, box, src, top, now, mid, old, speed, image, inner, yin, yext, pieces, along, beyond,
    near, bent, reach, held, xs_out, xs_in, corner_out, corner_in, w_main, w_edge, w_join, w_rows, w_ends,
    coarse, arrived,
    small_sem, load_sem, ysend, yrecv, xsend, xrecv, csend, crecv, shot_send, shot_recv,
):
    county, countx = counts
    nz, ny = speed.shape[0], speed.shape[1]
    planes = 2 * nz
    half = ny // 2
    groups = ny // ROWS
    gy, gx, shot = lax.axis_index("gy"), lax.axis_index("gx"), lax.axis_index("shot")
    has_up, has_down = gy > 0, gy < county - 1
    has_left, has_right = gx > 0, gx < countx - 1

    loads = []
    for i, (hbm, ref) in enumerate(
        (
            (f1_hbm.at[0], now.at[pl.ds(0, nz)]),
            (a2_hbm.at[0], now.at[pl.ds(nz, nz)]),
            (c_hbm, speed),
            (f0_hbm.at[0], old.at[pl.ds(0, nz)]),
            (a3_hbm.at[0], old.at[pl.ds(nz, nz)]),
        )
    ):
        loads.append(pltpu.make_async_copy(hbm, ref, load_sem.at[i]))
    smalls = []
    for i, (hbm, ref) in enumerate(((wave_hbm, wave), (box_hbm, box), (src_hbm, src), (top_hbm, top))):
        smalls.append(pltpu.make_async_copy(hbm, ref, small_sem.at[i]))
    for copy in loads[:2] + smalls + loads[2:]:
        copy.start()

    barrier = pltpu.get_barrier_semaphore()
    y_sides = [(has_up, {"gy": gy - 1}), (has_down, {"gy": gy + 1})]
    x_sides = [(has_left, {"gx": gx - 1}), (has_right, {"gx": gx + 1})]
    diagonal = [
        (v & h, {"gy": gy + dy, "gx": gx + dx})
        for v, dy in ((has_up, -1), (has_down, 1))
        for h, dx in ((has_left, -1), (has_right, 1))
    ]
    expected = shots - 1
    for there, device in y_sides + x_sides + diagonal:
        expected = expected + there.astype(jnp.int32)

        @pl.when(there)
        def _(device=device):
            pl.semaphore_signal(barrier, inc=1, device_id=device, device_id_type=MESH)
    for step in range(1, shots):
        pl.semaphore_signal(
            barrier, inc=1, device_id={"shot": lax.rem(shot + step, shots)}, device_id_type=MESH
        )

    for side, (there, _) in enumerate(y_sides):
        @pl.when(jnp.logical_not(there))
        def _(side=side):
            yin[side] = jnp.zeros(yin.shape[1:], jnp.float32)
    for side, (there, _) in enumerate(x_sides):
        @pl.when(jnp.logical_not(there))
        def _(side=side):
            xs_in[side] = jnp.zeros(xs_in.shape[1:], jnp.float32)
    for i, (there, _) in enumerate(diagonal):
        @pl.when(jnp.logical_not(there))
        def _(i=i):
            corner_in[i] = jnp.zeros((SUB, LANES), jnp.float32)

    lane = lax.broadcasted_iota(jnp.int32, (SUB, LANES), 1)
    group = lane >> 3
    low = (lane & 7) < 4

    def iotas(shape):
        return lax.broadcasted_iota(jnp.int32, shape, 0), lax.broadcasted_iota(jnp.int32, shape, 1)

    def table(distance, keep=None):
        weights = jnp.zeros(distance.shape, jnp.float32)
        for k in range(1, 5):
            hit = distance == k
            weights = jnp.where(hit if keep is None else keep & hit, RATIO[k], weights)
        return weights.astype(jnp.bfloat16)

    def inside_column(j):
        return jnp.where(j < 4, j + (LANES - 4), j - 4)

    def outside_column(j):
        return jnp.where(j < 4, j - 4, j + (LANES - 4))

    ri, ci = iotas((LANES, LANES))
    weights = table(jnp.abs(ri - ci))
    w_main[pl.ds(0, LANES)] = weights
    w_main[pl.ds(LANES, LANES)] = weights
    weights = table(jnp.abs(outside_column(ri & 7) - ci))
    w_main[pl.ds(2 * LANES, LANES)] = weights
    w_main[pl.ds(3 * LANES, LANES)] = weights
    ri, ci = iotas((SUB, LANES))
    own_column = inside_column(ri)
    for part, rows in enumerate(
        (
            (own_column == ci).astype(jnp.float32).astype(jnp.bfloat16),
            table(jnp.abs(own_column - ci)),
            table(jnp.abs(outside_column(ri) - ci)),
            jnp.zeros((SUB, LANES), jnp.bfloat16),
        )
    ):
        if part % 2 == 0:
            first = rows
        else:
            both = jnp.concatenate([first.astype(jnp.float32), rows.astype(jnp.float32)], 0)
            both = both.astype(jnp.bfloat16)
            w_edge[pl.ds(part // 2 * ROWS, ROWS), pl.ds(0, LANES)] = both
            w_edge[pl.ds(part // 2 * ROWS, ROWS), pl.ds(LANES, LANES)] = both
    ri, ci = iotas((LANES, 2 * LANES))
    weights = table(jnp.abs(outside_column(ri & 7) - (ci & (LANES - 1)))).astype(jnp.float32)
    plane = (ri >> 3) & (planes - 1)
    for q in range(nz):
        w_join[q] = jnp.where(plane == 2 * q + (ci >> 7), weights, 0.0).astype(jnp.bfloat16)
    ri, ci = iotas((ny, ny))
    w_rows[...] = table(jnp.abs(ri - ci))
    ri, ci = iotas((ROWS, ny))
    weights = table(jnp.abs(jnp.where(ri < SUB, ri - SUB, ri + (ny - SUB)) - ci))
    w_ends[pl.ds(0, ROWS)] = weights
    w_ends[pl.ds(ROWS, ROWS)] = weights

    def split(x):
        high = x.astype(jnp.bfloat16)
        return high, (x - high.astype(jnp.float32)).astype(jnp.bfloat16)

    def dot(pieces, weights):
        return jnp.dot(jnp.concatenate(pieces, 1), weights, preferred_element_type=jnp.float32)

    def edges(rows, cells):
        return lax.dot_general(
            w_edge[pl.ds(0, rows)], cells, (((1,), (1,)), ((), ())), preferred_element_type=jnp.float32
        )

    def parts(x):
        return [x[p * ROWS : (p + 1) * ROWS] for p in range(planes)]

    def hand(i, value):
        xs_out[1, pl.ds(4 * i, 4)] = value[:4]
        xs_out[0, pl.ds(4 * i, 4)] = value[4:]

    def handed(i):
        return jnp.concatenate([xs_in[0, pl.ds(4 * i, 4)], xs_in[1, pl.ds(4 * i, 4)]], 0)

    def turned(values):
        high, rest = split(jnp.concatenate(values, 0))
        both = jnp.concatenate([high.astype(jnp.float32), rest.astype(jnp.float32)], 0)
        return both.T.astype(jnp.bfloat16)

    def y_copies(side):
        there, device = y_sides[side]
        rows = pl.ds(0, SUB) if side == 0 else pl.ds(ny - SUB, SUB)
        sources = (f1_hbm.at[0], a2_hbm.at[0], f0_hbm.at[0], a3_hbm.at[0], c_hbm)
        return [
            pltpu.make_async_remote_copy(
                src_ref=source.at[:, rows, :], dst_ref=yin.at[1 - side, pl.ds(nz * i, nz)],
                send_sem=ysend.at[side, i], recv_sem=yrecv.at[1 - side, i],
                device_id=device, device_id_type=MESH,
            )
            for i, source in enumerate(sources)
        ]

    def x_copy(side, part):
        device = x_sides[side][1]
        rows = pl.ds(0, 4 * planes) if part == 0 else pl.ds(4 * planes, 4 * (planes + nz))
        return pltpu.make_async_remote_copy(
            src_ref=xs_out.at[side, rows], dst_ref=xs_in.at[1 - side, rows],
            send_sem=xsend.at[side, part], recv_sem=xrecv.at[1 - side, part],
            device_id=device, device_id_type=MESH,
        )

    def corner_copy(i):
        return pltpu.make_async_remote_copy(
            src_ref=corner_out.at[i // 2], dst_ref=corner_in.at[3 - i],
            send_sem=csend.at[i], recv_sem=crecv.at[3 - i],
            device_id=diagonal[i][1], device_id_type=MESH,
        )

    for f in range(2):
        loads[f].wait()
        for p in range(f * nz, (f + 1) * nz):
            cells = jnp.concatenate(split(now[p]), 1)
            pieces[p] = cells
            found = edges(2 * ROWS, cells)
            near[p] = found[:SUB]
            bent[p] = found[SUB : 2 * SUB]
            reach[p] = found[2 * SUB : 3 * SUB]
            hand(p, found[:SUB])
    upper = jnp.zeros((SUB, LANES), jnp.float32)
    lower = upper
    for p in range(planes):
        shift = (8 * p + 4) % LANES
        upper = jnp.where(group == p, pltpu.roll(now[p, pl.ds(0, SUB), :], shift, 1), upper)
        lower = jnp.where(group == p, pltpu.roll(now[p, pl.ds(ny - SUB, SUB), :], shift, 1), lower)
    corner_out[0] = upper
    corner_out[1] = lower

    pl.semaphore_wait(barrier, expected)
    for side in range(2):
        @pl.when(x_sides[side][0])
        def _(side=side):
            x_copy(side, 0).start()
    for side in range(2):
        @pl.when(y_sides[side][0])
        def _(side=side):
            for copy in y_copies(side):
                copy.start()
    for i in range(4):
        @pl.when(diagonal[i][0])
        def _(i=i):
            corner_copy(i).start()

    for copy in smalls:
        copy.wait()
    y0, y1, x0, x1 = box[0, 0], box[0, 1], box[0, 2], box[0, 3]
    sz, sy, sx = src[0, 0], src[0, 1], src[0, 2]

    def inside_of(cell_y, cell_x):
        inside = (cell_x >= x0) & (cell_x < x1) & (cell_y >= y0) & (cell_y < y1)
        return inside, (cell_x == sx) & (cell_y == sy)

    def place(at, rows):
        cell_y = gy * ny + at + lax.broadcasted_iota(jnp.int32, (rows, LANES), 0)
        cell_x = gx * LANES + lax.broadcasted_iota(jnp.int32, (rows, LANES), 1)
        return inside_of(cell_y, cell_x)

    def amplitude(step, z):
        return jnp.where(sz == z, wave[0, step], 0.0)

    def vertical(values, p, total):
        z = p % nz
        for k in range(1, 5):
            s = None
            for d in (z + k, z - k):
                if 0 <= d < nz:
                    s = values[p - z + d] if s is None else s + values[p - z + d]
            if s is not None:
                total[k] = s if total[k] is None else total[k] + s
        return total

    def combine(cells, centre, along_x):
        result = []
        for p in range(planes):
            sums = vertical(centre, p, [None] * 5)
            total = along_x[p] + RATIO[0] * centre[p]
            for k in range(1, 5):
                s = cells(p, k) + cells(p, -k)
                if sums[k] is not None:
                    s = s + sums[k]
                total = total + (s if k == 1 else RATIO[k] * s)
            result.append(total)
        return result

    at_y, at_x = iotas((ny, LANES))
    inside, _ = inside_of(gy * ny + at_y, gx * LANES + at_x)
    inner[...] = jnp.where(inside, LEAD, 0.0)
    row, at_y = iotas((SUB, ny))
    inside, source = inside_of(gy * ny + at_y, gx * LANES + inside_column(row))
    loads[2].wait()
    for z in range(nz):
        scaled = speed[z] * inner[...]
        speed[z] = scaled
        found = edges(ROWS, jnp.concatenate(split(scaled), 1))[:SUB]
        held[z] = found
        hand(2 * planes + z, found)
    centre = [near[p] for p in range(planes)]
    high, rest = split(jnp.concatenate(centre, 0))
    along_y = jnp.dot(jnp.concatenate([high, rest], 0), w_rows[...], preferred_element_type=jnp.float32)
    for f in range(2):
        loads[3 + f].wait()
        for z in range(nz):
            p = f * nz + z
            before = edges(ROWS, jnp.concatenate(split(old[p]), 1))[:SUB]
            total = bent[p] + RATIO[0] * centre[p]
            total = total + along_y[p * SUB : (p + 1) * SUB]
            total = total + along_y[(planes + p) * SUB : (planes + p + 1) * SUB]
            for k, s in enumerate(vertical(centre, p, [None] * 5)):
                if s is not None:
                    total = total + (s if k == 1 else RATIO[k] * s)
            value = 2.0 * centre[p] - before
            if f == 0:
                value = value + jnp.where(source, amplitude(0, z), 0.0)
            hand(planes + p, jnp.where(inside, value, 0.0) + held[z] * total)
    for side in range(2):
        @pl.when(x_sides[side][0])
        def _(side=side):
            x_copy(side, 1).start()

    def advance(cells, before, scale, along_x, at, first):
        inside, source = place(at, ROWS)
        centre = [cells(p, 0) for p in range(planes)]
        lap = combine(cells, centre, along_x(centre))
        scales = [scale(z) for z in range(nz)]
        for p in range(planes):
            new = 2.0 * centre[p] - before(p)
            if p < nz:
                new = new + jnp.where(source, amplitude(0, p), 0.0)
            mid[p, pl.ds(first, ROWS), :] = jnp.where(inside, new, 0.0) + scales[p % nz] * lap[p]

    def first_step(i, carry):
        at = pl.multiple_of(i * ROWS, ROWS) + SUB
        here = pl.ds(at, ROWS)
        advance(
            lambda p, k: now[p, pl.ds(at + k, ROWS), :],
            lambda p: old[p, here, :], lambda z: speed[z, here, :],
            lambda _: [along[p, here, :] for p in range(planes)], at, at + PAD,
        )
        return carry

    for p in range(planes):
        along[p] = jnp.dot(pieces[p], w_main[pl.ds(0, 2 * LANES)], preferred_element_type=jnp.float32)
    lax.fori_loop(0, groups - 1, first_step, 0)

    for side, (there, _) in enumerate(y_sides):
        @pl.when(there)
        def _(side=side):
            for copy in y_copies(1 - side):
                copy.wait_recv()
    for p in range(planes):
        yext[0, p, pl.ds(SUB, SUB), :] = yin[0, p]
        yext[0, p, pl.ds(2 * SUB, ROWS), :] = now[p, pl.ds(0, ROWS), :]
        yext[1, p, pl.ds(0, ROWS), :] = now[p, pl.ds(ny - ROWS, ROWS), :]
        yext[1, p, pl.ds(ROWS, SUB), :] = yin[1, p]
    for side in range(2):
        inside, _ = place(-SUB if side == 0 else ny, SUB)
        for z in range(nz):
            i = 2 * planes + z
            yin[side, i] = jnp.where(inside, LEAD * yin[side, i], 0.0)

        def joined(i, inner, side=side):
            pair = [yin[side, i], inner]
            return jnp.concatenate(pair if side == 0 else pair[::-1], 0)

        edge = pl.ds(0, SUB) if side == 0 else pl.ds(ny - SUB, SUB)
        advance(
            lambda p, k: yext[side, p, pl.ds(SUB + k, ROWS), :],
            lambda p: joined(planes + p, old[p, edge, :]),
            lambda z: joined(2 * planes + z, speed[z, edge, :]),
            lambda centre: parts(dot(split(jnp.concatenate(centre, 0)), w_main[pl.ds(0, 2 * LANES)])),
            -SUB if side == 0 else ny - SUB, 0 if side == 0 else ny,
        )

    for side, (there, _) in enumerate(x_sides):
        @pl.when(there)
        def _(side=side):
            x_copy(1 - side, 0).wait_recv()
    body = pl.ds(PAD, ny)
    columns = turned([handed(p) for p in range(planes)])
    for q in range(nz):
        lack = jnp.dot(columns, w_join[q], preferred_element_type=jnp.float32)
        for side in range(2):
            p = 2 * q + side
            mid[p, body, :] = mid[p, body, :] + speed[p % nz] * lack[:, side * LANES : (side + 1) * LANES]

    for i in range(4):
        @pl.when(diagonal[i][0])
        def _(i=i):
            corner_copy(3 - i).wait_recv()
    halves = [jnp.where(low, corner_in[2 * v], corner_in[2 * v + 1]) for v in range(2)]
    masked = [jnp.where(group == p, halves[v], 0.0) for v in range(2) for p in range(planes)]
    lack = dot(split(jnp.concatenate(masked, 0)), w_main[pl.ds(2 * LANES, 2 * LANES)])
    for v in range(2):
        here = pl.ds(0 if v == 0 else PAD + ny, SUB)
        for p in range(planes):
            at = (v * planes + p) * SUB
            mid[p, here, :] = mid[p, here, :] + yin[v, 2 * planes + p % nz] * lack[at : at + SUB]
    high, rest = split(jnp.concatenate(halves, 0))
    ends = lax.dot_general(
        jnp.concatenate([high, rest], 0), w_ends[...], (((0,), (0,)), ((), ())),
        preferred_element_type=jnp.float32,
    )
    for p in range(planes):
        along[p] = dot(split(mid[p, body, :]), w_main[pl.ds(0, 2 * LANES)])

    for side, (there, _) in enumerate(x_sides):
        @pl.when(there)
        def _(side=side):
            x_copy(1 - side, 1).wait_recv()
    scale = [handed(2 * planes + z) for z in range(nz)]
    columns = turned(
        [
            handed(planes + p) + scale[p % nz] * (reach[p] + ends[p * SUB : (p + 1) * SUB])
            for p in range(planes)
        ]
    )
    for q in range(nz):
        found = jnp.dot(columns, w_join[q], preferred_element_type=jnp.float32)
        for side in range(2):
            beyond[2 * q + side] = found[:, side * LANES : (side + 1) * LANES]

    def second_step(g, carry):
        at = pl.multiple_of(g * ROWS, ROWS)
        here, padded = pl.ds(at, ROWS), pl.ds(at + PAD, ROWS)
        inside, source = place(at, ROWS)
        centre = [mid[p, padded, :] for p in range(planes)]
        along_x = [along[p, here, :] + beyond[p, here, :] for p in range(planes)]
        lap = combine(lambda p, k: mid[p, pl.ds(at + PAD + k, ROWS), :], centre, along_x)
        total = None
        for z in range(nz):
            c = speed[z, here, :]
            f0, f1, a2 = old[z, here, :], now[z, here, :], now[nz + z, here, :]
            f2, a1 = centre[z], centre[nz + z]
            f3 = 2.0 * f2 - f1 + jnp.where(source, amplitude(1, z), 0.0)
            f3 = jnp.where(inside, f3, 0.0) + c * lap[z]
            a0 = jnp.where(inside, 2.0 * a1 - a2, 0.0) + c * lap[nz + z]
            part = a0 * (f2 - 2.0 * f1 + f0) + a1 * (f3 - 2.0 * f2 + f1)
            total = part if z % 2 == 0 else total + part
            if z % 2 == 1:
                image[z // 2, here, :] = total
        return carry

    lax.fori_loop(0, groups, second_step, 0)

    pair = lax.broadcasted_iota(jnp.int32, (LANES, LANES), 0) // 2
    column = lax.broadcasted_iota(jnp.int32, (LANES, LANES), 1)
    total = None
    for k in range(nz // 2):
        rows = image[k, pl.ds(0, half, stride=2), :] + image[k, pl.ds(1, half, stride=2), :]
        pick = (column == pair + 64 * k).astype(jnp.bfloat16)
        left, part = rows, None
        for _ in range(3):
            piece = left.astype(jnp.bfloat16)
            left = left - piece.astype(jnp.float32)
            term = lax.dot_general(
                pick, piece, (((0,), (1,)), ((), ())), preferred_element_type=jnp.float32
            )
            part = term if part is None else part + term
        total = part if total is None else total + part
    coarse[...] = total
    sends = []
    for step in range(1, shots):
        copy = pltpu.make_async_remote_copy(
            src_ref=coarse, dst_ref=arrived.at[step - 1],
            send_sem=shot_send.at[step - 1], recv_sem=shot_recv.at[step - 1],
            device_id={"shot": lax.rem(shot + step, shots)}, device_id_type=MESH,
        )
        copy.start()
        sends.append(copy)
    for side in range(2):
        @pl.when(y_sides[side][0])
        def _(side=side):
            for copy in y_copies(side):
                copy.wait_send()

        @pl.when(x_sides[side][0])
        def _(side=side):
            for part in range(2):
                x_copy(side, part).wait_send()
    for i in range(4):
        @pl.when(diagonal[i][0])
        def _(i=i):
            corner_copy(i).wait_send()
    for step, copy in enumerate(sends):
        copy.wait_recv()
        total = total + arrived[step]
    depth = top[0].astype(jnp.float32)
    for k in range(nz // 2):
        factor = (0.25 + (depth + (2.0 * k + 1.0)) / 128.0) * 0.125
        out_ref[k] = total[64 * k : 64 * k + 64] * factor
    for copy in sends:
        copy.wait_send()


def per_device(shots, counts, fwd_prev, fwd_cur, adj_late, adj_now, courant, wavelet, boxes, sources, slab_top):
    nz, ny, nx = courant.shape
    f32, b16 = jnp.float32, jnp.bfloat16
    planes = 2 * nz
    others = max(shots - 1, 1)
    hbm = pl.BlockSpec(memory_space=pltpu.HBM)
    dma = pltpu.SemaphoreType.DMA
    out = pl.pallas_call(
        functools.partial(kernel, shots, counts),
        out_shape=jax.ShapeDtypeStruct((nz // 2, nx // 2, ny // 2), f32),
        in_specs=[hbm] * 9,
        out_specs=pl.BlockSpec(memory_space=pltpu.VMEM),
        scratch_shapes=[
            pltpu.SMEM((1, 2), f32),
            pltpu.SMEM((1, 4), jnp.int32),
            pltpu.SMEM((1, 3), jnp.int32),
            pltpu.SMEM((1,), jnp.int32),
            pltpu.VMEM((planes, ny, nx), f32),
            pltpu.VMEM((planes, ny + 2 * PAD, nx), f32),
            pltpu.VMEM((planes, ny, nx), f32),
            pltpu.VMEM((nz, ny, nx), f32),
            pltpu.VMEM((nz // 2, ny, nx), f32),
            pltpu.VMEM((ny, nx), f32),
            pltpu.VMEM((2, 2 * planes + nz, SUB, nx), f32),
            pltpu.VMEM((2, planes, 4 * SUB, nx), f32),
            pltpu.VMEM((planes, ny, 2 * nx), b16),
            pltpu.VMEM((planes, ny, nx), f32),
            pltpu.VMEM((planes, ny, nx), f32),
            pltpu.VMEM((planes, SUB, ny), f32),
            pltpu.VMEM((planes, SUB, ny), f32),
            pltpu.VMEM((planes, SUB, ny), f32),
            pltpu.VMEM((nz, SUB, ny), f32),
            pltpu.VMEM((2, 4 * (2 * planes + nz), ny), f32),
            pltpu.VMEM((2, 4 * (2 * planes + nz), ny), f32),
            pltpu.VMEM((2, SUB, nx), f32),
            pltpu.VMEM((4, SUB, nx), f32),
            pltpu.VMEM((4 * nx, nx), b16),
            pltpu.VMEM((2 * ROWS, 2 * nx), b16),
            pltpu.VMEM((nz, nx, 2 * nx), b16),
            pltpu.VMEM((ny, ny), b16),
            pltpu.VMEM((2 * ROWS, ny), b16),
            pltpu.VMEM((nx, ny // 2), f32),
            pltpu.VMEM((others, nx, ny // 2), f32),
            dma((4,)),
            dma((5,)),
            dma((2, 5)),
            dma((2, 5)),
            dma((2, 2)),
            dma((2, 2)),
            dma((4,)),
            dma((4,)),
            dma((others,)),
            dma((others,)),
        ],
        compiler_params=pltpu.CompilerParams(
            collective_id=0, has_side_effects=True, vmem_limit_bytes=54912 * 1024
        ),
    )(wavelet, boxes, sources, slab_top, fwd_prev, fwd_cur, adj_late, adj_now, courant)
    return jnp.swapaxes(out, 1, 2)


def solution(mesh):
    shots = mesh.shape["shot"]
    counts = (mesh.shape["gy"], mesh.shape["gx"])
    return jax.shard_map(
        functools.partial(per_device, shots, counts),
        mesh=mesh,
        in_specs=(
            P("shot", None, "gy", "gx"),
            P("shot", None, "gy", "gx"),
            P("shot", None, "gy", "gx"),
            P("shot", None, "gy", "gx"),
            P(None, "gy", "gx"),
            P("shot", None),
            P("shot", None),
            P("shot", None),
            P(),
        ),
        out_specs=P(None, "gy", "gx"),
        check_vma=False,
    )
```

```python
import functools

import jax
import jax.numpy as jnp
from jax import lax
from jax.experimental import pallas as pl
from jax.experimental.pallas import tpu as pltpu
from jax.sharding import PartitionSpec as P

COEFFS = (-205.0 / 72.0, 8.0 / 5.0, -1.0 / 5.0, 8.0 / 315.0, -1.0 / 560.0)
LEAD = COEFFS[1]
RATIO = (3.0 * COEFFS[0] / LEAD, 1.0, COEFFS[2] / LEAD, COEFFS[3] / LEAD, COEFFS[4] / LEAD)
MESH = pl.DeviceIdType.MESH
PAD = 8
LANES = 128
ROWS = 16
SUB = 8


def kernel(
    shots, counts, wave_hbm, box_hbm, src_hbm, top_hbm, f0_hbm, f1_hbm, a3_hbm, a2_hbm, c_hbm, out_ref,
    wave, box, src, top, now, mid, old, speed, image, inner, yin, over, pieces, along,
    near, bent, reach, prior, held, xs_out, xs_in, corner_out, corner_in, w_main, w_edge, w_join, w_rows,
    w_ends, w_back, w_pairs, w_pick, coarse, arrived, patch, patches,
    small_sem, load_sem, ysend, yrecv, xsend, xrecv, csend, crecv, shot_send, shot_recv,
):
    county, countx = counts
    nz, ny = speed.shape[0], speed.shape[1]
    planes = 2 * nz
    half = ny // 2
    groups = ny // ROWS
    gy, gx, shot = lax.axis_index("gy"), lax.axis_index("gx"), lax.axis_index("shot")
    has_up, has_down = gy > 0, gy < county - 1
    has_left, has_right = gx > 0, gx < countx - 1

    loads = []
    for i, (hbm, ref) in enumerate(
        (
            (f1_hbm.at[0], now.at[pl.ds(0, nz), pl.ds(PAD, ny)]),
            (a2_hbm.at[0], now.at[pl.ds(nz, nz), pl.ds(PAD, ny)]),
            (c_hbm, speed),
            (f0_hbm.at[0], old.at[pl.ds(0, nz)]),
            (a3_hbm.at[0], old.at[pl.ds(nz, nz)]),
        )
    ):
        loads.append(pltpu.make_async_copy(hbm, ref, load_sem.at[i]))
    smalls = []
    for i, (hbm, ref) in enumerate(((wave_hbm, wave), (box_hbm, box), (src_hbm, src), (top_hbm, top))):
        smalls.append(pltpu.make_async_copy(hbm, ref, small_sem.at[i]))
    for copy in loads[:2] + smalls + loads[2:]:
        copy.start()

    barrier = pltpu.get_barrier_semaphore()
    y_sides = [(has_up, {"gy": gy - 1}), (has_down, {"gy": gy + 1})]
    x_sides = [(has_left, {"gx": gx - 1}), (has_right, {"gx": gx + 1})]
    diagonal = [
        (v & h, {"gy": gy + dy, "gx": gx + dx})
        for v, dy in ((has_up, -1), (has_down, 1))
        for h, dx in ((has_left, -1), (has_right, 1))
    ]
    expected = shots - 1
    for there, device in y_sides + x_sides + diagonal:
        expected = expected + there.astype(jnp.int32)

        @pl.when(there)
        def _(device=device):
            pl.semaphore_signal(barrier, inc=1, device_id=device, device_id_type=MESH)
    for step in range(1, shots):
        pl.semaphore_signal(
            barrier, inc=1, device_id={"shot": lax.rem(shot + step, shots)}, device_id_type=MESH
        )

    for side, (there, _) in enumerate(y_sides):
        @pl.when(jnp.logical_not(there))
        def _(side=side):
            yin[side] = jnp.zeros(yin.shape[1:], jnp.float32)
    for side, (there, _) in enumerate(x_sides):
        @pl.when(jnp.logical_not(there))
        def _(side=side):
            xs_in[side] = jnp.zeros(xs_in.shape[1:], jnp.float32)
    for i, (there, _) in enumerate(diagonal):
        @pl.when(jnp.logical_not(there))
        def _(i=i):
            corner_in[i] = jnp.zeros((SUB, LANES), jnp.float32)

    for p in range(planes):
        nothing = jnp.zeros((SUB, LANES), jnp.float32)
        now[p, pl.ds(0, PAD), :] = nothing
        now[p, pl.ds(PAD + ny, PAD), :] = nothing
        yin[0, p, pl.ds(SUB, SUB), :] = nothing
        yin[1, p, pl.ds(0, SUB), :] = nothing

    lane = lax.broadcasted_iota(jnp.int32, (SUB, LANES), 1)
    group = lane >> 3
    low = (lane & 7) < 4

    def iotas(shape):
        return lax.broadcasted_iota(jnp.int32, shape, 0), lax.broadcasted_iota(jnp.int32, shape, 1)

    def table(distance, keep=None):
        weights = jnp.zeros(distance.shape, jnp.float32)
        for k in range(1, 5):
            hit = distance == k
            weights = jnp.where(hit if keep is None else keep & hit, RATIO[k], weights)
        return weights.astype(jnp.bfloat16)

    def inside_column(j):
        return jnp.where(j < 4, j + (LANES - 4), j - 4)

    def outside_column(j):
        return jnp.where(j < 4, j - 4, j + (LANES - 4))

    ri, ci = iotas((LANES, LANES))
    weights = table(jnp.abs(ri - ci))
    w_main[pl.ds(0, LANES)] = weights
    w_main[pl.ds(LANES, LANES)] = weights
    weights = table(jnp.abs(outside_column(ri & 7) - ci))
    w_main[pl.ds(2 * LANES, LANES)] = weights
    w_main[pl.ds(3 * LANES, LANES)] = weights
    ri, ci = iotas((SUB, LANES))
    own_column = inside_column(ri)
    for part, rows in enumerate(
        (
            (own_column == ci).astype(jnp.float32).astype(jnp.bfloat16),
            table(jnp.abs(own_column - ci)),
            table(jnp.abs(outside_column(ri) - ci)),
            jnp.zeros((SUB, LANES), jnp.bfloat16),
        )
    ):
        if part % 2 == 0:
            first = rows
        else:
            both = jnp.concatenate([first.astype(jnp.float32), rows.astype(jnp.float32)], 0)
            both = both.astype(jnp.bfloat16)
            w_edge[pl.ds(part // 2 * ROWS, ROWS), pl.ds(0, LANES)] = both
            w_edge[pl.ds(part // 2 * ROWS, ROWS), pl.ds(LANES, LANES)] = both
    ri, ci = iotas((LANES, 2 * LANES))
    weights = table(jnp.abs(outside_column(ri & 7) - (ci & (LANES - 1)))).astype(jnp.float32)
    plane = (ri >> 3) & (planes - 1)
    for q in range(nz):
        w_join[q] = jnp.where(plane == 2 * q + (ci >> 7), weights, 0.0).astype(jnp.bfloat16)
    ri, ci = iotas((ny, ny))
    w_rows[...] = table(jnp.abs(ri - ci))
    ri, ci = iotas((ROWS, ny))
    weights = table(jnp.abs(jnp.where(ri < SUB, ri - SUB, ri + (ny - SUB)) - ci))
    w_ends[pl.ds(0, ROWS)] = weights
    w_ends[pl.ds(ROWS, ROWS)] = weights

    ri, ci = iotas((planes * SUB, LANES))
    weights = table(jnp.abs(inside_column(ri & 7) - outside_column(ci & 7)), ri >> 3 == (ci >> 3 & (planes - 1)))
    w_back[...] = weights
    ri, ci = iotas((ny, half))
    w_pairs[...] = (ri >> 1 == ci).astype(jnp.float32).astype(jnp.bfloat16)
    ri, ci = iotas((LANES, 2 * nz // 2 * LANES))
    hit = (ri & 63 == (ci & (LANES - 1)) >> 1) & (ri >> 6 == ci >> 8)
    w_pick[...] = hit.astype(jnp.float32).astype(jnp.bfloat16)

    def split(x):
        high = x.astype(jnp.bfloat16)
        return high, (x - high.astype(jnp.float32)).astype(jnp.bfloat16)

    def dot(pieces, weights):
        return jnp.dot(jnp.concatenate(pieces, 1), weights, preferred_element_type=jnp.float32)

    def edges(rows, cells):
        return lax.dot_general(
            w_edge[pl.ds(0, rows)], cells, (((1,), (1,)), ((), ())), preferred_element_type=jnp.float32
        )

    def parts(x):
        return [x[p * ROWS : (p + 1) * ROWS] for p in range(planes)]

    def hand(i, value):
        xs_out[1, pl.ds(4 * i, 4)] = value[:4]
        xs_out[0, pl.ds(4 * i, 4)] = value[4:]

    def handed(i):
        return jnp.concatenate([xs_in[0, pl.ds(4 * i, 4)], xs_in[1, pl.ds(4 * i, 4)]], 0)

    def turned(values):
        high, rest = split(jnp.concatenate(values, 0))
        both = jnp.concatenate([high.astype(jnp.float32), rest.astype(jnp.float32)], 0)
        return both.T.astype(jnp.bfloat16)

    def y_copies(side, late):
        start = 0 if side == 0 else ny - 4
        padded, bare = pl.ds(PAD + start, 4), pl.ds(start, 4)
        sources = [(now, padded, planes), (mid, padded, planes), (speed, bare, nz)]
        arrive = pl.ds(SUB, 4) if side == 0 else pl.ds(4, 4)
        return [
            pltpu.make_async_remote_copy(
                src_ref=sources[i][0].at[:, sources[i][1], :],
                dst_ref=yin.at[1 - side, pl.ds(planes * i, sources[i][2]), arrive, :],
                send_sem=ysend.at[side, i], recv_sem=yrecv.at[1 - side, i],
                device_id=y_sides[side][1], device_id_type=MESH,
            )
            for i in ((1, 2) if late else (0,))
        ]

    def y_each(late, action):
        for side in range(2):
            @pl.when(y_sides[side][0])
            def _(side=side):
                for copy in y_copies(side if action != "wait_recv" else 1 - side, late):
                    getattr(copy, action)()

    def x_copy(side, part):
        device = x_sides[side][1]
        rows = pl.ds(0, 4 * planes) if part == 0 else pl.ds(4 * planes, 4 * (planes + nz))
        return pltpu.make_async_remote_copy(
            src_ref=xs_out.at[side, rows], dst_ref=xs_in.at[1 - side, rows],
            send_sem=xsend.at[side, part], recv_sem=xrecv.at[1 - side, part],
            device_id=device, device_id_type=MESH,
        )

    def corner_copy(i):
        return pltpu.make_async_remote_copy(
            src_ref=corner_out.at[i // 2], dst_ref=corner_in.at[3 - i],
            send_sem=csend.at[i], recv_sem=crecv.at[3 - i],
            device_id=diagonal[i][1], device_id_type=MESH,
        )

    body = pl.ds(PAD, ny)
    for f in range(2):
        loads[f].wait()
        for p in range(f * nz, (f + 1) * nz):
            cells = jnp.concatenate(split(now[p, body, :]), 1)
            pieces[p] = cells
            found = edges(2 * ROWS, cells)
            near[p] = found[:SUB]
            bent[p] = found[SUB : 2 * SUB]
            reach[p] = found[2 * SUB : 3 * SUB]
            hand(p, found[:SUB])
    upper = jnp.zeros((SUB, LANES), jnp.float32)
    lower = upper
    for p in range(planes):
        shift = (8 * p + 4) % LANES
        upper = jnp.where(group == p, pltpu.roll(now[p, pl.ds(PAD, SUB), :], shift, 1), upper)
        lower = jnp.where(group == p, pltpu.roll(now[p, pl.ds(ny, SUB), :], shift, 1), lower)
    corner_out[0] = upper
    corner_out[1] = lower

    pl.semaphore_wait(barrier, expected)
    for side in range(2):
        @pl.when(x_sides[side][0])
        def _(side=side):
            x_copy(side, 0).start()
    y_each(False, "start")
    for i in range(4):
        @pl.when(diagonal[i][0])
        def _(i=i):
            corner_copy(i).start()

    for copy in smalls:
        copy.wait()
    y0, y1, x0, x1 = box[0, 0], box[0, 1], box[0, 2], box[0, 3]
    sz, sy, sx = src[0, 0], src[0, 1], src[0, 2]

    def inside_of(cell_y, cell_x):
        inside = (cell_x >= x0) & (cell_x < x1) & (cell_y >= y0) & (cell_y < y1)
        return inside, (cell_x == sx) & (cell_y == sy)

    def place(at, rows):
        cell_y = gy * ny + at + lax.broadcasted_iota(jnp.int32, (rows, LANES), 0)
        cell_x = gx * LANES + lax.broadcasted_iota(jnp.int32, (rows, LANES), 1)
        return inside_of(cell_y, cell_x)

    def amplitude(step, z):
        return jnp.where(sz == z, wave[0, step], 0.0)

    def vertical(values, p, total):
        z = p % nz
        for k in range(1, 5):
            s = None
            for d in (z + k, z - k):
                if 0 <= d < nz:
                    s = values[p - z + d] if s is None else s + values[p - z + d]
            if s is not None:
                total[k] = s if total[k] is None else total[k] + s
        return total

    def combine(cells, centre, along_x):
        result = []
        for p in range(planes):
            sums = vertical(centre, p, [None] * 5)
            total = along_x[p] + RATIO[0] * centre[p]
            for k in range(1, 5):
                s = cells(p, k) + cells(p, -k)
                if sums[k] is not None:
                    s = s + sums[k]
                total = total + (s if k == 1 else RATIO[k] * s)
            result.append(total)
        return result

    at_y, at_x = iotas((ny, LANES))
    inside, _ = inside_of(gy * ny + at_y, gx * LANES + at_x)
    inner[...] = jnp.where(inside, LEAD, 0.0)
    row, at_y = iotas((SUB, ny))
    inside, source = inside_of(gy * ny + at_y, gx * LANES + inside_column(row))
    loads[2].wait()
    for z in range(nz):
        scaled = speed[z] * inner[...]
        speed[z] = scaled
        found = edges(ROWS, jnp.concatenate(split(scaled), 1))[:SUB]
        held[z] = found
        hand(2 * planes + z, found)
    tips = [pieces[p, pl.ds(at, ROWS), :] for at in (0, ny - ROWS) for p in range(planes)]
    tips = jnp.dot(jnp.concatenate(tips, 0), w_main[pl.ds(0, 2 * LANES)], preferred_element_type=jnp.float32)
    centre = [near[p] for p in range(planes)]
    high, rest = split(jnp.concatenate(centre, 0))
    along_y = jnp.dot(jnp.concatenate([high, rest], 0), w_rows[...], preferred_element_type=jnp.float32)
    for f in range(2):
        loads[3 + f].wait()
        for z in range(nz):
            p = f * nz + z
            before = edges(ROWS, jnp.concatenate(split(old[p]), 1))[:SUB]
            prior[p] = before
            total = bent[p] + RATIO[0] * centre[p]
            total = total + along_y[p * SUB : (p + 1) * SUB]
            total = total + along_y[(planes + p) * SUB : (planes + p + 1) * SUB]
            for k, s in enumerate(vertical(centre, p, [None] * 5)):
                if s is not None:
                    total = total + (s if k == 1 else RATIO[k] * s)
            value = 2.0 * centre[p] - before
            if f == 0:
                value = value + jnp.where(source, amplitude(0, z), 0.0)
            hand(planes + p, jnp.where(inside, value, 0.0) + held[z] * total)

    def advance(at, along_x):
        inside, source = place(at, ROWS)
        here = pl.ds(at, ROWS)
        cells = lambda p, k: now[p, pl.ds(at + PAD + k, ROWS), :]
        centre = [cells(p, 0) for p in range(planes)]
        lap = combine(cells, centre, along_x)
        scales = [speed[z, here, :] for z in range(nz)]
        for p in range(planes):
            new = 2.0 * centre[p] - old[p, here, :]
            if p < nz:
                new = new + jnp.where(source, amplitude(0, p), 0.0)
            mid[p, pl.ds(at + PAD, ROWS), :] = jnp.where(inside, new, 0.0) + scales[p % nz] * lap[p]

    advance(0, parts(tips[: planes * ROWS]))
    advance(ny - ROWS, parts(tips[planes * ROWS :]))
    for side in range(2):
        @pl.when(x_sides[side][0])
        def _(side=side):
            x_copy(side, 1).start()

    y_each(True, "start")

    def first_step(i, carry):
        at = pl.multiple_of(i * ROWS, ROWS)
        advance(at, [along[p, pl.ds(at, ROWS), :] for p in range(planes)])
        return carry

    for p in range(planes):
        along[p] = jnp.dot(pieces[p], w_main[pl.ds(0, 2 * LANES)], preferred_element_type=jnp.float32)
    lax.fori_loop(1, groups - 1, first_step, 0)

    for p in range(planes):
        for v in range(2):
            total = None
            for k in range(1, 5):
                term = RATIO[k] * now[p, pl.ds(k if v == 0 else PAD + ny - k, SUB), :]
                total = term if total is None else total + term
            over[v, p] = total

    y_each(True, "wait_send")
    for side, (there, _) in enumerate(x_sides):
        @pl.when(there)
        def _(side=side):
            x_copy(1 - side, 0).wait_recv()
    y_each(False, "wait_recv")
    columns = turned([handed(p) for p in range(planes)])
    for q in range(nz):
        lack = jnp.dot(columns, w_join[q], preferred_element_type=jnp.float32)
        for side in range(2):
            p = 2 * q + side
            mid[p, body, :] = mid[p, body, :] + speed[p % nz] * lack[:, side * LANES : (side + 1) * LANES]
    for p in range(planes):
        for v in range(2):
            total = None
            for k in range(1, 5):
                term = RATIO[k] * yin[v, p, pl.ds(SUB - k if v == 0 else k, SUB), :]
                total = term if total is None else total + term
            at = 0 if v == 0 else ny - SUB
            here = pl.ds(PAD + at, SUB)
            mid[p, here, :] = mid[p, here, :] + speed[p % nz, pl.ds(at, SUB), :] * total
    for p in range(planes):
        cells = jnp.concatenate(split(mid[p, body, :]), 1)
        along[p] = jnp.dot(cells, w_main[pl.ds(0, 2 * LANES)], preferred_element_type=jnp.float32)
        found = edges(ROWS, cells)[:SUB]
        bent[p] = found - 2.0 * near[p] + prior[p] if p < nz else found

    def second_step(g, carry):
        at = pl.multiple_of(g * ROWS, ROWS)
        here, padded = pl.ds(at, ROWS), pl.ds(at + PAD, ROWS)
        inside, source = place(at, ROWS)
        centre = [mid[p, padded, :] for p in range(planes)]
        along_x = [along[p, here, :] for p in range(planes)]
        lap = combine(lambda p, k: mid[p, pl.ds(at + PAD + k, ROWS), :], centre, along_x)
        total = None
        for z in range(nz):
            c = speed[z, here, :]
            f0, f1, a2 = old[z, here, :], now[z, padded, :], now[nz + z, padded, :]
            f2, a1 = centre[z], centre[nz + z]
            f3 = 2.0 * f2 - f1 + jnp.where(source, amplitude(1, z), 0.0)
            f3 = jnp.where(inside, f3, 0.0) + c * lap[z]
            a0 = jnp.where(inside, 2.0 * a1 - a2, 0.0) + c * lap[nz + z]
            part = a0 * (f2 - 2.0 * f1 + f0) + a1 * (f3 - 2.0 * f2 + f1)
            total = part if z % 2 == 0 else total + part
            if z % 2 == 1:
                image[z // 2, here, :] = total
        return carry

    lax.fori_loop(1, groups - 1, second_step, 0)

    for i in range(4):
        @pl.when(diagonal[i][0])
        def _(i=i):
            corner_copy(3 - i).wait_recv()
    halves = [jnp.where(low, corner_in[2 * v], corner_in[2 * v + 1]) for v in range(2)]
    masked = [jnp.where(group == p, halves[v], 0.0) for v in range(2) for p in range(planes)]
    lack = dot(split(jnp.concatenate(masked, 0)), w_main[pl.ds(2 * LANES, 2 * LANES)])
    high, rest = split(jnp.concatenate(halves, 0))
    ends = lax.dot_general(
        jnp.concatenate([high, rest], 0), w_ends[...], (((0,), (0,)), ((), ())),
        preferred_element_type=jnp.float32,
    )
    for p in range(planes):
        reach[p] = reach[p] + ends[p * SUB : (p + 1) * SUB]
    y_each(True, "wait_recv")
    for v in range(2):
        here = pl.ds(0 if v == 0 else PAD + ny, SUB)
        rows = pl.ds(0 if v == 0 else SUB, SUB)
        for p in range(planes):
            at = (v * planes + p) * SUB
            extra = over[v, p] + lack[at : at + SUB]
            mid[p, here, :] = yin[v, planes + p, rows, :] + yin[v, 2 * planes + p % nz, rows, :] * extra
    second_step(0, 0)
    second_step(groups - 1, 0)

    rows = [
        image[k, pl.ds(0, half, stride=2), :] + image[k, pl.ds(1, half, stride=2), :] for k in range(nz // 2)
    ]
    cells = jnp.concatenate([x for k in range(nz // 2) for x in split(rows[k])], 1)
    total = lax.dot_general(
        w_pick[...], cells, (((1,), (1,)), ((), ())), preferred_element_type=jnp.float32
    )
    coarse[...] = total

    def exchange(ref, into, lane_of):
        copies = []
        for step in range(1, shots):
            copy = pltpu.make_async_remote_copy(
                src_ref=ref, dst_ref=into.at[step - 1],
                send_sem=shot_send.at[lane_of, step - 1], recv_sem=shot_recv.at[lane_of, step - 1],
                device_id={"shot": lax.rem(shot + step, shots)}, device_id_type=MESH,
            )
            copy.start()
            copies.append(copy)
        return copies

    sends = exchange(coarse, arrived, 0)

    for side, (there, _) in enumerate(x_sides):
        @pl.when(there)
        def _(side=side):
            x_copy(1 - side, 1).wait_recv()
    outer = jnp.concatenate(
        [handed(planes + p) + handed(2 * planes + p % nz) * reach[p] for p in range(planes)], 0
    )
    lack = jnp.dot(w_back[...], jnp.concatenate(split(outer), 0), preferred_element_type=jnp.float32)
    fixes = []
    for z in range(nz):
        f, a = lack[z * SUB : (z + 1) * SUB], lack[(nz + z) * SUB : (nz + z + 1) * SUB]
        fixes.append(held[z] * (a * bent[z] + bent[nz + z] * f))
    fixes = jnp.concatenate([fixes[2 * k] + fixes[2 * k + 1] for k in range(nz // 2)], 0)
    both = jnp.dot(jnp.concatenate(split(fixes), 0), w_pairs[...], preferred_element_type=jnp.float32)
    fixes = both[: nz // 2 * SUB] + both[nz // 2 * SUB :]
    patch[...] = fixes
    sends = sends + exchange(patch, patches, 1)

    y_each(False, "wait_send")
    for side in range(2):
        @pl.when(x_sides[side][0])
        def _(side=side):
            for part in range(2):
                x_copy(side, part).wait_send()
    for i in range(4):
        @pl.when(diagonal[i][0])
        def _(i=i):
            corner_copy(i).wait_send()
    for copy in sends:
        copy.wait_recv()
    for step in range(shots - 1):
        total = total + arrived[step]
        fixes = fixes + patches[step]
    depth = top[0].astype(jnp.float32)
    width = LANES // 2
    for k in range(nz // 2):
        factor = (0.25 + (depth + (2.0 * k + 1.0)) / 128.0) * 0.125
        out_ref[k] = total[width * k : width * k + width] * factor
        for i, at in enumerate((width - 2, width - 1, 0, 1)):
            first = k * SUB + 2 * i
            row = (fixes[first : first + 1] + fixes[first + 1 : first + 2]) * factor
            out_ref[k, pl.ds(at, 1), :] = out_ref[k, pl.ds(at, 1), :] + row
    for copy in sends:
        copy.wait_send()


def per_device(shots, counts, fwd_prev, fwd_cur, adj_late, adj_now, courant, wavelet, boxes, sources, slab_top):
    nz, ny, nx = courant.shape
    f32, b16 = jnp.float32, jnp.bfloat16
    planes = 2 * nz
    others = max(shots - 1, 1)
    hbm = pl.BlockSpec(memory_space=pltpu.HBM)
    dma = pltpu.SemaphoreType.DMA
    out = pl.pallas_call(
        functools.partial(kernel, shots, counts),
        out_shape=jax.ShapeDtypeStruct((nz // 2, nx // 2, ny // 2), f32),
        in_specs=[hbm] * 9,
        out_specs=pl.BlockSpec(memory_space=pltpu.VMEM),
        scratch_shapes=[
            pltpu.SMEM((1, 2), f32),
            pltpu.SMEM((1, 4), jnp.int32),
            pltpu.SMEM((1, 3), jnp.int32),
            pltpu.SMEM((1,), jnp.int32),
            pltpu.VMEM((planes, ny + 2 * PAD, nx), f32),
            pltpu.VMEM((planes, ny + 2 * PAD, nx), f32),
            pltpu.VMEM((planes, ny, nx), f32),
            pltpu.VMEM((nz, ny, nx), f32),
            pltpu.VMEM((nz // 2, ny, nx), f32),
            pltpu.VMEM((ny, nx), f32),
            pltpu.VMEM((2, 2 * planes + nz, ROWS, nx), f32),
            pltpu.VMEM((2, planes, SUB, nx), f32),
            pltpu.VMEM((planes, ny, 2 * nx), b16),
            pltpu.VMEM((planes, ny, nx), f32),
            pltpu.VMEM((planes, SUB, ny), f32),
            pltpu.VMEM((planes, SUB, ny), f32),
            pltpu.VMEM((planes, SUB, ny), f32),
            pltpu.VMEM((planes, SUB, ny), f32),
            pltpu.VMEM((nz, SUB, ny), f32),
            pltpu.VMEM((2, 4 * (2 * planes + nz), ny), f32),
            pltpu.VMEM((2, 4 * (2 * planes + nz), ny), f32),
            pltpu.VMEM((2, SUB, nx), f32),
            pltpu.VMEM((4, SUB, nx), f32),
            pltpu.VMEM((4 * nx, nx), b16),
            pltpu.VMEM((2 * ROWS, 2 * nx), b16),
            pltpu.VMEM((nz, nx, 2 * nx), b16),
            pltpu.VMEM((ny, ny), b16),
            pltpu.VMEM((2 * ROWS, ny), b16),
            pltpu.VMEM((planes * SUB, nx), b16),
            pltpu.VMEM((ny, ny // 2), b16),
            pltpu.VMEM((nx, nz * nx), b16),
            pltpu.VMEM((nx, ny // 2), f32),
            pltpu.VMEM((others, nx, ny // 2), f32),
            pltpu.VMEM((nz // 2 * SUB, ny // 2), f32),
            pltpu.VMEM((others, nz // 2 * SUB, ny // 2), f32),
            dma((4,)),
            dma((5,)),
            dma((2, 3)),
            dma((2, 3)),
            dma((2, 2)),
            dma((2, 2)),
            dma((4,)),
            dma((4,)),
            dma((2, others)),
            dma((2, others)),
        ],
        compiler_params=pltpu.CompilerParams(
            collective_id=0, has_side_effects=True, vmem_limit_bytes=54912 * 1024
        ),
    )(wavelet, boxes, sources, slab_top, fwd_prev, fwd_cur, adj_late, adj_now, courant)
    return jnp.swapaxes(out, 1, 2)


def solution(mesh):
    shots = mesh.shape["shot"]
    counts = (mesh.shape["gy"], mesh.shape["gx"])
    return jax.shard_map(
        functools.partial(per_device, shots, counts),
        mesh=mesh,
        in_specs=(
            P("shot", None, "gy", "gx"),
            P("shot", None, "gy", "gx"),
            P("shot", None, "gy", "gx"),
            P("shot", None, "gy", "gx"),
            P(None, "gy", "gx"),
            P("shot", None),
            P("shot", None),
            P("shot", None),
            P(),
        ),
        out_specs=P(None, "gy", "gx"),
        check_vma=False,
    )
```

```python
import functools

import jax
import jax.numpy as jnp
from jax import lax
from jax.experimental import pallas as pl
from jax.experimental.pallas import tpu as pltpu
from jax.sharding import PartitionSpec as P

COEFFS = (-205.0 / 72.0, 8.0 / 5.0, -1.0 / 5.0, 8.0 / 315.0, -1.0 / 560.0)
LEAD = COEFFS[1]
RATIO = (3.0 * COEFFS[0] / LEAD, 1.0, COEFFS[2] / LEAD, COEFFS[3] / LEAD, COEFFS[4] / LEAD)
MESH = pl.DeviceIdType.MESH
PAD = 8
LANES = 128
ROWS = 16
SUB = 8


def kernel(
    shots, counts, wave_hbm, box_hbm, src_hbm, top_hbm, f0_hbm, f1_hbm, a3_hbm, a2_hbm, c_hbm, out_ref,
    wave, box, src, top, now, mid, old, speed, image, inner, yin, over, pieces, along,
    near, bent, reach, prior, held, middle, deep_bent, deep_late, deep_held, deep_sums, xs_out, xs_in, corner_out, corner_in, w_main, w_edge, w_join, w_rows,
    w_ends, w_back, w_near, w_pairs, w_pick, coarse, arrived, patch, patches,
    small_sem, load_sem, ysend, yrecv, xsend, xrecv, csend, crecv, shot_send, shot_recv,
):
    county, countx = counts
    nz, ny = speed.shape[0], speed.shape[1]
    planes = 2 * nz
    half = ny // 2
    groups = ny // ROWS
    gy, gx, shot = lax.axis_index("gy"), lax.axis_index("gx"), lax.axis_index("shot")
    has_up, has_down = gy > 0, gy < county - 1
    has_left, has_right = gx > 0, gx < countx - 1

    loads = []
    for i, (hbm, ref) in enumerate(
        (
            (f1_hbm.at[0], now.at[pl.ds(0, nz), pl.ds(PAD, ny)]),
            (a2_hbm.at[0], now.at[pl.ds(nz, nz), pl.ds(PAD, ny)]),
            (c_hbm, speed),
            (f0_hbm.at[0], old.at[pl.ds(0, nz)]),
            (a3_hbm.at[0], old.at[pl.ds(nz, nz)]),
        )
    ):
        loads.append(pltpu.make_async_copy(hbm, ref, load_sem.at[i]))
    smalls = []
    for i, (hbm, ref) in enumerate(((wave_hbm, wave), (box_hbm, box), (src_hbm, src), (top_hbm, top))):
        smalls.append(pltpu.make_async_copy(hbm, ref, small_sem.at[i]))
    for copy in loads[:2] + smalls + loads[2:]:
        copy.start()

    barrier = pltpu.get_barrier_semaphore()
    y_sides = [(has_up, {"gy": gy - 1}), (has_down, {"gy": gy + 1})]
    x_sides = [(has_left, {"gx": gx - 1}), (has_right, {"gx": gx + 1})]
    diagonal = [
        (v & h, {"gy": gy + dy, "gx": gx + dx})
        for v, dy in ((has_up, -1), (has_down, 1))
        for h, dx in ((has_left, -1), (has_right, 1))
    ]
    expected = shots - 1
    for there, device in y_sides + x_sides + diagonal:
        expected = expected + there.astype(jnp.int32)

        @pl.when(there)
        def _(device=device):
            pl.semaphore_signal(barrier, inc=1, device_id=device, device_id_type=MESH)
    for step in range(1, shots):
        pl.semaphore_signal(
            barrier, inc=1, device_id={"shot": lax.rem(shot + step, shots)}, device_id_type=MESH
        )

    for side, (there, _) in enumerate(y_sides):
        @pl.when(jnp.logical_not(there))
        def _(side=side):
            yin[side] = jnp.zeros(yin.shape[1:], jnp.float32)
    for side, (there, _) in enumerate(x_sides):
        @pl.when(jnp.logical_not(there))
        def _(side=side):
            xs_in[side] = jnp.zeros(xs_in.shape[1:], jnp.float32)
    for i, (there, _) in enumerate(diagonal):
        @pl.when(jnp.logical_not(there))
        def _(i=i):
            corner_in[i] = jnp.zeros((SUB, LANES), jnp.float32)

    for p in range(planes):
        nothing = jnp.zeros((SUB, LANES), jnp.float32)
        now[p, pl.ds(0, PAD), :] = nothing
        now[p, pl.ds(PAD + ny, PAD), :] = nothing
        yin[0, p, pl.ds(SUB, SUB), :] = nothing
        yin[1, p, pl.ds(0, SUB), :] = nothing

    lane = lax.broadcasted_iota(jnp.int32, (SUB, LANES), 1)
    group = lane >> 3
    low = (lane & 7) < 4

    def iotas(shape):
        return lax.broadcasted_iota(jnp.int32, shape, 0), lax.broadcasted_iota(jnp.int32, shape, 1)

    def table(distance, keep=None):
        weights = jnp.zeros(distance.shape, jnp.float32)
        for k in range(1, 5):
            hit = distance == k
            weights = jnp.where(hit if keep is None else keep & hit, RATIO[k], weights)
        return weights.astype(jnp.bfloat16)

    def inside_column(j):
        return jnp.where(j < 4, j + (LANES - 4), j - 4)

    def outside_column(j):
        return jnp.where(j < 4, j - 4, j + (LANES - 4))

    def deep_inside(j):
        return jnp.where(j < 4, j + (LANES - 8), j)

    ri, ci = iotas((LANES, LANES))
    weights = table(jnp.abs(ri - ci))
    w_main[pl.ds(0, LANES)] = weights
    w_main[pl.ds(LANES, LANES)] = weights
    weights = table(jnp.abs(outside_column(ri & 7) - ci))
    w_main[pl.ds(2 * LANES, LANES)] = weights
    w_main[pl.ds(3 * LANES, LANES)] = weights
    ri, ci = iotas((SUB, LANES))
    own_column = inside_column(ri)
    deep_column = deep_inside(ri)
    for part, rows in enumerate(
        (
            (own_column == ci).astype(jnp.float32).astype(jnp.bfloat16),
            table(jnp.abs(own_column - ci)),
            table(jnp.abs(outside_column(ri) - ci)),
            (deep_column == ci).astype(jnp.float32).astype(jnp.bfloat16),
        )
    ):
        if part % 2 == 0:
            first = rows
        else:
            both = jnp.concatenate([first.astype(jnp.float32), rows.astype(jnp.float32)], 0)
            both = both.astype(jnp.bfloat16)
            w_edge[pl.ds(part // 2 * ROWS, ROWS), pl.ds(0, LANES)] = both
            w_edge[pl.ds(part // 2 * ROWS, ROWS), pl.ds(LANES, LANES)] = both
    ri, ci = iotas((LANES, 2 * LANES))
    weights = table(jnp.abs(outside_column(ri & 7) - (ci & (LANES - 1)))).astype(jnp.float32)
    plane = (ri >> 3) & (planes - 1)
    for q in range(nz):
        w_join[q] = jnp.where(plane == 2 * q + (ci >> 7), weights, 0.0).astype(jnp.bfloat16)
    ri, ci = iotas((ny, ny))
    w_rows[...] = table(jnp.abs(ri - ci))
    ri, ci = iotas((ROWS, ny))
    weights = table(jnp.abs(jnp.where(ri < SUB, ri - SUB, ri + (ny - SUB)) - ci))
    w_ends[pl.ds(0, ROWS)] = weights
    w_ends[pl.ds(ROWS, ROWS)] = weights

    ri, ci = iotas((planes * SUB, LANES))
    weights = table(jnp.abs(inside_column(ri & 7) - outside_column(ci & 7)), ri >> 3 == (ci >> 3 & (planes - 1)))
    w_back[...] = weights
    same = ri >> 3 == (ci >> 3 & (planes - 1))
    source_column = inside_column(ci & 7)
    w_near[pl.ds(0, planes * SUB)] = table(jnp.abs(inside_column(ri & 7) - source_column), same)
    w_near[pl.ds(planes * SUB, planes * SUB)] = table(jnp.abs(deep_inside(ri & 7) - source_column), same)
    ri, ci = iotas((ny, half))
    w_pairs[...] = ((ri >> 1 == ci) & (ri >= ROWS) & (ri < ny - ROWS)).astype(jnp.float32).astype(jnp.bfloat16)
    ri, ci = iotas((LANES, 2 * nz // 2 * LANES))
    hit = (ri & 63 == (ci & (LANES - 1)) >> 1) & (ri >> 6 == ci >> 8)
    w_pick[...] = hit.astype(jnp.float32).astype(jnp.bfloat16)

    def split(x):
        high = x.astype(jnp.bfloat16)
        return high, (x - high.astype(jnp.float32)).astype(jnp.bfloat16)

    def dot(pieces, weights):
        return jnp.dot(jnp.concatenate(pieces, 1), weights, preferred_element_type=jnp.float32)

    def edges(rows, cells):
        return lax.dot_general(
            w_edge[pl.ds(0, rows)], cells, (((1,), (1,)), ((), ())), preferred_element_type=jnp.float32
        )

    def parts(x):
        return [x[p * ROWS : (p + 1) * ROWS] for p in range(planes)]

    def hand(i, value):
        xs_out[1, pl.ds(4 * i, 4)] = value[:4]
        xs_out[0, pl.ds(4 * i, 4)] = value[4:]

    def handed(i):
        return jnp.concatenate([xs_in[0, pl.ds(4 * i, 4)], xs_in[1, pl.ds(4 * i, 4)]], 0)

    def turned(values):
        values = jnp.concatenate(values, 0)
        first = lax.broadcasted_iota(jnp.int32, (values.shape[0], LANES), 1) < LANES // 2
        high, rest = split(jnp.where(first, values[:, :LANES], values[:, LANES:]))
        both = jnp.concatenate([high.astype(jnp.float32), rest.astype(jnp.float32)], 0)
        return both.T.astype(jnp.bfloat16)

    def y_copies(side, late):
        start = 0 if side == 0 else ny - 4
        padded, bare = pl.ds(PAD + start, 4), pl.ds(start, 4)
        sources = [(now, padded, planes), (mid, padded, planes), (speed, bare, nz)]
        arrive = pl.ds(SUB, 4) if side == 0 else pl.ds(4, 4)
        return [
            pltpu.make_async_remote_copy(
                src_ref=sources[i][0].at[:, sources[i][1], :],
                dst_ref=yin.at[1 - side, pl.ds(planes * i, sources[i][2]), arrive, :],
                send_sem=ysend.at[side, i], recv_sem=yrecv.at[1 - side, i],
                device_id=y_sides[side][1], device_id_type=MESH,
            )
            for i in ((1, 2) if late else (0,))
        ]

    def y_each(late, action):
        for side in range(2):
            @pl.when(y_sides[side][0])
            def _(side=side):
                for copy in y_copies(side if action != "wait_recv" else 1 - side, late):
                    getattr(copy, action)()

    def x_copy(side, part):
        device = x_sides[side][1]
        rows = pl.ds(0, 4 * planes) if part == 0 else pl.ds(4 * planes, 4 * (planes + nz))
        return pltpu.make_async_remote_copy(
            src_ref=xs_out.at[side, rows], dst_ref=xs_in.at[1 - side, rows],
            send_sem=xsend.at[side, part], recv_sem=xrecv.at[1 - side, part],
            device_id=device, device_id_type=MESH,
        )

    def corner_copy(i):
        return pltpu.make_async_remote_copy(
            src_ref=corner_out.at[i // 2], dst_ref=corner_in.at[3 - i],
            send_sem=csend.at[i], recv_sem=crecv.at[3 - i],
            device_id=diagonal[i][1], device_id_type=MESH,
        )

    body = pl.ds(PAD, ny)
    for f in range(2):
        loads[f].wait()
        for p in range(f * nz, (f + 1) * nz):
            cells = jnp.concatenate(split(now[p, body, :]), 1)
            pieces[p] = cells
            found = edges(2 * ROWS, cells)
            near[p] = found[:SUB]
            bent[p] = found[SUB : 2 * SUB]
            reach[p] = found[2 * SUB : 3 * SUB]
            if p < nz:
                deep_bent[p] = -2.0 * found[3 * SUB :]
            hand(p, found[:SUB])
    upper = jnp.zeros((SUB, LANES), jnp.float32)
    lower = upper
    for p in range(planes):
        shift = (8 * p + 4) % LANES
        upper = jnp.where(group == p, pltpu.roll(now[p, pl.ds(PAD, SUB), :], shift, 1), upper)
        lower = jnp.where(group == p, pltpu.roll(now[p, pl.ds(ny, SUB), :], shift, 1), lower)
    corner_out[0] = upper
    corner_out[1] = lower

    pl.semaphore_wait(barrier, expected)
    for i in range(4):
        @pl.when(diagonal[i][0])
        def _(i=i):
            corner_copy(i).start()
    for side in range(2):
        @pl.when(x_sides[side][0])
        def _(side=side):
            x_copy(side, 0).start()
    y_each(False, "start")

    for copy in smalls:
        copy.wait()
    y0, y1, x0, x1 = box[0, 0], box[0, 1], box[0, 2], box[0, 3]
    sz, sy, sx = src[0, 0], src[0, 1], src[0, 2]

    def inside_of(cell_y, cell_x):
        inside = (cell_x >= x0) & (cell_x < x1) & (cell_y >= y0) & (cell_y < y1)
        return inside, (cell_x == sx) & (cell_y == sy)

    def place(at, rows):
        cell_y = gy * ny + at + lax.broadcasted_iota(jnp.int32, (rows, LANES), 0)
        cell_x = gx * LANES + lax.broadcasted_iota(jnp.int32, (rows, LANES), 1)
        return inside_of(cell_y, cell_x)

    def amplitude(step, z):
        return jnp.where(sz == z, wave[0, step], 0.0)

    def vertical(values, p, total):
        z = p % nz
        for k in range(1, 5):
            s = None
            for d in (z + k, z - k):
                if 0 <= d < nz:
                    s = values[p - z + d] if s is None else s + values[p - z + d]
            if s is not None:
                total[k] = s if total[k] is None else total[k] + s
        return total

    def combine(cells, centre, along_x):
        result = []
        for p in range(planes):
            sums = vertical(centre, p, [None] * 5)
            total = along_x[p] + RATIO[0] * centre[p]
            for k in range(1, 5):
                s = cells(p, k) + cells(p, -k)
                if sums[k] is not None:
                    s = s + sums[k]
                total = total + (s if k == 1 else RATIO[k] * s)
            result.append(total)
        return result

    at_y, at_x = iotas((ny, LANES))
    inside, _ = inside_of(gy * ny + at_y, gx * LANES + at_x)
    inner[...] = jnp.where(inside, LEAD, 0.0)
    row, at_y = iotas((SUB, ny))
    edge_inside, edge_source = inside_of(gy * ny + at_y, gx * LANES + inside_column(row))
    at_lane = lax.broadcasted_iota(jnp.int32, (ROWS, LANES), 1)
    loads[2].wait()
    for z in range(nz):
        scaled = speed[z] * inner[...]
        speed[z] = scaled
        found = edges(2 * ROWS, jnp.concatenate(split(scaled), 1))
        deep_held[z] = found[3 * SUB :]
        found = found[:SUB]
        held[z] = found
        hand(2 * planes + z, found)
    tips = [pieces[p, pl.ds(at, ROWS), :] for at in (0, ny - ROWS) for p in range(planes)]
    tips = jnp.dot(jnp.concatenate(tips, 0), w_main[pl.ds(0, 2 * LANES)], preferred_element_type=jnp.float32)
    centre = [near[p] for p in range(planes)]
    high, rest = split(jnp.concatenate(centre, 0))
    along_y = jnp.dot(jnp.concatenate([high, rest], 0), w_rows[...], preferred_element_type=jnp.float32)
    for f in range(2):
        loads[3 + f].wait()
        for z in range(nz):
            p = f * nz + z
            before = edges(2 * ROWS if f == 0 else ROWS, jnp.concatenate(split(old[p]), 1))
            if f == 0:
                deep_bent[p] = deep_bent[p] + before[3 * SUB :]
            before = before[:SUB]
            prior[p] = before
            total = bent[p] + RATIO[0] * centre[p]
            total = total + along_y[p * SUB : (p + 1) * SUB]
            total = total + along_y[(planes + p) * SUB : (planes + p + 1) * SUB]
            for k, s in enumerate(vertical(centre, p, [None] * 5)):
                if s is not None:
                    total = total + (s if k == 1 else RATIO[k] * s)
            value = 2.0 * centre[p] - before
            if f == 0:
                value = value + jnp.where(edge_source, amplitude(0, z), 0.0)
            hand(planes + p, jnp.where(edge_inside, value, 0.0) + held[z] * total)
    for side in range(2):
        @pl.when(x_sides[side][0])
        def _(side=side):
            x_copy(side, 1).start()

    def advance(at, along_x):
        inside, source = place(at, ROWS)
        here = pl.ds(at, ROWS)
        cells = lambda p, k: now[p, pl.ds(at + PAD + k, ROWS), :]
        centre = [cells(p, 0) for p in range(planes)]
        lap = combine(cells, centre, along_x)
        scales = [speed[z, here, :] for z in range(nz)]
        for p in range(planes):
            new = 2.0 * centre[p] - old[p, here, :]
            if p < nz:
                new = new + jnp.where(source, amplitude(0, p), 0.0)
            mid[p, pl.ds(at + PAD, ROWS), :] = jnp.where(inside, new, 0.0) + scales[p % nz] * lap[p]

    advance(0, parts(tips[: planes * ROWS]))
    advance(ny - ROWS, parts(tips[planes * ROWS :]))

    y_each(True, "start")

    def first_step(i, carry):
        at = pl.multiple_of(i * ROWS, ROWS)
        advance(at, [along[p, pl.ds(at, ROWS), :] for p in range(planes)])
        return carry

    for p in range(planes):
        along[p] = jnp.dot(pieces[p], w_main[pl.ds(0, 2 * LANES)], preferred_element_type=jnp.float32)
    lax.fori_loop(1, groups - 1, first_step, 0)

    for p in range(planes):
        for v in range(2):
            total = None
            for k in range(1, 5):
                term = RATIO[k] * now[p, pl.ds(k if v == 0 else PAD + ny - k, SUB), :]
                total = term if total is None else total + term
            over[v, p] = total

    for p in range(planes):
        cells = jnp.concatenate(split(mid[p, body, :]), 1)
        along[p] = jnp.dot(cells, w_main[pl.ds(0, 2 * LANES)], preferred_element_type=jnp.float32)
        found = edges(2 * ROWS, cells)
        middle[p] = found[:SUB]
        bent[p] = found[SUB : 2 * SUB]
        if p < nz:
            deep_bent[p] = deep_bent[p] + found[3 * SUB :]
        else:
            deep_late[p - nz] = found[3 * SUB :]

    def twice(at, along_x, keep):
        here, padded = pl.ds(at, ROWS), pl.ds(at + PAD, ROWS)
        inside, source = place(at, ROWS)
        centre = [mid[p, padded, :] for p in range(planes)]
        lap = combine(lambda p, k: mid[p, pl.ds(at + PAD + k, ROWS), :], centre, along_x)
        total = None
        for z in range(nz):
            c = speed[z, here, :]
            f0, f1, a2 = old[z, here, :], now[z, padded, :], now[nz + z, padded, :]
            f2, a1 = centre[z], centre[nz + z]
            f3 = 2.0 * f2 - f1 + jnp.where(source, amplitude(1, z), 0.0)
            f3 = jnp.where(inside, f3, 0.0) + c * lap[z]
            a0 = jnp.where(inside, 2.0 * a1 - a2, 0.0) + c * lap[nz + z]
            part = a0 * (f2 - 2.0 * f1 + f0) + a1 * (f3 - 2.0 * f2 + f1)
            total = part if z % 2 == 0 else total + part
            if z % 2 == 1:
                image[z // 2, here, :] = total if keep is None else jnp.where(keep, total, 0.0)

    keep = (at_lane >= 4) & (at_lane < LANES - 4)

    def second_step(g, carry):
        at = pl.multiple_of(g * ROWS, ROWS)
        twice(at, [along[p, pl.ds(at, ROWS), :] for p in range(planes)], keep)
        return carry

    lax.fori_loop(1, groups - 1, second_step, 0)

    y_each(True, "wait_send")
    for side, (there, _) in enumerate(x_sides):
        @pl.when(there)
        def _(side=side):
            x_copy(1 - side, 0).wait_recv()
    y_each(False, "wait_recv")
    outer = [handed(p) for p in range(planes)]
    lack = jnp.dot(
        w_back[...], jnp.concatenate(split(jnp.concatenate(outer, 0)), 0), preferred_element_type=jnp.float32
    )
    gain = [held[p % nz] * lack[p * SUB : (p + 1) * SUB] for p in range(planes)]
    second = [middle[p] + gain[p] for p in range(planes)]
    spread = jnp.dot(
        w_near[...], jnp.concatenate(split(jnp.concatenate(gain, 0)), 0), preferred_element_type=jnp.float32
    )
    along_y = jnp.dot(
        jnp.concatenate(split(jnp.concatenate(second, 0)), 0), w_rows[...], preferred_element_type=jnp.float32
    )
    for p in range(planes):
        total = bent[p] + spread[p * SUB : (p + 1) * SUB] + RATIO[0] * second[p]
        total = total + along_y[p * SUB : (p + 1) * SUB]
        total = total + along_y[(planes + p) * SUB : (planes + p + 1) * SUB]
        for k, s in enumerate(vertical(second, p, [None] * 5)):
            if s is not None:
                total = total + (s if k == 1 else RATIO[k] * s)
        bent[p] = total
        middle[p] = second[p]
    deep = []
    for z in range(nz):
        f = spread[(planes + z) * SUB : (planes + z + 1) * SUB]
        a = spread[(planes + nz + z) * SUB : (planes + nz + z + 1) * SUB]
        deep.append(deep_held[z] * (a * deep_bent[z] + deep_late[z] * f))
    deep_sums[...] = jnp.concatenate([deep[2 * k] + deep[2 * k + 1] for k in range(nz // 2)], 0)

    span = 2 * ROWS
    columns = turned(outer)
    columns = jnp.concatenate([columns[:span], columns[LANES - span :]], 0)
    for q in range(nz):
        lack = jnp.dot(columns, w_join[q], preferred_element_type=jnp.float32)
        for side in range(2):
            p = 2 * q + side
            for v, at in enumerate((0, ny - span)):
                here = pl.ds(PAD + at, span)
                part = lack[v * span : (v + 1) * span, side * LANES : (side + 1) * LANES]
                mid[p, here, :] = mid[p, here, :] + speed[p % nz, pl.ds(at, span), :] * part
    for p in range(planes):
        for v in range(2):
            total = None
            for k in range(1, 5):
                term = RATIO[k] * yin[v, p, pl.ds(SUB - k if v == 0 else k, SUB), :]
                total = term if total is None else total + term
            at = 0 if v == 0 else ny - SUB
            here = pl.ds(PAD + at, SUB)
            mid[p, here, :] = mid[p, here, :] + speed[p % nz, pl.ds(at, SUB), :] * total
    tips = [mid[p, pl.ds(PAD + at, ROWS), :] for at in (0, ny - ROWS) for p in range(planes)]
    tips = dot(split(jnp.concatenate(tips, 0)), w_main[pl.ds(0, 2 * LANES)])
    for v in range(2):
        for p in range(planes):
            at = (v * planes + p) * ROWS
            along[p, pl.ds(v * ROWS, ROWS), :] = tips[at : at + ROWS]

    for i in range(4):
        @pl.when(diagonal[i][0])
        def _(i=i):
            corner_copy(3 - i).wait_recv()
    halves = [jnp.where(low, corner_in[2 * v], corner_in[2 * v + 1]) for v in range(2)]
    masked = [jnp.where(group == p, halves[v], 0.0) for v in range(2) for p in range(planes)]
    lack = dot(split(jnp.concatenate(masked, 0)), w_main[pl.ds(2 * LANES, 2 * LANES)])
    high, rest = split(jnp.concatenate(halves, 0))
    ends = lax.dot_general(
        jnp.concatenate([high, rest], 0), w_ends[...], (((0,), (0,)), ((), ())),
        preferred_element_type=jnp.float32,
    )
    for p in range(planes):
        reach[p] = reach[p] + ends[p * SUB : (p + 1) * SUB]
        for v in range(2):
            at = (v * planes + p) * SUB
            over[v, p] = over[v, p] + lack[at : at + SUB]

    for side, (there, _) in enumerate(x_sides):
        @pl.when(there)
        def _(side=side):
            x_copy(1 - side, 1).wait_recv()
    y_each(True, "wait_recv")
    outer = [handed(planes + p) + handed(2 * planes + p % nz) * reach[p] for p in range(planes)]
    lack = jnp.dot(
        w_back[...], jnp.concatenate(split(jnp.concatenate(outer, 0)), 0), preferred_element_type=jnp.float32
    )
    columns = turned(outer)
    columns = jnp.concatenate([columns[:ROWS], columns[LANES - ROWS :]], 0)
    found = [jnp.dot(columns, w_join[q], preferred_element_type=jnp.float32) for q in range(nz)]
    for v in range(2):
        here = pl.ds(0 if v == 0 else PAD + ny, SUB)
        rows = pl.ds(0 if v == 0 else SUB, SUB)
        for p in range(planes):
            mid[p, here, :] = yin[v, planes + p, rows, :] + yin[v, 2 * planes + p % nz, rows, :] * over[v, p]
    for v, at in enumerate((0, ny - ROWS)):
        here = pl.ds(v * ROWS, ROWS)
        twice(
            at,
            [
                along[p, here, :]
                + found[p // 2][v * ROWS : (v + 1) * ROWS, p % 2 * LANES : (p % 2 + 1) * LANES]
                for p in range(planes)
            ],
            None,
        )
    fixes = []
    for z in range(nz):
        f2, a1 = middle[z], middle[nz + z]
        f1, a2 = near[z], near[nz + z]
        f3 = 2.0 * f2 - f1 + jnp.where(edge_source, amplitude(1, z), 0.0)
        f3 = jnp.where(edge_inside, f3, 0.0) + held[z] * (bent[z] + lack[z * SUB : (z + 1) * SUB])
        a0 = jnp.where(edge_inside, 2.0 * a1 - a2, 0.0)
        a0 = a0 + held[z] * (bent[nz + z] + lack[(nz + z) * SUB : (nz + z + 1) * SUB])
        fixes.append(a0 * (f2 - 2.0 * f1 + prior[z]) + a1 * (f3 - 2.0 * f2 + f1))
    fixes = jnp.concatenate([fixes[2 * k] + fixes[2 * k + 1] for k in range(nz // 2)] + [deep_sums[...]], 0)
    both = jnp.dot(jnp.concatenate(split(fixes), 0), w_pairs[...], preferred_element_type=jnp.float32)
    fixes = both[: nz * SUB] + both[nz * SUB :]
    patch[...] = fixes

    rows = [
        image[k, pl.ds(0, half, stride=2), :] + image[k, pl.ds(1, half, stride=2), :] for k in range(nz // 2)
    ]
    cells = jnp.concatenate([x for k in range(nz // 2) for x in split(rows[k])], 1)
    total = lax.dot_general(
        w_pick[...], cells, (((1,), (1,)), ((), ())), preferred_element_type=jnp.float32
    )
    coarse[...] = total

    def exchange(ref, into, lane_of):
        copies = []
        for step in range(1, shots):
            copy = pltpu.make_async_remote_copy(
                src_ref=ref, dst_ref=into.at[step - 1],
                send_sem=shot_send.at[lane_of, step - 1], recv_sem=shot_recv.at[lane_of, step - 1],
                device_id={"shot": lax.rem(shot + step, shots)}, device_id_type=MESH,
            )
            copy.start()
            copies.append(copy)
        return copies

    sends = exchange(coarse, arrived, 0)

    sends = sends + exchange(patch, patches, 1)

    y_each(False, "wait_send")
    for side in range(2):
        @pl.when(x_sides[side][0])
        def _(side=side):
            for part in range(2):
                x_copy(side, part).wait_send()
    for i in range(4):
        @pl.when(diagonal[i][0])
        def _(i=i):
            corner_copy(i).wait_send()
    for copy in sends:
        copy.wait_recv()
    for step in range(shots - 1):
        total = total + arrived[step]
        fixes = fixes + patches[step]
    depth = top[0].astype(jnp.float32)
    width = LANES // 2
    for k in range(nz // 2):
        factor = (0.25 + (depth + (2.0 * k + 1.0)) / 128.0) * 0.125
        out_ref[k] = total[width * k : width * k + width] * factor
        for i, at in enumerate((width - 2, width - 1, 0, 1, width - 4, width - 3, 2, 3)):
            first = (k + i // 4 * (nz // 2)) * SUB + 2 * (i % 4)
            row = (fixes[first : first + 1] + fixes[first + 1 : first + 2]) * factor
            out_ref[k, pl.ds(at, 1), :] = out_ref[k, pl.ds(at, 1), :] + row
    for copy in sends:
        copy.wait_send()


def per_device(shots, counts, fwd_prev, fwd_cur, adj_late, adj_now, courant, wavelet, boxes, sources, slab_top):
    nz, ny, nx = courant.shape
    f32, b16 = jnp.float32, jnp.bfloat16
    planes = 2 * nz
    others = max(shots - 1, 1)
    hbm = pl.BlockSpec(memory_space=pltpu.HBM)
    dma = pltpu.SemaphoreType.DMA
    smalls = [pltpu.with_memory_space_constraint(x, pltpu.HBM) for x in (wavelet, boxes, sources)]
    out = pl.pallas_call(
        functools.partial(kernel, shots, counts),
        out_shape=jax.ShapeDtypeStruct((nz // 2, nx // 2, ny // 2), f32),
        in_specs=[hbm] * 9,
        out_specs=pl.BlockSpec(memory_space=pltpu.VMEM),
        scratch_shapes=[
            pltpu.SMEM((1, 2), f32),
            pltpu.SMEM((1, 4), jnp.int32),
            pltpu.SMEM((1, 3), jnp.int32),
            pltpu.SMEM((1,), jnp.int32),
            pltpu.VMEM((planes, ny + 2 * PAD, nx), f32),
            pltpu.VMEM((planes, ny + 2 * PAD, nx), f32),
            pltpu.VMEM((planes, ny, nx), f32),
            pltpu.VMEM((nz, ny, nx), f32),
            pltpu.VMEM((nz // 2, ny, nx), f32),
            pltpu.VMEM((ny, nx), f32),
            pltpu.VMEM((2, 2 * planes + nz, ROWS, nx), f32),
            pltpu.VMEM((2, planes, SUB, nx), f32),
            pltpu.VMEM((planes, ny, 2 * nx), b16),
            pltpu.VMEM((planes, ny, nx), f32),
            pltpu.VMEM((planes, SUB, ny), f32),
            pltpu.VMEM((planes, SUB, ny), f32),
            pltpu.VMEM((planes, SUB, ny), f32),
            pltpu.VMEM((planes, SUB, ny), f32),
            pltpu.VMEM((nz, SUB, ny), f32),
            pltpu.VMEM((planes, SUB, ny), f32),
            pltpu.VMEM((nz, SUB, ny), f32),
            pltpu.VMEM((nz, SUB, ny), f32),
            pltpu.VMEM((nz, SUB, ny), f32),
            pltpu.VMEM((nz // 2 * SUB, ny), f32),
            pltpu.VMEM((2, 4 * (2 * planes + nz), ny), f32),
            pltpu.VMEM((2, 4 * (2 * planes + nz), ny), f32),
            pltpu.VMEM((2, SUB, nx), f32),
            pltpu.VMEM((4, SUB, nx), f32),
            pltpu.VMEM((4 * nx, nx), b16),
            pltpu.VMEM((2 * ROWS, 2 * nx), b16),
            pltpu.VMEM((nz, nx, 2 * nx), b16),
            pltpu.VMEM((ny, ny), b16),
            pltpu.VMEM((2 * ROWS, ny), b16),
            pltpu.VMEM((planes * SUB, nx), b16),
            pltpu.VMEM((2 * planes * SUB, nx), b16),
            pltpu.VMEM((ny, ny // 2), b16),
            pltpu.VMEM((nx, nz * nx), b16),
            pltpu.VMEM((nx, ny // 2), f32),
            pltpu.VMEM((others, nx, ny // 2), f32),
            pltpu.VMEM((nz * SUB, ny // 2), f32),
            pltpu.VMEM((others, nz * SUB, ny // 2), f32),
            dma((4,)),
            dma((5,)),
            dma((2, 3)),
            dma((2, 3)),
            dma((2, 2)),
            dma((2, 2)),
            dma((4,)),
            dma((4,)),
            dma((2, others)),
            dma((2, others)),
        ],
        compiler_params=pltpu.CompilerParams(
            collective_id=0, has_side_effects=True, vmem_limit_bytes=54912 * 1024
        ),
    )(*smalls, slab_top, fwd_prev, fwd_cur, adj_late, adj_now, courant)
    return jnp.swapaxes(out, 1, 2)


def solution(mesh):
    shots = mesh.shape["shot"]
    counts = (mesh.shape["gy"], mesh.shape["gx"])
    return jax.shard_map(
        functools.partial(per_device, shots, counts),
        mesh=mesh,
        in_specs=(
            P("shot", None, "gy", "gx"),
            P("shot", None, "gy", "gx"),
            P("shot", None, "gy", "gx"),
            P("shot", None, "gy", "gx"),
            P(None, "gy", "gx"),
            P("shot", None),
            P("shot", None),
            P("shot", None),
            P(),
        ),
        out_specs=P(None, "gy", "gx"),
        check_vma=False,
    )
```

```python
import functools

import jax
import jax.numpy as jnp
from jax import lax
from jax.experimental import pallas as pl
from jax.experimental.pallas import tpu as pltpu
from jax.sharding import PartitionSpec as P

COEFFS = (-205.0 / 72.0, 8.0 / 5.0, -1.0 / 5.0, 8.0 / 315.0, -1.0 / 560.0)
LEAD = COEFFS[1]
RATIO = (3.0 * COEFFS[0] / LEAD, 1.0, COEFFS[2] / LEAD, COEFFS[3] / LEAD, COEFFS[4] / LEAD)
MESH = pl.DeviceIdType.MESH
PAD = 8
LANES = 128
ROWS = 16
SUB = 8


def kernel(
    shots, counts, wave_hbm, box_hbm, src_hbm, top_hbm, f0_hbm, f1_hbm, a3_hbm, a2_hbm, c_hbm, out_ref,
    wave, box, src, top, now, mid, old, speed, image, inner, yin, over, pieces, along,
    near, bent, reach, prior, held, middle, deep_bent, deep_late, deep_held, deep_sums, xs_out, xs_in, corner_out, corner_in, w_main, w_edge, w_join, w_rows,
    w_ends, w_back, w_near, w_pairs, w_pick, coarse, arrived, patch, patches,
    small_sem, load_sem, ysend, yrecv, xsend, xrecv, csend, crecv, shot_send, shot_recv,
):
    county, countx = counts
    nz, ny = speed.shape[0], speed.shape[1]
    planes = 2 * nz
    half = ny // 2
    groups = ny // ROWS
    gy, gx, shot = lax.axis_index("gy"), lax.axis_index("gx"), lax.axis_index("shot")
    has_up, has_down = gy > 0, gy < county - 1
    has_left, has_right = gx > 0, gx < countx - 1

    loads = []
    for i, (hbm, ref) in enumerate(
        (
            (f1_hbm.at[0], now.at[pl.ds(0, nz), pl.ds(PAD, ny)]),
            (a2_hbm.at[0], now.at[pl.ds(nz, nz), pl.ds(PAD, ny)]),
            (c_hbm, speed),
            (f0_hbm.at[0], old.at[pl.ds(0, nz)]),
            (a3_hbm.at[0], old.at[pl.ds(nz, nz)]),
        )
    ):
        loads.append(pltpu.make_async_copy(hbm, ref, load_sem.at[i]))
    smalls = []
    for i, (hbm, ref) in enumerate(((wave_hbm, wave), (box_hbm, box), (src_hbm, src), (top_hbm, top))):
        smalls.append(pltpu.make_async_copy(hbm, ref, small_sem.at[i]))
    for copy in loads[:2] + smalls + loads[2:]:
        copy.start()

    barrier = pltpu.get_barrier_semaphore()
    y_sides = [(has_up, {"gy": gy - 1}), (has_down, {"gy": gy + 1})]
    x_sides = [(has_left, {"gx": gx - 1}), (has_right, {"gx": gx + 1})]
    diagonal = [
        (v & h, {"gy": gy + dy, "gx": gx + dx})
        for v, dy in ((has_up, -1), (has_down, 1))
        for h, dx in ((has_left, -1), (has_right, 1))
    ]
    expected = shots - 1
    for there, device in y_sides + x_sides + diagonal:
        expected = expected + there.astype(jnp.int32)

        @pl.when(there)
        def _(device=device):
            pl.semaphore_signal(barrier, inc=1, device_id=device, device_id_type=MESH)
    for step in range(1, shots):
        pl.semaphore_signal(
            barrier, inc=1, device_id={"shot": lax.rem(shot + step, shots)}, device_id_type=MESH
        )

    for side, (there, _) in enumerate(y_sides):
        @pl.when(jnp.logical_not(there))
        def _(side=side):
            yin[side] = jnp.zeros(yin.shape[1:], jnp.float32)
    for side, (there, _) in enumerate(x_sides):
        @pl.when(jnp.logical_not(there))
        def _(side=side):
            xs_in[side] = jnp.zeros(xs_in.shape[1:], jnp.float32)
    for i, (there, _) in enumerate(diagonal):
        @pl.when(jnp.logical_not(there))
        def _(i=i):
            corner_in[i] = jnp.zeros((SUB, LANES), jnp.float32)

    for p in range(planes):
        nothing = jnp.zeros((SUB, LANES), jnp.float32)
        now[p, pl.ds(0, PAD), :] = nothing
        now[p, pl.ds(PAD + ny, PAD), :] = nothing
        yin[0, p, pl.ds(SUB, SUB), :] = nothing
        yin[1, p, pl.ds(0, SUB), :] = nothing

    lane = lax.broadcasted_iota(jnp.int32, (SUB, LANES), 1)
    group = lane >> 3
    low = (lane & 7) < 4

    def iotas(shape):
        return lax.broadcasted_iota(jnp.int32, shape, 0), lax.broadcasted_iota(jnp.int32, shape, 1)

    def table(distance, keep=None):
        weights = jnp.zeros(distance.shape, jnp.float32)
        for k in range(1, 5):
            hit = distance == k
            weights = jnp.where(hit if keep is None else keep & hit, RATIO[k], weights)
        return weights.astype(jnp.bfloat16)

    def inside_column(j):
        return jnp.where(j < 4, j + (LANES - 4), j - 4)

    def outside_column(j):
        return jnp.where(j < 4, j - 4, j + (LANES - 4))

    def deep_inside(j):
        return jnp.where(j < 4, j + (LANES - 8), j)

    ri, ci = iotas((LANES, LANES))
    weights = table(jnp.abs(ri - ci))
    w_main[pl.ds(0, LANES)] = weights
    w_main[pl.ds(LANES, LANES)] = weights
    weights = table(jnp.abs(outside_column(ri & 7) - ci))
    w_main[pl.ds(2 * LANES, LANES)] = weights
    w_main[pl.ds(3 * LANES, LANES)] = weights
    ri, ci = iotas((SUB, LANES))
    own_column = inside_column(ri)
    deep_column = deep_inside(ri)
    for part, rows in enumerate(
        (
            (own_column == ci).astype(jnp.float32).astype(jnp.bfloat16),
            table(jnp.abs(own_column - ci)),
            table(jnp.abs(outside_column(ri) - ci)),
            (deep_column == ci).astype(jnp.float32).astype(jnp.bfloat16),
        )
    ):
        if part % 2 == 0:
            first = rows
        else:
            both = jnp.concatenate([first.astype(jnp.float32), rows.astype(jnp.float32)], 0)
            both = both.astype(jnp.bfloat16)
            w_edge[pl.ds(part // 2 * ROWS, ROWS), pl.ds(0, LANES)] = both
            w_edge[pl.ds(part // 2 * ROWS, ROWS), pl.ds(LANES, LANES)] = both
    ri, ci = iotas((LANES, 2 * LANES))
    weights = table(jnp.abs(outside_column(ri & 7) - (ci & (LANES - 1)))).astype(jnp.float32)
    plane = (ri >> 3) & (planes - 1)
    for q in range(nz):
        w_join[q] = jnp.where(plane == 2 * q + (ci >> 7), weights, 0.0).astype(jnp.bfloat16)
    ri, ci = iotas((ny, ny))
    w_rows[...] = table(jnp.abs(ri - ci))
    ri, ci = iotas((ROWS, ny))
    weights = table(jnp.abs(jnp.where(ri < SUB, ri - SUB, ri + (ny - SUB)) - ci))
    w_ends[pl.ds(0, ROWS)] = weights
    w_ends[pl.ds(ROWS, ROWS)] = weights

    ri, ci = iotas((planes * SUB, LANES))
    weights = table(jnp.abs(inside_column(ri & 7) - outside_column(ci & 7)), ri >> 3 == (ci >> 3 & (planes - 1)))
    w_back[...] = weights
    same = ri >> 3 == (ci >> 3 & (planes - 1))
    source_column = inside_column(ci & 7)
    w_near[pl.ds(0, planes * SUB)] = table(jnp.abs(inside_column(ri & 7) - source_column), same)
    w_near[pl.ds(planes * SUB, planes * SUB)] = table(jnp.abs(deep_inside(ri & 7) - source_column), same)
    ri, ci = iotas((ny, half))
    w_pairs[...] = ((ri >> 1 == ci) & (ri >= ROWS) & (ri < ny - ROWS)).astype(jnp.float32).astype(jnp.bfloat16)
    ri, ci = iotas((LANES, 2 * nz // 2 * LANES))
    hit = (ri & 63 == (ci & (LANES - 1)) >> 1) & (ri >> 6 == ci >> 8)
    w_pick[...] = hit.astype(jnp.float32).astype(jnp.bfloat16)

    def split(x):
        high = x.astype(jnp.bfloat16)
        return high, (x - high.astype(jnp.float32)).astype(jnp.bfloat16)

    def dot(pieces, weights):
        return jnp.dot(jnp.concatenate(pieces, 1), weights, preferred_element_type=jnp.float32)

    def edges(rows, cells):
        return lax.dot_general(
            w_edge[pl.ds(0, rows)], cells, (((1,), (1,)), ((), ())), preferred_element_type=jnp.float32
        )

    def parts(x):
        return [x[p * ROWS : (p + 1) * ROWS] for p in range(planes)]

    def hand(i, value):
        xs_out[1, pl.ds(4 * i, 4)] = value[:4]
        xs_out[0, pl.ds(4 * i, 4)] = value[4:]

    def handed(i):
        return jnp.concatenate([xs_in[0, pl.ds(4 * i, 4)], xs_in[1, pl.ds(4 * i, 4)]], 0)

    def turned(values):
        values = jnp.concatenate(values, 0)
        first = lax.broadcasted_iota(jnp.int32, (values.shape[0], LANES), 1) < LANES // 2
        high, rest = split(jnp.where(first, values[:, :LANES], values[:, LANES:]))
        both = jnp.concatenate([high.astype(jnp.float32), rest.astype(jnp.float32)], 0)
        return both.T.astype(jnp.bfloat16)

    def y_copies(side, late):
        start = 0 if side == 0 else ny - 4
        padded, bare = pl.ds(PAD + start, 4), pl.ds(start, 4)
        sources = [(now, padded, planes), (mid, padded, planes), (speed, bare, nz)]
        arrive = pl.ds(SUB, 4) if side == 0 else pl.ds(4, 4)
        return [
            pltpu.make_async_remote_copy(
                src_ref=sources[i][0].at[:, sources[i][1], :],
                dst_ref=yin.at[1 - side, pl.ds(planes * i, sources[i][2]), arrive, :],
                send_sem=ysend.at[side, i], recv_sem=yrecv.at[1 - side, i],
                device_id=y_sides[side][1], device_id_type=MESH,
            )
            for i in ((1, 2) if late else (0,))
        ]

    def y_each(late, action):
        for side in range(2):
            @pl.when(y_sides[side][0])
            def _(side=side):
                for copy in y_copies(side if action != "wait_recv" else 1 - side, late):
                    getattr(copy, action)()

    def x_copy(side, part):
        device = x_sides[side][1]
        rows = pl.ds(0, 4 * planes) if part == 0 else pl.ds(4 * planes, 4 * (planes + nz))
        return pltpu.make_async_remote_copy(
            src_ref=xs_out.at[side, rows], dst_ref=xs_in.at[1 - side, rows],
            send_sem=xsend.at[side, part], recv_sem=xrecv.at[1 - side, part],
            device_id=device, device_id_type=MESH,
        )

    def corner_copy(i):
        return pltpu.make_async_remote_copy(
            src_ref=corner_out.at[i // 2], dst_ref=corner_in.at[3 - i],
            send_sem=csend.at[i], recv_sem=crecv.at[3 - i],
            device_id=diagonal[i][1], device_id_type=MESH,
        )

    body = pl.ds(PAD, ny)
    for f in range(2):
        loads[f].wait()
        for p in range(f * nz, (f + 1) * nz):
            cells = jnp.concatenate(split(now[p, body, :]), 1)
            pieces[p] = cells
            found = edges(2 * ROWS, cells)
            near[p] = found[:SUB]
            bent[p] = found[SUB : 2 * SUB]
            reach[p] = found[2 * SUB : 3 * SUB]
            if p < nz:
                deep_bent[p] = -2.0 * found[3 * SUB :]
            hand(p, found[:SUB])
    upper = jnp.zeros((SUB, LANES), jnp.float32)
    lower = upper
    for p in range(planes):
        shift = (8 * p + 4) % LANES
        upper = jnp.where(group == p, pltpu.roll(now[p, pl.ds(PAD, SUB), :], shift, 1), upper)
        lower = jnp.where(group == p, pltpu.roll(now[p, pl.ds(ny, SUB), :], shift, 1), lower)
    corner_out[0] = upper
    corner_out[1] = lower

    for copy in smalls:
        copy.wait()
    y0, y1, x0, x1 = box[0, 0], box[0, 1], box[0, 2], box[0, 3]
    sz, sy, sx = src[0, 0], src[0, 1], src[0, 2]

    def inside_of(cell_y, cell_x):
        inside = (cell_x >= x0) & (cell_x < x1) & (cell_y >= y0) & (cell_y < y1)
        return inside, (cell_x == sx) & (cell_y == sy)

    def place(at, rows):
        cell_y = gy * ny + at + lax.broadcasted_iota(jnp.int32, (rows, LANES), 0)
        cell_x = gx * LANES + lax.broadcasted_iota(jnp.int32, (rows, LANES), 1)
        return inside_of(cell_y, cell_x)

    def amplitude(step, z):
        return jnp.where(sz == z, wave[0, step], 0.0)

    def vertical(values, p, total):
        z = p % nz
        for k in range(1, 5):
            s = None
            for d in (z + k, z - k):
                if 0 <= d < nz:
                    s = values[p - z + d] if s is None else s + values[p - z + d]
            if s is not None:
                total[k] = s if total[k] is None else total[k] + s
        return total

    def combine(cells, centre, along_x):
        result = []
        for p in range(planes):
            sums = vertical(centre, p, [None] * 5)
            total = along_x[p] + RATIO[0] * centre[p]
            for k in range(1, 5):
                s = cells(p, k) + cells(p, -k)
                if sums[k] is not None:
                    s = s + sums[k]
                total = total + (s if k == 1 else RATIO[k] * s)
            result.append(total)
        return result

    at_y, at_x = iotas((ny, LANES))
    inside, _ = inside_of(gy * ny + at_y, gx * LANES + at_x)
    inner[...] = jnp.where(inside, LEAD, 0.0)
    row, at_y = iotas((SUB, ny))
    edge_inside, edge_source = inside_of(gy * ny + at_y, gx * LANES + inside_column(row))
    at_lane = lax.broadcasted_iota(jnp.int32, (ROWS, LANES), 1)
    loads[2].wait()
    for z in range(nz):
        scaled = speed[z] * inner[...]
        speed[z] = scaled
        found = edges(2 * ROWS, jnp.concatenate(split(scaled), 1))
        deep_held[z] = found[3 * SUB :]
        found = found[:SUB]
        held[z] = found
        hand(2 * planes + z, found)
    tips = [pieces[p, pl.ds(at, ROWS), :] for at in (0, ny - ROWS) for p in range(planes)]
    tips = jnp.dot(jnp.concatenate(tips, 0), w_main[pl.ds(0, 2 * LANES)], preferred_element_type=jnp.float32)
    centre = [near[p] for p in range(planes)]
    high, rest = split(jnp.concatenate(centre, 0))
    along_y = jnp.dot(jnp.concatenate([high, rest], 0), w_rows[...], preferred_element_type=jnp.float32)
    for f in range(2):
        loads[3 + f].wait()
        for z in range(nz):
            p = f * nz + z
            before = edges(2 * ROWS if f == 0 else ROWS, jnp.concatenate(split(old[p]), 1))
            if f == 0:
                deep_bent[p] = deep_bent[p] + before[3 * SUB :]
            before = before[:SUB]
            prior[p] = before
            total = bent[p] + RATIO[0] * centre[p]
            total = total + along_y[p * SUB : (p + 1) * SUB]
            total = total + along_y[(planes + p) * SUB : (planes + p + 1) * SUB]
            for k, s in enumerate(vertical(centre, p, [None] * 5)):
                if s is not None:
                    total = total + (s if k == 1 else RATIO[k] * s)
            value = 2.0 * centre[p] - before
            if f == 0:
                value = value + jnp.where(edge_source, amplitude(0, z), 0.0)
            hand(planes + p, jnp.where(edge_inside, value, 0.0) + held[z] * total)

    def advance(at, along_x):
        inside, source = place(at, ROWS)
        here = pl.ds(at, ROWS)
        cells = lambda p, k: now[p, pl.ds(at + PAD + k, ROWS), :]
        centre = [cells(p, 0) for p in range(planes)]
        lap = combine(cells, centre, along_x)
        scales = [speed[z, here, :] for z in range(nz)]
        for p in range(planes):
            new = 2.0 * centre[p] - old[p, here, :]
            if p < nz:
                new = new + jnp.where(source, amplitude(0, p), 0.0)
            mid[p, pl.ds(at + PAD, ROWS), :] = jnp.where(inside, new, 0.0) + scales[p % nz] * lap[p]

    advance(0, parts(tips[: planes * ROWS]))
    advance(ny - ROWS, parts(tips[planes * ROWS :]))

    pl.semaphore_wait(barrier, expected)
    for i in range(4):
        @pl.when(diagonal[i][0])
        def _(i=i):
            corner_copy(i).start()
    for side in range(2):
        @pl.when(x_sides[side][0])
        def _(side=side):
            x_copy(side, 0).start()
    y_each(False, "start")
    for side in range(2):
        @pl.when(x_sides[side][0])
        def _(side=side):
            x_copy(side, 1).start()
    y_each(True, "start")


    def first_step(i, carry):
        at = pl.multiple_of(i * ROWS, ROWS)
        advance(at, [along[p, pl.ds(at, ROWS), :] for p in range(planes)])
        return carry

    for p in range(planes):
        along[p] = jnp.dot(pieces[p], w_main[pl.ds(0, 2 * LANES)], preferred_element_type=jnp.float32)
    lax.fori_loop(1, groups - 1, first_step, 0)

    for p in range(planes):
        for v in range(2):
            total = None
            for k in range(1, 5):
                term = RATIO[k] * now[p, pl.ds(k if v == 0 else PAD + ny - k, SUB), :]
                total = term if total is None else total + term
            over[v, p] = total

    for p in range(planes):
        cells = jnp.concatenate(split(mid[p, body, :]), 1)
        along[p] = jnp.dot(cells, w_main[pl.ds(0, 2 * LANES)], preferred_element_type=jnp.float32)
        found = edges(2 * ROWS, cells)
        middle[p] = found[:SUB]
        bent[p] = found[SUB : 2 * SUB]
        if p < nz:
            deep_bent[p] = deep_bent[p] + found[3 * SUB :]
        else:
            deep_late[p - nz] = found[3 * SUB :]

    def twice(at, along_x, keep):
        here, padded = pl.ds(at, ROWS), pl.ds(at + PAD, ROWS)
        inside, source = place(at, ROWS)
        centre = [mid[p, padded, :] for p in range(planes)]
        lap = combine(lambda p, k: mid[p, pl.ds(at + PAD + k, ROWS), :], centre, along_x)
        total = None
        for z in range(nz):
            c = speed[z, here, :]
            f0, f1, a2 = old[z, here, :], now[z, padded, :], now[nz + z, padded, :]
            f2, a1 = centre[z], centre[nz + z]
            f3 = 2.0 * f2 - f1 + jnp.where(source, amplitude(1, z), 0.0)
            f3 = jnp.where(inside, f3, 0.0) + c * lap[z]
            a0 = jnp.where(inside, 2.0 * a1 - a2, 0.0) + c * lap[nz + z]
            part = a0 * (f2 - 2.0 * f1 + f0) + a1 * (f3 - 2.0 * f2 + f1)
            total = part if z % 2 == 0 else total + part
            if z % 2 == 1:
                image[z // 2, here, :] = total if keep is None else jnp.where(keep, total, 0.0)

    keep = (at_lane >= 4) & (at_lane < LANES - 4)

    def second_step(g, carry):
        at = pl.multiple_of(g * ROWS, ROWS)
        twice(at, [along[p, pl.ds(at, ROWS), :] for p in range(planes)], keep)
        return carry

    lax.fori_loop(1, groups - 1, second_step, 0)

    y_each(True, "wait_send")
    for side, (there, _) in enumerate(x_sides):
        @pl.when(there)
        def _(side=side):
            x_copy(1 - side, 0).wait_recv()
    y_each(False, "wait_recv")
    outer = [handed(p) for p in range(planes)]
    lack = jnp.dot(
        w_back[...], jnp.concatenate(split(jnp.concatenate(outer, 0)), 0), preferred_element_type=jnp.float32
    )
    gain = [held[p % nz] * lack[p * SUB : (p + 1) * SUB] for p in range(planes)]
    second = [middle[p] + gain[p] for p in range(planes)]
    spread = jnp.dot(
        w_near[...], jnp.concatenate(split(jnp.concatenate(gain, 0)), 0), preferred_element_type=jnp.float32
    )
    along_y = jnp.dot(
        jnp.concatenate(split(jnp.concatenate(second, 0)), 0), w_rows[...], preferred_element_type=jnp.float32
    )
    for p in range(planes):
        total = bent[p] + spread[p * SUB : (p + 1) * SUB] + RATIO[0] * second[p]
        total = total + along_y[p * SUB : (p + 1) * SUB]
        total = total + along_y[(planes + p) * SUB : (planes + p + 1) * SUB]
        for k, s in enumerate(vertical(second, p, [None] * 5)):
            if s is not None:
                total = total + (s if k == 1 else RATIO[k] * s)
        bent[p] = total
        middle[p] = second[p]
    deep = []
    for z in range(nz):
        f = spread[(planes + z) * SUB : (planes + z + 1) * SUB]
        a = spread[(planes + nz + z) * SUB : (planes + nz + z + 1) * SUB]
        deep.append(deep_held[z] * (a * deep_bent[z] + deep_late[z] * f))
    deep_sums[...] = jnp.concatenate([deep[2 * k] + deep[2 * k + 1] for k in range(nz // 2)], 0)

    span = 2 * ROWS
    columns = turned(outer)
    columns = jnp.concatenate([columns[:span], columns[LANES - span :]], 0)
    for q in range(nz):
        lack = jnp.dot(columns, w_join[q], preferred_element_type=jnp.float32)
        for side in range(2):
            p = 2 * q + side
            for v, at in enumerate((0, ny - span)):
                here = pl.ds(PAD + at, span)
                part = lack[v * span : (v + 1) * span, side * LANES : (side + 1) * LANES]
                mid[p, here, :] = mid[p, here, :] + speed[p % nz, pl.ds(at, span), :] * part
    for p in range(planes):
        for v in range(2):
            total = None
            for k in range(1, 5):
                term = RATIO[k] * yin[v, p, pl.ds(SUB - k if v == 0 else k, SUB), :]
                total = term if total is None else total + term
            at = 0 if v == 0 else ny - SUB
            here = pl.ds(PAD + at, SUB)
            mid[p, here, :] = mid[p, here, :] + speed[p % nz, pl.ds(at, SUB), :] * total
    tips = [mid[p, pl.ds(PAD + at, ROWS), :] for at in (0, ny - ROWS) for p in range(planes)]
    tips = dot(split(jnp.concatenate(tips, 0)), w_main[pl.ds(0, 2 * LANES)])
    for v in range(2):
        for p in range(planes):
            at = (v * planes + p) * ROWS
            along[p, pl.ds(v * ROWS, ROWS), :] = tips[at : at + ROWS]

    for i in range(4):
        @pl.when(diagonal[i][0])
        def _(i=i):
            corner_copy(3 - i).wait_recv()
    halves = [jnp.where(low, corner_in[2 * v], corner_in[2 * v + 1]) for v in range(2)]
    masked = [jnp.where(group == p, halves[v], 0.0) for v in range(2) for p in range(planes)]
    lack = dot(split(jnp.concatenate(masked, 0)), w_main[pl.ds(2 * LANES, 2 * LANES)])
    high, rest = split(jnp.concatenate(halves, 0))
    ends = lax.dot_general(
        jnp.concatenate([high, rest], 0), w_ends[...], (((0,), (0,)), ((), ())),
        preferred_element_type=jnp.float32,
    )
    for p in range(planes):
        reach[p] = reach[p] + ends[p * SUB : (p + 1) * SUB]
        for v in range(2):
            at = (v * planes + p) * SUB
            over[v, p] = over[v, p] + lack[at : at + SUB]

    for side, (there, _) in enumerate(x_sides):
        @pl.when(there)
        def _(side=side):
            x_copy(1 - side, 1).wait_recv()
    y_each(True, "wait_recv")
    outer = [handed(planes + p) + handed(2 * planes + p % nz) * reach[p] for p in range(planes)]
    lack = jnp.dot(
        w_back[...], jnp.concatenate(split(jnp.concatenate(outer, 0)), 0), preferred_element_type=jnp.float32
    )
    columns = turned(outer)
    columns = jnp.concatenate([columns[:ROWS], columns[LANES - ROWS :]], 0)
    found = [jnp.dot(columns, w_join[q], preferred_element_type=jnp.float32) for q in range(nz)]
    for v in range(2):
        here = pl.ds(0 if v == 0 else PAD + ny, SUB)
        rows = pl.ds(0 if v == 0 else SUB, SUB)
        for p in range(planes):
            mid[p, here, :] = yin[v, planes + p, rows, :] + yin[v, 2 * planes + p % nz, rows, :] * over[v, p]
    for v, at in enumerate((0, ny - ROWS)):
        here = pl.ds(v * ROWS, ROWS)
        twice(
            at,
            [
                along[p, here, :]
                + found[p // 2][v * ROWS : (v + 1) * ROWS, p % 2 * LANES : (p % 2 + 1) * LANES]
                for p in range(planes)
            ],
            None,
        )
    fixes = []
    for z in range(nz):
        f2, a1 = middle[z], middle[nz + z]
        f1, a2 = near[z], near[nz + z]
        f3 = 2.0 * f2 - f1 + jnp.where(edge_source, amplitude(1, z), 0.0)
        f3 = jnp.where(edge_inside, f3, 0.0) + held[z] * (bent[z] + lack[z * SUB : (z + 1) * SUB])
        a0 = jnp.where(edge_inside, 2.0 * a1 - a2, 0.0)
        a0 = a0 + held[z] * (bent[nz + z] + lack[(nz + z) * SUB : (nz + z + 1) * SUB])
        fixes.append(a0 * (f2 - 2.0 * f1 + prior[z]) + a1 * (f3 - 2.0 * f2 + f1))
    fixes = jnp.concatenate([fixes[2 * k] + fixes[2 * k + 1] for k in range(nz // 2)] + [deep_sums[...]], 0)
    both = jnp.dot(jnp.concatenate(split(fixes), 0), w_pairs[...], preferred_element_type=jnp.float32)
    fixes = both[: nz * SUB] + both[nz * SUB :]
    patch[...] = fixes

    rows = [
        image[k, pl.ds(0, half, stride=2), :] + image[k, pl.ds(1, half, stride=2), :] for k in range(nz // 2)
    ]
    cells = jnp.concatenate([x for k in range(nz // 2) for x in split(rows[k])], 1)
    total = lax.dot_general(
        w_pick[...], cells, (((1,), (1,)), ((), ())), preferred_element_type=jnp.float32
    )
    coarse[...] = total

    def exchange(ref, into, lane_of):
        copies = []
        for step in range(1, shots):
            copy = pltpu.make_async_remote_copy(
                src_ref=ref, dst_ref=into.at[step - 1],
                send_sem=shot_send.at[lane_of, step - 1], recv_sem=shot_recv.at[lane_of, step - 1],
                device_id={"shot": lax.rem(shot + step, shots)}, device_id_type=MESH,
            )
            copy.start()
            copies.append(copy)
        return copies

    sends = exchange(coarse, arrived, 0)

    sends = sends + exchange(patch, patches, 1)

    y_each(False, "wait_send")
    for side in range(2):
        @pl.when(x_sides[side][0])
        def _(side=side):
            for part in range(2):
                x_copy(side, part).wait_send()
    for i in range(4):
        @pl.when(diagonal[i][0])
        def _(i=i):
            corner_copy(i).wait_send()
    for copy in sends:
        copy.wait_recv()
    for step in range(shots - 1):
        total = total + arrived[step]
        fixes = fixes + patches[step]
    depth = top[0].astype(jnp.float32)
    width = LANES // 2
    for k in range(nz // 2):
        factor = (0.25 + (depth + (2.0 * k + 1.0)) / 128.0) * 0.125
        out_ref[k] = total[width * k : width * k + width] * factor
        for i, at in enumerate((width - 2, width - 1, 0, 1, width - 4, width - 3, 2, 3)):
            first = (k + i // 4 * (nz // 2)) * SUB + 2 * (i % 4)
            row = (fixes[first : first + 1] + fixes[first + 1 : first + 2]) * factor
            out_ref[k, pl.ds(at, 1), :] = out_ref[k, pl.ds(at, 1), :] + row
    for copy in sends:
        copy.wait_send()


def per_device(shots, counts, fwd_prev, fwd_cur, adj_late, adj_now, courant, wavelet, boxes, sources, slab_top):
    nz, ny, nx = courant.shape
    f32, b16 = jnp.float32, jnp.bfloat16
    planes = 2 * nz
    others = max(shots - 1, 1)
    hbm = pl.BlockSpec(memory_space=pltpu.HBM)
    dma = pltpu.SemaphoreType.DMA
    smalls = [pltpu.with_memory_space_constraint(x, pltpu.HBM) for x in (wavelet, boxes, sources)]
    out = pl.pallas_call(
        functools.partial(kernel, shots, counts),
        out_shape=jax.ShapeDtypeStruct((nz // 2, nx // 2, ny // 2), f32),
        in_specs=[hbm] * 9,
        out_specs=pl.BlockSpec(memory_space=pltpu.VMEM),
        scratch_shapes=[
            pltpu.SMEM((1, 2), f32),
            pltpu.SMEM((1, 4), jnp.int32),
            pltpu.SMEM((1, 3), jnp.int32),
            pltpu.SMEM((1,), jnp.int32),
            pltpu.VMEM((planes, ny + 2 * PAD, nx), f32),
            pltpu.VMEM((planes, ny + 2 * PAD, nx), f32),
            pltpu.VMEM((planes, ny, nx), f32),
            pltpu.VMEM((nz, ny, nx), f32),
            pltpu.VMEM((nz // 2, ny, nx), f32),
            pltpu.VMEM((ny, nx), f32),
            pltpu.VMEM((2, 2 * planes + nz, ROWS, nx), f32),
            pltpu.VMEM((2, planes, SUB, nx), f32),
            pltpu.VMEM((planes, ny, 2 * nx), b16),
            pltpu.VMEM((planes, ny, nx), f32),
            pltpu.VMEM((planes, SUB, ny), f32),
            pltpu.VMEM((planes, SUB, ny), f32),
            pltpu.VMEM((planes, SUB, ny), f32),
            pltpu.VMEM((planes, SUB, ny), f32),
            pltpu.VMEM((nz, SUB, ny), f32),
            pltpu.VMEM((planes, SUB, ny), f32),
            pltpu.VMEM((nz, SUB, ny), f32),
            pltpu.VMEM((nz, SUB, ny), f32),
            pltpu.VMEM((nz, SUB, ny), f32),
            pltpu.VMEM((nz // 2 * SUB, ny), f32),
            pltpu.VMEM((2, 4 * (2 * planes + nz), ny), f32),
            pltpu.VMEM((2, 4 * (2 * planes + nz), ny), f32),
            pltpu.VMEM((2, SUB, nx), f32),
            pltpu.VMEM((4, SUB, nx), f32),
            pltpu.VMEM((4 * nx, nx), b16),
            pltpu.VMEM((2 * ROWS, 2 * nx), b16),
            pltpu.VMEM((nz, nx, 2 * nx), b16),
            pltpu.VMEM((ny, ny), b16),
            pltpu.VMEM((2 * ROWS, ny), b16),
            pltpu.VMEM((planes * SUB, nx), b16),
            pltpu.VMEM((2 * planes * SUB, nx), b16),
            pltpu.VMEM((ny, ny // 2), b16),
            pltpu.VMEM((nx, nz * nx), b16),
            pltpu.VMEM((nx, ny // 2), f32),
            pltpu.VMEM((others, nx, ny // 2), f32),
            pltpu.VMEM((nz * SUB, ny // 2), f32),
            pltpu.VMEM((others, nz * SUB, ny // 2), f32),
            dma((4,)),
            dma((5,)),
            dma((2, 3)),
            dma((2, 3)),
            dma((2, 2)),
            dma((2, 2)),
            dma((4,)),
            dma((4,)),
            dma((2, others)),
            dma((2, others)),
        ],
        compiler_params=pltpu.CompilerParams(
            collective_id=0, has_side_effects=True, vmem_limit_bytes=54912 * 1024
        ),
    )(*smalls, slab_top, fwd_prev, fwd_cur, adj_late, adj_now, courant)
    return jnp.swapaxes(out, 1, 2)


def solution(mesh):
    shots = mesh.shape["shot"]
    counts = (mesh.shape["gy"], mesh.shape["gx"])
    return jax.shard_map(
        functools.partial(per_device, shots, counts),
        mesh=mesh,
        in_specs=(
            P("shot", None, "gy", "gx"),
            P("shot", None, "gy", "gx"),
            P("shot", None, "gy", "gx"),
            P("shot", None, "gy", "gx"),
            P(None, "gy", "gx"),
            P("shot", None),
            P("shot", None),
            P("shot", None),
            P(),
        ),
        out_specs=P(None, "gy", "gx"),
        check_vma=False,
    )
```

```python
import functools

import jax
import jax.numpy as jnp
from jax import lax
from jax.experimental import pallas as pl
from jax.experimental.pallas import tpu as pltpu
from jax.sharding import PartitionSpec as P

COEFFS = (-205.0 / 72.0, 8.0 / 5.0, -1.0 / 5.0, 8.0 / 315.0, -1.0 / 560.0)
LEAD = COEFFS[1]
RATIO = (3.0 * COEFFS[0] / LEAD, 1.0, COEFFS[2] / LEAD, COEFFS[3] / LEAD, COEFFS[4] / LEAD)
MESH = pl.DeviceIdType.MESH
PAD = 8
LANES = 128
ROWS = 16
SUB = 8


def kernel(
    shots, counts, wave_hbm, box_hbm, src_hbm, top_hbm, f0_hbm, f1_hbm, a3_hbm, a2_hbm, c_hbm, out_ref,
    wave, box, src, top, now, mid, old, speed, image, inner, yin, over, pieces, along,
    near, bent, reach, prior, held, middle, deep_bent, deep_late, deep_held, deep_sums, xs_out, xs_in, corner_out, corner_in, w_main, w_edge, w_join, w_rows,
    w_ends, w_back, w_near, w_pairs, w_pick, coarse, arrived, patch, patches,
    small_sem, load_sem, ysend, yrecv, xsend, xrecv, csend, crecv, shot_send, shot_recv,
):
    county, countx = counts
    nz, ny = speed.shape[0], speed.shape[1]
    planes = 2 * nz
    half = ny // 2
    groups = ny // ROWS
    gy, gx, shot = lax.axis_index("gy"), lax.axis_index("gx"), lax.axis_index("shot")
    has_up, has_down = gy > 0, gy < county - 1
    has_left, has_right = gx > 0, gx < countx - 1

    loads = []
    for i, (hbm, ref) in enumerate(
        (
            (f1_hbm.at[0], now.at[pl.ds(0, nz), pl.ds(PAD, ny)]),
            (a2_hbm.at[0], now.at[pl.ds(nz, nz), pl.ds(PAD, ny)]),
            (c_hbm, speed),
            (f0_hbm.at[0], old.at[pl.ds(0, nz)]),
            (a3_hbm.at[0], old.at[pl.ds(nz, nz)]),
        )
    ):
        loads.append(pltpu.make_async_copy(hbm, ref, load_sem.at[i]))
    smalls = []
    for i, (hbm, ref) in enumerate(((wave_hbm, wave), (box_hbm, box), (src_hbm, src), (top_hbm, top))):
        smalls.append(pltpu.make_async_copy(hbm, ref, small_sem.at[i]))
    for copy in loads[:2] + smalls + loads[2:]:
        copy.start()

    barrier = pltpu.get_barrier_semaphore()
    y_sides = [(has_up, {"gy": gy - 1}), (has_down, {"gy": gy + 1})]
    x_sides = [(has_left, {"gx": gx - 1}), (has_right, {"gx": gx + 1})]
    diagonal = [
        (v & h, {"gy": gy + dy, "gx": gx + dx})
        for v, dy in ((has_up, -1), (has_down, 1))
        for h, dx in ((has_left, -1), (has_right, 1))
    ]
    expected = shots - 1
    for there, device in y_sides + x_sides + diagonal:
        expected = expected + there.astype(jnp.int32)

        @pl.when(there)
        def _(device=device):
            pl.semaphore_signal(barrier, inc=1, device_id=device, device_id_type=MESH)
    for step in range(1, shots):
        pl.semaphore_signal(
            barrier, inc=1, device_id={"shot": lax.rem(shot + step, shots)}, device_id_type=MESH
        )

    for side, (there, _) in enumerate(y_sides):
        @pl.when(jnp.logical_not(there))
        def _(side=side):
            yin[side] = jnp.zeros(yin.shape[1:], jnp.float32)
    for side, (there, _) in enumerate(x_sides):
        @pl.when(jnp.logical_not(there))
        def _(side=side):
            xs_in[side] = jnp.zeros(xs_in.shape[1:], jnp.float32)
    for i, (there, _) in enumerate(diagonal):
        @pl.when(jnp.logical_not(there))
        def _(i=i):
            corner_in[i] = jnp.zeros((SUB, LANES), jnp.float32)

    for p in range(planes):
        nothing = jnp.zeros((SUB, LANES), jnp.float32)
        now[p, pl.ds(0, PAD), :] = nothing
        now[p, pl.ds(PAD + ny, PAD), :] = nothing
        yin[0, p, pl.ds(SUB, SUB), :] = nothing
        yin[1, p, pl.ds(0, SUB), :] = nothing

    lane = lax.broadcasted_iota(jnp.int32, (SUB, LANES), 1)
    group = lane >> 3
    low = (lane & 7) < 4

    def iotas(shape):
        return lax.broadcasted_iota(jnp.int32, shape, 0), lax.broadcasted_iota(jnp.int32, shape, 1)

    def table(distance, keep=None):
        weights = jnp.zeros(distance.shape, jnp.float32)
        for k in range(1, 5):
            hit = distance == k
            weights = jnp.where(hit if keep is None else keep & hit, RATIO[k], weights)
        return weights.astype(jnp.bfloat16)

    def inside_column(j):
        return jnp.where(j < 4, j + (LANES - 4), j - 4)

    def outside_column(j):
        return jnp.where(j < 4, j - 4, j + (LANES - 4))

    def deep_inside(j):
        return jnp.where(j < 4, j + (LANES - 8), j)

    ri, ci = iotas((LANES, LANES))
    weights = table(jnp.abs(ri - ci))
    w_main[pl.ds(0, LANES)] = weights
    w_main[pl.ds(LANES, LANES)] = weights
    weights = table(jnp.abs(outside_column(ri & 7) - ci))
    w_main[pl.ds(2 * LANES, LANES)] = weights
    w_main[pl.ds(3 * LANES, LANES)] = weights
    ri, ci = iotas((SUB, LANES))
    own_column = inside_column(ri)
    deep_column = deep_inside(ri)
    for part, rows in enumerate(
        (
            (own_column == ci).astype(jnp.float32).astype(jnp.bfloat16),
            table(jnp.abs(own_column - ci)),
            table(jnp.abs(outside_column(ri) - ci)),
            (deep_column == ci).astype(jnp.float32).astype(jnp.bfloat16),
        )
    ):
        if part % 2 == 0:
            first = rows
        else:
            both = jnp.concatenate([first.astype(jnp.float32), rows.astype(jnp.float32)], 0)
            both = both.astype(jnp.bfloat16)
            w_edge[pl.ds(part // 2 * ROWS, ROWS), pl.ds(0, LANES)] = both
            w_edge[pl.ds(part // 2 * ROWS, ROWS), pl.ds(LANES, LANES)] = both
    ri, ci = iotas((LANES, 2 * LANES))
    weights = table(jnp.abs(outside_column(ri & 7) - (ci & (LANES - 1)))).astype(jnp.float32)
    plane = (ri >> 3) & (planes - 1)
    for q in range(nz):
        w_join[q] = jnp.where(plane == 2 * q + (ci >> 7), weights, 0.0).astype(jnp.bfloat16)
    ri, ci = iotas((ny, ny))
    w_rows[...] = table(jnp.abs(ri - ci))
    ri, ci = iotas((ROWS, ny))
    weights = table(jnp.abs(jnp.where(ri < SUB, ri - SUB, ri + (ny - SUB)) - ci))
    w_ends[pl.ds(0, ROWS)] = weights
    w_ends[pl.ds(ROWS, ROWS)] = weights

    ri, ci = iotas((planes * SUB, LANES))
    weights = table(jnp.abs(inside_column(ri & 7) - outside_column(ci & 7)), ri >> 3 == (ci >> 3 & (planes - 1)))
    w_back[...] = weights
    same = ri >> 3 == (ci >> 3 & (planes - 1))
    source_column = inside_column(ci & 7)
    w_near[pl.ds(0, planes * SUB)] = table(jnp.abs(inside_column(ri & 7) - source_column), same)
    w_near[pl.ds(planes * SUB, planes * SUB)] = table(jnp.abs(deep_inside(ri & 7) - source_column), same)
    ri, ci = iotas((ny, half))
    w_pairs[...] = ((ri >> 1 == ci) & (ri >= ROWS) & (ri < ny - ROWS)).astype(jnp.float32).astype(jnp.bfloat16)
    ri, ci = iotas((LANES, 2 * nz // 2 * LANES))
    hit = (ri & 63 == (ci & (LANES - 1)) >> 1) & (ri >> 6 == ci >> 8)
    w_pick[...] = hit.astype(jnp.float32).astype(jnp.bfloat16)

    def split(x):
        high = x.astype(jnp.bfloat16)
        return high, (x - high.astype(jnp.float32)).astype(jnp.bfloat16)

    def dot(pieces, weights):
        return jnp.dot(jnp.concatenate(pieces, 1), weights, preferred_element_type=jnp.float32)

    def edges(rows, cells):
        return lax.dot_general(
            w_edge[pl.ds(0, rows)], cells, (((1,), (1,)), ((), ())), preferred_element_type=jnp.float32
        )

    def parts(x):
        return [x[p * ROWS : (p + 1) * ROWS] for p in range(planes)]

    def hand(i, value):
        xs_out[1, pl.ds(4 * i, 4)] = value[:4]
        xs_out[0, pl.ds(4 * i, 4)] = value[4:]

    def handed(i):
        return jnp.concatenate([xs_in[0, pl.ds(4 * i, 4)], xs_in[1, pl.ds(4 * i, 4)]], 0)

    def turned(values):
        values = jnp.concatenate(values, 0)
        first = lax.broadcasted_iota(jnp.int32, (values.shape[0], LANES), 1) < LANES // 2
        high, rest = split(jnp.where(first, values[:, :LANES], values[:, LANES:]))
        both = jnp.concatenate([high.astype(jnp.float32), rest.astype(jnp.float32)], 0)
        return both.T.astype(jnp.bfloat16)

    def y_copies(side, late):
        start = 0 if side == 0 else ny - 4
        padded, bare = pl.ds(PAD + start, 4), pl.ds(start, 4)
        sources = [(now, padded, planes), (mid, padded, planes), (speed, bare, nz)]
        arrive = pl.ds(SUB, 4) if side == 0 else pl.ds(4, 4)
        return [
            pltpu.make_async_remote_copy(
                src_ref=sources[i][0].at[:, sources[i][1], :],
                dst_ref=yin.at[1 - side, pl.ds(planes * i, sources[i][2]), arrive, :],
                send_sem=ysend.at[side, i], recv_sem=yrecv.at[1 - side, i],
                device_id=y_sides[side][1], device_id_type=MESH,
            )
            for i in ((1, 2) if late else (0,))
        ]

    def y_each(late, action):
        for side in range(2):
            @pl.when(y_sides[side][0])
            def _(side=side):
                for copy in y_copies(side if action != "wait_recv" else 1 - side, late):
                    getattr(copy, action)()

    def x_copy(side, part):
        device = x_sides[side][1]
        rows = pl.ds(0, 4 * planes) if part == 0 else pl.ds(4 * planes, 4 * (planes + nz))
        return pltpu.make_async_remote_copy(
            src_ref=xs_out.at[side, rows], dst_ref=xs_in.at[1 - side, rows],
            send_sem=xsend.at[side, part], recv_sem=xrecv.at[1 - side, part],
            device_id=device, device_id_type=MESH,
        )

    def corner_copy(i):
        return pltpu.make_async_remote_copy(
            src_ref=corner_out.at[i // 2], dst_ref=corner_in.at[3 - i],
            send_sem=csend.at[i], recv_sem=crecv.at[3 - i],
            device_id=diagonal[i][1], device_id_type=MESH,
        )

    body = pl.ds(PAD, ny)
    for f in range(2):
        loads[f].wait()
        for p in range(f * nz, (f + 1) * nz):
            cells = jnp.concatenate(split(now[p, body, :]), 1)
            pieces[p] = cells
            found = edges(2 * ROWS, cells)
            near[p] = found[:SUB]
            bent[p] = found[SUB : 2 * SUB]
            reach[p] = found[2 * SUB : 3 * SUB]
            if p < nz:
                deep_bent[p] = -2.0 * found[3 * SUB :]
            hand(p, found[:SUB])
    upper = jnp.zeros((SUB, LANES), jnp.float32)
    lower = upper
    for p in range(planes):
        shift = (8 * p + 4) % LANES
        upper = jnp.where(group == p, pltpu.roll(now[p, pl.ds(PAD, SUB), :], shift, 1), upper)
        lower = jnp.where(group == p, pltpu.roll(now[p, pl.ds(ny, SUB), :], shift, 1), lower)
    corner_out[0] = upper
    corner_out[1] = lower

    for copy in smalls:
        copy.wait()
    y0, y1, x0, x1 = box[0, 0], box[0, 1], box[0, 2], box[0, 3]
    sz, sy, sx = src[0, 0], src[0, 1], src[0, 2]

    def inside_of(cell_y, cell_x):
        inside = (cell_x >= x0) & (cell_x < x1) & (cell_y >= y0) & (cell_y < y1)
        return inside, (cell_x == sx) & (cell_y == sy)

    def place(at, rows):
        cell_y = gy * ny + at + lax.broadcasted_iota(jnp.int32, (rows, LANES), 0)
        cell_x = gx * LANES + lax.broadcasted_iota(jnp.int32, (rows, LANES), 1)
        return inside_of(cell_y, cell_x)

    def amplitude(step, z):
        return jnp.where(sz == z, wave[0, step], 0.0)

    def vertical(values, p, total):
        z = p % nz
        for k in range(1, 5):
            s = None
            for d in (z + k, z - k):
                if 0 <= d < nz:
                    s = values[p - z + d] if s is None else s + values[p - z + d]
            if s is not None:
                total[k] = s if total[k] is None else total[k] + s
        return total

    def combine(cells, centre, along_x):
        result = []
        for p in range(planes):
            sums = vertical(centre, p, [None] * 5)
            total = along_x[p] + RATIO[0] * centre[p]
            for k in range(1, 5):
                s = cells(p, k) + cells(p, -k)
                if sums[k] is not None:
                    s = s + sums[k]
                total = total + (s if k == 1 else RATIO[k] * s)
            result.append(total)
        return result

    at_y, at_x = iotas((ny, LANES))
    inside, _ = inside_of(gy * ny + at_y, gx * LANES + at_x)
    inner[...] = jnp.where(inside, LEAD, 0.0)
    row, at_y = iotas((SUB, ny))
    edge_inside, edge_source = inside_of(gy * ny + at_y, gx * LANES + inside_column(row))
    at_lane = lax.broadcasted_iota(jnp.int32, (ROWS, LANES), 1)
    loads[2].wait()
    for z in range(nz):
        scaled = speed[z] * inner[...]
        speed[z] = scaled
        found = edges(2 * ROWS, jnp.concatenate(split(scaled), 1))
        deep_held[z] = found[3 * SUB :]
        found = found[:SUB]
        held[z] = found
        hand(2 * planes + z, found)
    tips = [pieces[p, pl.ds(at, ROWS), :] for at in (0, ny - ROWS) for p in range(planes)]
    tips = jnp.dot(jnp.concatenate(tips, 0), w_main[pl.ds(0, 2 * LANES)], preferred_element_type=jnp.float32)
    centre = [near[p] for p in range(planes)]
    high, rest = split(jnp.concatenate(centre, 0))
    along_y = jnp.dot(jnp.concatenate([high, rest], 0), w_rows[...], preferred_element_type=jnp.float32)
    for f in range(2):
        if f == 1:
            pl.semaphore_wait(barrier, expected)
            for i in range(4):
                @pl.when(diagonal[i][0])
                def _(i=i):
                    corner_copy(i).start()
            for side in range(2):
                @pl.when(x_sides[side][0])
                def _(side=side):
                    x_copy(side, 0).start()
            y_each(False, "start")
        loads[3 + f].wait()
        for z in range(nz):
            p = f * nz + z
            before = edges(2 * ROWS if f == 0 else ROWS, jnp.concatenate(split(old[p]), 1))
            if f == 0:
                deep_bent[p] = deep_bent[p] + before[3 * SUB :]
            before = before[:SUB]
            prior[p] = before
            total = bent[p] + RATIO[0] * centre[p]
            total = total + along_y[p * SUB : (p + 1) * SUB]
            total = total + along_y[(planes + p) * SUB : (planes + p + 1) * SUB]
            for k, s in enumerate(vertical(centre, p, [None] * 5)):
                if s is not None:
                    total = total + (s if k == 1 else RATIO[k] * s)
            value = 2.0 * centre[p] - before
            if f == 0:
                value = value + jnp.where(edge_source, amplitude(0, z), 0.0)
            hand(planes + p, jnp.where(edge_inside, value, 0.0) + held[z] * total)
    for side in range(2):
        @pl.when(x_sides[side][0])
        def _(side=side):
            x_copy(side, 1).start()

    def advance(at, along_x):
        inside, source = place(at, ROWS)
        here = pl.ds(at, ROWS)
        cells = lambda p, k: now[p, pl.ds(at + PAD + k, ROWS), :]
        centre = [cells(p, 0) for p in range(planes)]
        lap = combine(cells, centre, along_x)
        scales = [speed[z, here, :] for z in range(nz)]
        for p in range(planes):
            new = 2.0 * centre[p] - old[p, here, :]
            if p < nz:
                new = new + jnp.where(source, amplitude(0, p), 0.0)
            mid[p, pl.ds(at + PAD, ROWS), :] = jnp.where(inside, new, 0.0) + scales[p % nz] * lap[p]

    advance(0, parts(tips[: planes * ROWS]))
    advance(ny - ROWS, parts(tips[planes * ROWS :]))

    y_each(True, "start")


    def first_step(i, carry):
        at = pl.multiple_of(i * ROWS, ROWS)
        advance(at, [along[p, pl.ds(at, ROWS), :] for p in range(planes)])
        return carry

    for p in range(planes):
        along[p] = jnp.dot(pieces[p], w_main[pl.ds(0, 2 * LANES)], preferred_element_type=jnp.float32)
    lax.fori_loop(1, groups - 1, first_step, 0)

    for p in range(planes):
        for v in range(2):
            total = None
            for k in range(1, 5):
                term = RATIO[k] * now[p, pl.ds(k if v == 0 else PAD + ny - k, SUB), :]
                total = term if total is None else total + term
            over[v, p] = total

    for p in range(planes):
        cells = jnp.concatenate(split(mid[p, body, :]), 1)
        along[p] = jnp.dot(cells, w_main[pl.ds(0, 2 * LANES)], preferred_element_type=jnp.float32)
        found = edges(2 * ROWS, cells)
        middle[p] = found[:SUB]
        bent[p] = found[SUB : 2 * SUB]
        if p < nz:
            deep_bent[p] = deep_bent[p] + found[3 * SUB :]
        else:
            deep_late[p - nz] = found[3 * SUB :]

    def twice(at, along_x, keep):
        here, padded = pl.ds(at, ROWS), pl.ds(at + PAD, ROWS)
        inside, source = place(at, ROWS)
        centre = [mid[p, padded, :] for p in range(planes)]
        lap = combine(lambda p, k: mid[p, pl.ds(at + PAD + k, ROWS), :], centre, along_x)
        total = None
        for z in range(nz):
            c = speed[z, here, :]
            f0, f1, a2 = old[z, here, :], now[z, padded, :], now[nz + z, padded, :]
            f2, a1 = centre[z], centre[nz + z]
            f3 = 2.0 * f2 - f1 + jnp.where(source, amplitude(1, z), 0.0)
            f3 = jnp.where(inside, f3, 0.0) + c * lap[z]
            a0 = jnp.where(inside, 2.0 * a1 - a2, 0.0) + c * lap[nz + z]
            part = a0 * (f2 - 2.0 * f1 + f0) + a1 * (f3 - 2.0 * f2 + f1)
            total = part if z % 2 == 0 else total + part
            if z % 2 == 1:
                image[z // 2, here, :] = total if keep is None else jnp.where(keep, total, 0.0)

    keep = (at_lane >= 4) & (at_lane < LANES - 4)

    def second_step(g, carry):
        at = pl.multiple_of(g * ROWS, ROWS)
        twice(at, [along[p, pl.ds(at, ROWS), :] for p in range(planes)], keep)
        return carry

    lax.fori_loop(1, groups - 1, second_step, 0)

    y_each(True, "wait_send")
    for side, (there, _) in enumerate(x_sides):
        @pl.when(there)
        def _(side=side):
            x_copy(1 - side, 0).wait_recv()
    y_each(False, "wait_recv")
    outer = [handed(p) for p in range(planes)]
    lack = jnp.dot(
        w_back[...], jnp.concatenate(split(jnp.concatenate(outer, 0)), 0), preferred_element_type=jnp.float32
    )
    gain = [held[p % nz] * lack[p * SUB : (p + 1) * SUB] for p in range(planes)]
    second = [middle[p] + gain[p] for p in range(planes)]
    spread = jnp.dot(
        w_near[...], jnp.concatenate(split(jnp.concatenate(gain, 0)), 0), preferred_element_type=jnp.float32
    )
    along_y = jnp.dot(
        jnp.concatenate(split(jnp.concatenate(second, 0)), 0), w_rows[...], preferred_element_type=jnp.float32
    )
    for p in range(planes):
        total = bent[p] + spread[p * SUB : (p + 1) * SUB] + RATIO[0] * second[p]
        total = total + along_y[p * SUB : (p + 1) * SUB]
        total = total + along_y[(planes + p) * SUB : (planes + p + 1) * SUB]
        for k, s in enumerate(vertical(second, p, [None] * 5)):
            if s is not None:
                total = total + (s if k == 1 else RATIO[k] * s)
        bent[p] = total
        middle[p] = second[p]
    deep = []
    for z in range(nz):
        f = spread[(planes + z) * SUB : (planes + z + 1) * SUB]
        a = spread[(planes + nz + z) * SUB : (planes + nz + z + 1) * SUB]
        deep.append(deep_held[z] * (a * deep_bent[z] + deep_late[z] * f))
    deep_sums[...] = jnp.concatenate([deep[2 * k] + deep[2 * k + 1] for k in range(nz // 2)], 0)

    span = 2 * ROWS
    columns = turned(outer)
    columns = jnp.concatenate([columns[:span], columns[LANES - span :]], 0)
    for q in range(nz):
        lack = jnp.dot(columns, w_join[q], preferred_element_type=jnp.float32)
        for side in range(2):
            p = 2 * q + side
            for v, at in enumerate((0, ny - span)):
                here = pl.ds(PAD + at, span)
                part = lack[v * span : (v + 1) * span, side * LANES : (side + 1) * LANES]
                mid[p, here, :] = mid[p, here, :] + speed[p % nz, pl.ds(at, span), :] * part
    for p in range(planes):
        for v in range(2):
            total = None
            for k in range(1, 5):
                term = RATIO[k] * yin[v, p, pl.ds(SUB - k if v == 0 else k, SUB), :]
                total = term if total is None else total + term
            at = 0 if v == 0 else ny - SUB
            here = pl.ds(PAD + at, SUB)
            mid[p, here, :] = mid[p, here, :] + speed[p % nz, pl.ds(at, SUB), :] * total
    tips = [mid[p, pl.ds(PAD + at, ROWS), :] for at in (0, ny - ROWS) for p in range(planes)]
    tips = dot(split(jnp.concatenate(tips, 0)), w_main[pl.ds(0, 2 * LANES)])
    for v in range(2):
        for p in range(planes):
            at = (v * planes + p) * ROWS
            along[p, pl.ds(v * ROWS, ROWS), :] = tips[at : at + ROWS]

    for side, (there, _) in enumerate(x_sides):
        @pl.when(there)
        def _(side=side):
            x_copy(1 - side, 1).wait_recv()
    y_each(True, "wait_recv")
    for i in range(4):
        @pl.when(diagonal[i][0])
        def _(i=i):
            corner_copy(3 - i).wait_recv()
    halves = [jnp.where(low, corner_in[2 * v], corner_in[2 * v + 1]) for v in range(2)]
    masked = [jnp.where(group == p, halves[v], 0.0) for v in range(2) for p in range(planes)]
    halo = dot(split(jnp.concatenate(masked, 0)), w_main[pl.ds(2 * LANES, 2 * LANES)])
    high, rest = split(jnp.concatenate(halves, 0))
    ends = lax.dot_general(
        jnp.concatenate([high, rest], 0), w_ends[...], (((0,), (0,)), ((), ())),
        preferred_element_type=jnp.float32,
    )
    for p in range(planes):
        for v in range(2):
            at = (v * planes + p) * SUB
            over[v, p] = over[v, p] + halo[at : at + SUB]
    outer = [handed(planes + p) + handed(2 * planes + p % nz) * reach[p] for p in range(planes)]
    lack = jnp.dot(
        w_back[...], jnp.concatenate(split(jnp.concatenate(outer, 0)), 0), preferred_element_type=jnp.float32
    )
    columns = turned(
        [outer[p] + handed(2 * planes + p % nz) * ends[p * SUB : (p + 1) * SUB] for p in range(planes)]
    )
    columns = jnp.concatenate([columns[:ROWS], columns[LANES - ROWS :]], 0)
    found = [jnp.dot(columns, w_join[q], preferred_element_type=jnp.float32) for q in range(nz)]
    for v in range(2):
        here = pl.ds(0 if v == 0 else PAD + ny, SUB)
        rows = pl.ds(0 if v == 0 else SUB, SUB)
        for p in range(planes):
            mid[p, here, :] = yin[v, planes + p, rows, :] + yin[v, 2 * planes + p % nz, rows, :] * over[v, p]
    for v, at in enumerate((0, ny - ROWS)):
        here = pl.ds(v * ROWS, ROWS)
        twice(
            at,
            [
                along[p, here, :]
                + found[p // 2][v * ROWS : (v + 1) * ROWS, p % 2 * LANES : (p % 2 + 1) * LANES]
                for p in range(planes)
            ],
            None,
        )
    fixes = []
    for z in range(nz):
        f2, a1 = middle[z], middle[nz + z]
        f1, a2 = near[z], near[nz + z]
        f3 = 2.0 * f2 - f1 + jnp.where(edge_source, amplitude(1, z), 0.0)
        f3 = jnp.where(edge_inside, f3, 0.0) + held[z] * (bent[z] + lack[z * SUB : (z + 1) * SUB])
        a0 = jnp.where(edge_inside, 2.0 * a1 - a2, 0.0)
        a0 = a0 + held[z] * (bent[nz + z] + lack[(nz + z) * SUB : (nz + z + 1) * SUB])
        fixes.append(a0 * (f2 - 2.0 * f1 + prior[z]) + a1 * (f3 - 2.0 * f2 + f1))
    fixes = jnp.concatenate([fixes[2 * k] + fixes[2 * k + 1] for k in range(nz // 2)] + [deep_sums[...]], 0)
    both = jnp.dot(jnp.concatenate(split(fixes), 0), w_pairs[...], preferred_element_type=jnp.float32)
    fixes = both[: nz * SUB] + both[nz * SUB :]
    patch[...] = fixes

    rows = [
        image[k, pl.ds(0, half, stride=2), :] + image[k, pl.ds(1, half, stride=2), :] for k in range(nz // 2)
    ]
    cells = jnp.concatenate([x for k in range(nz // 2) for x in split(rows[k])], 1)
    total = lax.dot_general(
        w_pick[...], cells, (((1,), (1,)), ((), ())), preferred_element_type=jnp.float32
    )
    coarse[...] = total

    def exchange(ref, into, lane_of):
        copies = []
        for step in range(1, shots):
            copy = pltpu.make_async_remote_copy(
                src_ref=ref, dst_ref=into.at[step - 1],
                send_sem=shot_send.at[lane_of, step - 1], recv_sem=shot_recv.at[lane_of, step - 1],
                device_id={"shot": lax.rem(shot + step, shots)}, device_id_type=MESH,
            )
            copy.start()
            copies.append(copy)
        return copies

    sends = exchange(coarse, arrived, 0)

    sends = sends + exchange(patch, patches, 1)

    y_each(False, "wait_send")
    for side in range(2):
        @pl.when(x_sides[side][0])
        def _(side=side):
            for part in range(2):
                x_copy(side, part).wait_send()
    for i in range(4):
        @pl.when(diagonal[i][0])
        def _(i=i):
            corner_copy(i).wait_send()
    for copy in sends:
        copy.wait_recv()
    for step in range(shots - 1):
        total = total + arrived[step]
        fixes = fixes + patches[step]
    depth = top[0].astype(jnp.float32)
    width = LANES // 2
    for k in range(nz // 2):
        factor = (0.25 + (depth + (2.0 * k + 1.0)) / 128.0) * 0.125
        out_ref[k] = total[width * k : width * k + width] * factor
        for i, at in enumerate((width - 2, width - 1, 0, 1, width - 4, width - 3, 2, 3)):
            first = (k + i // 4 * (nz // 2)) * SUB + 2 * (i % 4)
            row = (fixes[first : first + 1] + fixes[first + 1 : first + 2]) * factor
            out_ref[k, pl.ds(at, 1), :] = out_ref[k, pl.ds(at, 1), :] + row
    for copy in sends:
        copy.wait_send()


def per_device(shots, counts, fwd_prev, fwd_cur, adj_late, adj_now, courant, wavelet, boxes, sources, slab_top):
    nz, ny, nx = courant.shape
    f32, b16 = jnp.float32, jnp.bfloat16
    planes = 2 * nz
    others = max(shots - 1, 1)
    hbm = pl.BlockSpec(memory_space=pltpu.HBM)
    dma = pltpu.SemaphoreType.DMA
    smalls = [pltpu.with_memory_space_constraint(x, pltpu.HBM) for x in (wavelet, boxes, sources)]
    out = pl.pallas_call(
        functools.partial(kernel, shots, counts),
        out_shape=jax.ShapeDtypeStruct((nz // 2, nx // 2, ny // 2), f32),
        in_specs=[hbm] * 9,
        out_specs=pl.BlockSpec(memory_space=pltpu.VMEM),
        scratch_shapes=[
            pltpu.SMEM((1, 2), f32),
            pltpu.SMEM((1, 4), jnp.int32),
            pltpu.SMEM((1, 3), jnp.int32),
            pltpu.SMEM((1,), jnp.int32),
            pltpu.VMEM((planes, ny + 2 * PAD, nx), f32),
            pltpu.VMEM((planes, ny + 2 * PAD, nx), f32),
            pltpu.VMEM((planes, ny, nx), f32),
            pltpu.VMEM((nz, ny, nx), f32),
            pltpu.VMEM((nz // 2, ny, nx), f32),
            pltpu.VMEM((ny, nx), f32),
            pltpu.VMEM((2, 2 * planes + nz, ROWS, nx), f32),
            pltpu.VMEM((2, planes, SUB, nx), f32),
            pltpu.VMEM((planes, ny, 2 * nx), b16),
            pltpu.VMEM((planes, ny, nx), f32),
            pltpu.VMEM((planes, SUB, ny), f32),
            pltpu.VMEM((planes, SUB, ny), f32),
            pltpu.VMEM((planes, SUB, ny), f32),
            pltpu.VMEM((planes, SUB, ny), f32),
            pltpu.VMEM((nz, SUB, ny), f32),
            pltpu.VMEM((planes, SUB, ny), f32),
            pltpu.VMEM((nz, SUB, ny), f32),
            pltpu.VMEM((nz, SUB, ny), f32),
            pltpu.VMEM((nz, SUB, ny), f32),
            pltpu.VMEM((nz // 2 * SUB, ny), f32),
            pltpu.VMEM((2, 4 * (2 * planes + nz), ny), f32),
            pltpu.VMEM((2, 4 * (2 * planes + nz), ny), f32),
            pltpu.VMEM((2, SUB, nx), f32),
            pltpu.VMEM((4, SUB, nx), f32),
            pltpu.VMEM((4 * nx, nx), b16),
            pltpu.VMEM((2 * ROWS, 2 * nx), b16),
            pltpu.VMEM((nz, nx, 2 * nx), b16),
            pltpu.VMEM((ny, ny), b16),
            pltpu.VMEM((2 * ROWS, ny), b16),
            pltpu.VMEM((planes * SUB, nx), b16),
            pltpu.VMEM((2 * planes * SUB, nx), b16),
            pltpu.VMEM((ny, ny // 2), b16),
            pltpu.VMEM((nx, nz * nx), b16),
            pltpu.VMEM((nx, ny // 2), f32),
            pltpu.VMEM((others, nx, ny // 2), f32),
            pltpu.VMEM((nz * SUB, ny // 2), f32),
            pltpu.VMEM((others, nz * SUB, ny // 2), f32),
            dma((4,)),
            dma((5,)),
            dma((2, 3)),
            dma((2, 3)),
            dma((2, 2)),
            dma((2, 2)),
            dma((4,)),
            dma((4,)),
            dma((2, others)),
            dma((2, others)),
        ],
        compiler_params=pltpu.CompilerParams(
            collective_id=0, has_side_effects=True, vmem_limit_bytes=54912 * 1024
        ),
    )(*smalls, slab_top, fwd_prev, fwd_cur, adj_late, adj_now, courant)
    return jnp.swapaxes(out, 1, 2)


def solution(mesh):
    shots = mesh.shape["shot"]
    counts = (mesh.shape["gy"], mesh.shape["gx"])
    return jax.shard_map(
        functools.partial(per_device, shots, counts),
        mesh=mesh,
        in_specs=(
            P("shot", None, "gy", "gx"),
            P("shot", None, "gy", "gx"),
            P("shot", None, "gy", "gx"),
            P("shot", None, "gy", "gx"),
            P(None, "gy", "gx"),
            P("shot", None),
            P("shot", None),
            P("shot", None),
            P(),
        ),
        out_specs=P(None, "gy", "gx"),
        check_vma=False,
    )
```

```python
import functools

import jax
import jax.numpy as jnp
from jax import lax
from jax.experimental import pallas as pl
from jax.experimental.pallas import tpu as pltpu
from jax.sharding import PartitionSpec as P

COEFFS = (-205.0 / 72.0, 8.0 / 5.0, -1.0 / 5.0, 8.0 / 315.0, -1.0 / 560.0)
LEAD = COEFFS[1]
RATIO = (3.0 * COEFFS[0] / LEAD, 1.0, COEFFS[2] / LEAD, COEFFS[3] / LEAD, COEFFS[4] / LEAD)
MESH = pl.DeviceIdType.MESH
PAD = 8
LANES = 128
ROWS = 16
SUB = 8


def kernel(
    shots, counts, wave_hbm, box_hbm, src_hbm, top_hbm, f0_hbm, f1_hbm, a3_hbm, a2_hbm, c_hbm, out_ref,
    wave, box, src, top, now, mid, old, speed, image, inner, yin, over, pieces, along,
    near, bent, reach, prior, held, middle, deep_bent, deep_late, deep_held, deep_sums, xs_out, xs_in, corner_out, corner_in, w_main, w_edge, w_join, w_rows,
    w_ends, w_back, w_near, w_pairs, w_pick, coarse, arrived, patch, patches,
    small_sem, load_sem, ysend, yrecv, xsend, xrecv, csend, crecv, shot_send, shot_recv,
):
    county, countx = counts
    nz, ny = speed.shape[0], speed.shape[1]
    planes = 2 * nz
    half = ny // 2
    groups = ny // ROWS
    gy, gx, shot = lax.axis_index("gy"), lax.axis_index("gx"), lax.axis_index("shot")
    has_up, has_down = gy > 0, gy < county - 1
    has_left, has_right = gx > 0, gx < countx - 1

    loads = []
    for i, (hbm, ref) in enumerate(
        (
            (f1_hbm.at[0], now.at[pl.ds(0, nz), pl.ds(PAD, ny)]),
            (a2_hbm.at[0], now.at[pl.ds(nz, nz), pl.ds(PAD, ny)]),
            (c_hbm, speed),
            (f0_hbm.at[0], old.at[pl.ds(0, nz)]),
            (a3_hbm.at[0], old.at[pl.ds(nz, nz)]),
        )
    ):
        loads.append(pltpu.make_async_copy(hbm, ref, load_sem.at[i]))
    smalls = []
    for i, (hbm, ref) in enumerate(((wave_hbm, wave), (box_hbm, box), (src_hbm, src), (top_hbm, top))):
        smalls.append(pltpu.make_async_copy(hbm, ref, small_sem.at[i]))
    for copy in loads[:2] + smalls + loads[2:]:
        copy.start()

    barrier = pltpu.get_barrier_semaphore()
    y_sides = [(has_up, {"gy": gy - 1}), (has_down, {"gy": gy + 1})]
    x_sides = [(has_left, {"gx": gx - 1}), (has_right, {"gx": gx + 1})]
    diagonal = [
        (v & h, {"gy": gy + dy, "gx": gx + dx})
        for v, dy in ((has_up, -1), (has_down, 1))
        for h, dx in ((has_left, -1), (has_right, 1))
    ]
    expected = shots - 1
    for there, device in y_sides + x_sides + diagonal:
        expected = expected + there.astype(jnp.int32)

        @pl.when(there)
        def _(device=device):
            pl.semaphore_signal(barrier, inc=1, device_id=device, device_id_type=MESH)
    for step in range(1, shots):
        pl.semaphore_signal(
            barrier, inc=1, device_id={"shot": lax.rem(shot + step, shots)}, device_id_type=MESH
        )

    for side, (there, _) in enumerate(y_sides):
        @pl.when(jnp.logical_not(there))
        def _(side=side):
            yin[side] = jnp.zeros(yin.shape[1:], jnp.float32)
    for side, (there, _) in enumerate(x_sides):
        @pl.when(jnp.logical_not(there))
        def _(side=side):
            xs_in[side] = jnp.zeros(xs_in.shape[1:], jnp.float32)
    for i, (there, _) in enumerate(diagonal):
        @pl.when(jnp.logical_not(there))
        def _(i=i):
            corner_in[i] = jnp.zeros((SUB, LANES), jnp.float32)

    for p in range(planes):
        nothing = jnp.zeros((SUB, LANES), jnp.float32)
        now[p, pl.ds(0, PAD), :] = nothing
        now[p, pl.ds(PAD + ny, PAD), :] = nothing
        yin[0, p, pl.ds(SUB, SUB), :] = nothing
        yin[1, p, pl.ds(0, SUB), :] = nothing

    lane = lax.broadcasted_iota(jnp.int32, (SUB, LANES), 1)
    group = lane >> 3
    low = (lane & 7) < 4

    def iotas(shape):
        return lax.broadcasted_iota(jnp.int32, shape, 0), lax.broadcasted_iota(jnp.int32, shape, 1)

    def table(distance, keep=None):
        weights = jnp.zeros(distance.shape, jnp.float32)
        for k in range(1, 5):
            hit = distance == k
            weights = jnp.where(hit if keep is None else keep & hit, RATIO[k], weights)
        return weights.astype(jnp.bfloat16)

    def inside_column(j):
        return jnp.where(j < 4, j + (LANES - 4), j - 4)

    def outside_column(j):
        return jnp.where(j < 4, j - 4, j + (LANES - 4))

    def deep_inside(j):
        return jnp.where(j < 4, j + (LANES - 8), j)

    ri, ci = iotas((LANES, LANES))
    weights = table(jnp.abs(ri - ci))
    w_main[pl.ds(0, LANES)] = weights
    w_main[pl.ds(LANES, LANES)] = weights
    weights = table(jnp.abs(outside_column(ri & 7) - ci))
    w_main[pl.ds(2 * LANES, LANES)] = weights
    w_main[pl.ds(3 * LANES, LANES)] = weights
    ri, ci = iotas((SUB, LANES))
    own_column = inside_column(ri)
    deep_column = deep_inside(ri)
    for part, rows in enumerate(
        (
            (own_column == ci).astype(jnp.float32).astype(jnp.bfloat16),
            table(jnp.abs(own_column - ci)),
            table(jnp.abs(outside_column(ri) - ci)),
            (deep_column == ci).astype(jnp.float32).astype(jnp.bfloat16),
        )
    ):
        if part % 2 == 0:
            first = rows
        else:
            both = jnp.concatenate([first.astype(jnp.float32), rows.astype(jnp.float32)], 0)
            both = both.astype(jnp.bfloat16)
            w_edge[pl.ds(part // 2 * ROWS, ROWS), pl.ds(0, LANES)] = both
            w_edge[pl.ds(part // 2 * ROWS, ROWS), pl.ds(LANES, LANES)] = both
    ri, ci = iotas((LANES, 2 * LANES))
    weights = table(jnp.abs(outside_column(ri & 7) - (ci & (LANES - 1)))).astype(jnp.float32)
    plane = (ri >> 3) & (planes - 1)
    for q in range(nz):
        w_join[q] = jnp.where(plane == 2 * q + (ci >> 7), weights, 0.0).astype(jnp.bfloat16)
    ri, ci = iotas((ny, ny))
    w_rows[...] = table(jnp.abs(ri - ci))
    ri, ci = iotas((ROWS, ny))
    weights = table(jnp.abs(jnp.where(ri < SUB, ri - SUB, ri + (ny - SUB)) - ci))
    w_ends[pl.ds(0, ROWS)] = weights
    w_ends[pl.ds(ROWS, ROWS)] = weights

    ri, ci = iotas((planes * SUB, LANES))
    weights = table(jnp.abs(inside_column(ri & 7) - outside_column(ci & 7)), ri >> 3 == (ci >> 3 & (planes - 1)))
    w_back[...] = weights
    same = ri >> 3 == (ci >> 3 & (planes - 1))
    source_column = inside_column(ci & 7)
    w_near[pl.ds(0, planes * SUB)] = table(jnp.abs(inside_column(ri & 7) - source_column), same)
    w_near[pl.ds(planes * SUB, planes * SUB)] = table(jnp.abs(deep_inside(ri & 7) - source_column), same)
    ri, ci = iotas((ny, half))
    w_pairs[...] = ((ri >> 1 == ci) & (ri >= ROWS) & (ri < ny - ROWS)).astype(jnp.float32).astype(jnp.bfloat16)
    ri, ci = iotas((LANES, 2 * nz // 2 * LANES))
    hit = (ri & 63 == (ci & (LANES - 1)) >> 1) & (ri >> 6 == ci >> 8)
    w_pick[...] = hit.astype(jnp.float32).astype(jnp.bfloat16)

    def split(x):
        high = x.astype(jnp.bfloat16)
        return high, (x - high.astype(jnp.float32)).astype(jnp.bfloat16)

    def dot(pieces, weights):
        return jnp.dot(jnp.concatenate(pieces, 1), weights, preferred_element_type=jnp.float32)

    def edges(rows, cells):
        return lax.dot_general(
            w_edge[pl.ds(0, rows)], cells, (((1,), (1,)), ((), ())), preferred_element_type=jnp.float32
        )

    def parts(x):
        return [x[p * ROWS : (p + 1) * ROWS] for p in range(planes)]

    def hand(i, value):
        xs_out[1, pl.ds(4 * i, 4)] = value[:4]
        xs_out[0, pl.ds(4 * i, 4)] = value[4:]

    def handed(i):
        return jnp.concatenate([xs_in[0, pl.ds(4 * i, 4)], xs_in[1, pl.ds(4 * i, 4)]], 0)

    def turned(values):
        values = jnp.concatenate(values, 0)
        first = lax.broadcasted_iota(jnp.int32, (values.shape[0], LANES), 1) < LANES // 2
        high, rest = split(jnp.where(first, values[:, :LANES], values[:, LANES:]))
        both = jnp.concatenate([high.astype(jnp.float32), rest.astype(jnp.float32)], 0)
        return both.T.astype(jnp.bfloat16)

    def y_copies(side, late):
        start = 0 if side == 0 else ny - 4
        padded, bare = pl.ds(PAD + start, 4), pl.ds(start, 4)
        sources = [(now, padded, planes), (mid, padded, planes), (speed, bare, nz)]
        arrive = pl.ds(SUB, 4) if side == 0 else pl.ds(4, 4)
        return [
            pltpu.make_async_remote_copy(
                src_ref=sources[i][0].at[:, sources[i][1], :],
                dst_ref=yin.at[1 - side, pl.ds(planes * i, sources[i][2]), arrive, :],
                send_sem=ysend.at[side, i], recv_sem=yrecv.at[1 - side, i],
                device_id=y_sides[side][1], device_id_type=MESH,
            )
            for i in ((1, 2) if late else (0,))
        ]

    def y_each(late, action):
        for side in range(2):
            @pl.when(y_sides[side][0])
            def _(side=side):
                for copy in y_copies(side if action != "wait_recv" else 1 - side, late):
                    getattr(copy, action)()

    def x_copy(side, part):
        device = x_sides[side][1]
        rows = pl.ds(4 * planes * part, 4 * planes if part < 2 else 4 * nz)
        return pltpu.make_async_remote_copy(
            src_ref=xs_out.at[side, rows], dst_ref=xs_in.at[1 - side, rows],
            send_sem=xsend.at[side, part], recv_sem=xrecv.at[1 - side, part],
            device_id=device, device_id_type=MESH,
        )

    def corner_copy(i):
        return pltpu.make_async_remote_copy(
            src_ref=corner_out.at[i // 2], dst_ref=corner_in.at[3 - i],
            send_sem=csend.at[i], recv_sem=crecv.at[3 - i],
            device_id=diagonal[i][1], device_id_type=MESH,
        )

    body = pl.ds(PAD, ny)
    for f in range(2):
        loads[f].wait()
        for p in range(f * nz, (f + 1) * nz):
            cells = jnp.concatenate(split(now[p, body, :]), 1)
            pieces[p] = cells
            found = edges(2 * ROWS, cells)
            near[p] = found[:SUB]
            bent[p] = found[SUB : 2 * SUB]
            reach[p] = found[2 * SUB : 3 * SUB]
            if p < nz:
                deep_bent[p] = -2.0 * found[3 * SUB :]
            hand(p, found[:SUB])
    upper = jnp.zeros((SUB, LANES), jnp.float32)
    lower = upper
    for p in range(planes):
        shift = (8 * p + 4) % LANES
        upper = jnp.where(group == p, pltpu.roll(now[p, pl.ds(PAD, SUB), :], shift, 1), upper)
        lower = jnp.where(group == p, pltpu.roll(now[p, pl.ds(ny, SUB), :], shift, 1), lower)
    corner_out[0] = upper
    corner_out[1] = lower

    for copy in smalls:
        copy.wait()
    y0, y1, x0, x1 = box[0, 0], box[0, 1], box[0, 2], box[0, 3]
    sz, sy, sx = src[0, 0], src[0, 1], src[0, 2]

    def inside_of(cell_y, cell_x):
        inside = (cell_x >= x0) & (cell_x < x1) & (cell_y >= y0) & (cell_y < y1)
        return inside, (cell_x == sx) & (cell_y == sy)

    def place(at, rows):
        cell_y = gy * ny + at + lax.broadcasted_iota(jnp.int32, (rows, LANES), 0)
        cell_x = gx * LANES + lax.broadcasted_iota(jnp.int32, (rows, LANES), 1)
        return inside_of(cell_y, cell_x)

    def amplitude(step, z):
        return jnp.where(sz == z, wave[0, step], 0.0)

    def vertical(values, p, total):
        z = p % nz
        for k in range(1, 5):
            s = None
            for d in (z + k, z - k):
                if 0 <= d < nz:
                    s = values[p - z + d] if s is None else s + values[p - z + d]
            if s is not None:
                total[k] = s if total[k] is None else total[k] + s
        return total

    def combine(cells, centre, along_x):
        result = []
        for p in range(planes):
            sums = vertical(centre, p, [None] * 5)
            total = along_x[p] + RATIO[0] * centre[p]
            for k in range(1, 5):
                s = cells(p, k) + cells(p, -k)
                if sums[k] is not None:
                    s = s + sums[k]
                total = total + (s if k == 1 else RATIO[k] * s)
            result.append(total)
        return result

    at_y, at_x = iotas((ny, LANES))
    inside, _ = inside_of(gy * ny + at_y, gx * LANES + at_x)
    inner[...] = jnp.where(inside, LEAD, 0.0)
    row, at_y = iotas((SUB, ny))
    edge_inside, edge_source = inside_of(gy * ny + at_y, gx * LANES + inside_column(row))
    at_lane = lax.broadcasted_iota(jnp.int32, (ROWS, LANES), 1)
    loads[2].wait()
    for z in range(nz):
        scaled = speed[z] * inner[...]
        speed[z] = scaled
        found = edges(2 * ROWS, jnp.concatenate(split(scaled), 1))
        deep_held[z] = found[3 * SUB :]
        found = found[:SUB]
        held[z] = found
        hand(planes + z, found)
    tips = [pieces[p, pl.ds(at, ROWS), :] for at in (0, ny - ROWS) for p in range(planes)]
    tips = jnp.dot(jnp.concatenate(tips, 0), w_main[pl.ds(0, 2 * LANES)], preferred_element_type=jnp.float32)
    centre = [near[p] for p in range(planes)]
    high, rest = split(jnp.concatenate(centre, 0))
    along_y = jnp.dot(jnp.concatenate([high, rest], 0), w_rows[...], preferred_element_type=jnp.float32)
    for f in range(2):
        if f == 1:
            pl.semaphore_wait(barrier, expected)
            for i in range(4):
                @pl.when(diagonal[i][0])
                def _(i=i):
                    corner_copy(i).start()
            for side in range(2):
                @pl.when(x_sides[side][0])
                def _(side=side):
                    for part in range(2):
                        x_copy(side, part).start()
            y_each(False, "start")
        loads[3 + f].wait()
        for z in range(nz):
            p = f * nz + z
            before = edges(2 * ROWS if f == 0 else ROWS, jnp.concatenate(split(old[p]), 1))
            if f == 0:
                deep_bent[p] = deep_bent[p] + before[3 * SUB :]
            before = before[:SUB]
            prior[p] = before
            total = bent[p] + RATIO[0] * centre[p]
            total = total + along_y[p * SUB : (p + 1) * SUB]
            total = total + along_y[(planes + p) * SUB : (planes + p + 1) * SUB]
            for k, s in enumerate(vertical(centre, p, [None] * 5)):
                if s is not None:
                    total = total + (s if k == 1 else RATIO[k] * s)
            value = 2.0 * centre[p] - before
            if f == 0:
                value = value + jnp.where(edge_source, amplitude(0, z), 0.0)
            hand(planes + nz + p, jnp.where(edge_inside, value, 0.0) + held[z] * total)
    for side in range(2):
        @pl.when(x_sides[side][0])
        def _(side=side):
            x_copy(side, 2).start()

    def advance(at, along_x):
        inside, source = place(at, ROWS)
        here = pl.ds(at, ROWS)
        cells = lambda p, k: now[p, pl.ds(at + PAD + k, ROWS), :]
        centre = [cells(p, 0) for p in range(planes)]
        lap = combine(cells, centre, along_x)
        scales = [speed[z, here, :] for z in range(nz)]
        for p in range(planes):
            new = 2.0 * centre[p] - old[p, here, :]
            if p < nz:
                new = new + jnp.where(source, amplitude(0, p), 0.0)
            mid[p, pl.ds(at + PAD, ROWS), :] = jnp.where(inside, new, 0.0) + scales[p % nz] * lap[p]

    advance(0, parts(tips[: planes * ROWS]))
    advance(ny - ROWS, parts(tips[planes * ROWS :]))

    y_each(True, "start")


    def first_step(i, carry):
        at = pl.multiple_of(i * ROWS, ROWS)
        advance(at, [along[p, pl.ds(at, ROWS), :] for p in range(planes)])
        return carry

    for p in range(planes):
        along[p] = jnp.dot(pieces[p], w_main[pl.ds(0, 2 * LANES)], preferred_element_type=jnp.float32)
    lax.fori_loop(1, groups - 1, first_step, 0)

    for p in range(planes):
        for v in range(2):
            total = None
            for k in range(1, 5):
                term = RATIO[k] * now[p, pl.ds(k if v == 0 else PAD + ny - k, SUB), :]
                total = term if total is None else total + term
            over[v, p] = total

    for p in range(planes):
        cells = jnp.concatenate(split(mid[p, body, :]), 1)
        along[p] = jnp.dot(cells, w_main[pl.ds(0, 2 * LANES)], preferred_element_type=jnp.float32)
        found = edges(2 * ROWS, cells)
        middle[p] = found[:SUB]
        bent[p] = found[SUB : 2 * SUB]
        if p < nz:
            deep_bent[p] = deep_bent[p] + found[3 * SUB :]
        else:
            deep_late[p - nz] = found[3 * SUB :]

    def twice(at, along_x, keep):
        here, padded = pl.ds(at, ROWS), pl.ds(at + PAD, ROWS)
        inside, source = place(at, ROWS)
        centre = [mid[p, padded, :] for p in range(planes)]
        lap = combine(lambda p, k: mid[p, pl.ds(at + PAD + k, ROWS), :], centre, along_x)
        total = None
        for z in range(nz):
            c = speed[z, here, :]
            f0, f1, a2 = old[z, here, :], now[z, padded, :], now[nz + z, padded, :]
            f2, a1 = centre[z], centre[nz + z]
            f3 = 2.0 * f2 - f1 + jnp.where(source, amplitude(1, z), 0.0)
            f3 = jnp.where(inside, f3, 0.0) + c * lap[z]
            a0 = jnp.where(inside, 2.0 * a1 - a2, 0.0) + c * lap[nz + z]
            part = a0 * (f2 - 2.0 * f1 + f0) + a1 * (f3 - 2.0 * f2 + f1)
            total = part if z % 2 == 0 else total + part
            if z % 2 == 1:
                image[z // 2, here, :] = total if keep is None else jnp.where(keep, total, 0.0)

    keep = (at_lane >= 4) & (at_lane < LANES - 4)

    def second_step(g, carry):
        at = pl.multiple_of(g * ROWS, ROWS)
        twice(at, [along[p, pl.ds(at, ROWS), :] for p in range(planes)], keep)
        return carry

    lax.fori_loop(1, groups - 1, second_step, 0)

    y_each(True, "wait_send")
    for side, (there, _) in enumerate(x_sides):
        @pl.when(there)
        def _(side=side):
            x_copy(1 - side, 0).wait_recv()
    y_each(False, "wait_recv")
    outer = [handed(p) for p in range(planes)]
    lack = jnp.dot(
        w_back[...], jnp.concatenate(split(jnp.concatenate(outer, 0)), 0), preferred_element_type=jnp.float32
    )
    gain = [held[p % nz] * lack[p * SUB : (p + 1) * SUB] for p in range(planes)]
    second = [middle[p] + gain[p] for p in range(planes)]
    spread = jnp.dot(
        w_near[...], jnp.concatenate(split(jnp.concatenate(gain, 0)), 0), preferred_element_type=jnp.float32
    )
    along_y = jnp.dot(
        jnp.concatenate(split(jnp.concatenate(second, 0)), 0), w_rows[...], preferred_element_type=jnp.float32
    )
    for p in range(planes):
        total = bent[p] + spread[p * SUB : (p + 1) * SUB] + RATIO[0] * second[p]
        total = total + along_y[p * SUB : (p + 1) * SUB]
        total = total + along_y[(planes + p) * SUB : (planes + p + 1) * SUB]
        for k, s in enumerate(vertical(second, p, [None] * 5)):
            if s is not None:
                total = total + (s if k == 1 else RATIO[k] * s)
        bent[p] = total
        middle[p] = second[p]
    deep = []
    for z in range(nz):
        f = spread[(planes + z) * SUB : (planes + z + 1) * SUB]
        a = spread[(planes + nz + z) * SUB : (planes + nz + z + 1) * SUB]
        deep.append(deep_held[z] * (a * deep_bent[z] + deep_late[z] * f))
    deep_sums[...] = jnp.concatenate([deep[2 * k] + deep[2 * k + 1] for k in range(nz // 2)], 0)

    span = 2 * ROWS
    columns = turned(outer)
    columns = jnp.concatenate([columns[:span], columns[LANES - span :]], 0)
    for q in range(nz):
        lack = jnp.dot(columns, w_join[q], preferred_element_type=jnp.float32)
        for side in range(2):
            p = 2 * q + side
            for v, at in enumerate((0, ny - span)):
                here = pl.ds(PAD + at, span)
                part = lack[v * span : (v + 1) * span, side * LANES : (side + 1) * LANES]
                mid[p, here, :] = mid[p, here, :] + speed[p % nz, pl.ds(at, span), :] * part
    for p in range(planes):
        for v in range(2):
            total = None
            for k in range(1, 5):
                term = RATIO[k] * yin[v, p, pl.ds(SUB - k if v == 0 else k, SUB), :]
                total = term if total is None else total + term
            at = 0 if v == 0 else ny - SUB
            here = pl.ds(PAD + at, SUB)
            mid[p, here, :] = mid[p, here, :] + speed[p % nz, pl.ds(at, SUB), :] * total
    tips = [mid[p, pl.ds(PAD + at, ROWS), :] for at in (0, ny - ROWS) for p in range(planes)]
    tips = dot(split(jnp.concatenate(tips, 0)), w_main[pl.ds(0, 2 * LANES)])
    for v in range(2):
        for p in range(planes):
            at = (v * planes + p) * ROWS
            along[p, pl.ds(v * ROWS, ROWS), :] = tips[at : at + ROWS]

    for side, (there, _) in enumerate(x_sides):
        @pl.when(there)
        def _(side=side):
            for part in (1, 2):
                x_copy(1 - side, part).wait_recv()
    y_each(True, "wait_recv")
    for i in range(4):
        @pl.when(diagonal[i][0])
        def _(i=i):
            corner_copy(3 - i).wait_recv()
    halves = [jnp.where(low, corner_in[2 * v], corner_in[2 * v + 1]) for v in range(2)]
    masked = [jnp.where(group == p, halves[v], 0.0) for v in range(2) for p in range(planes)]
    halo = dot(split(jnp.concatenate(masked, 0)), w_main[pl.ds(2 * LANES, 2 * LANES)])
    high, rest = split(jnp.concatenate(halves, 0))
    ends = lax.dot_general(
        jnp.concatenate([high, rest], 0), w_ends[...], (((0,), (0,)), ((), ())),
        preferred_element_type=jnp.float32,
    )
    for p in range(planes):
        for v in range(2):
            at = (v * planes + p) * SUB
            over[v, p] = over[v, p] + halo[at : at + SUB]
    outer = [handed(planes + nz + p) + handed(planes + p % nz) * reach[p] for p in range(planes)]
    lack = jnp.dot(
        w_back[...], jnp.concatenate(split(jnp.concatenate(outer, 0)), 0), preferred_element_type=jnp.float32
    )
    columns = turned(
        [outer[p] + handed(planes + p % nz) * ends[p * SUB : (p + 1) * SUB] for p in range(planes)]
    )
    columns = jnp.concatenate([columns[:ROWS], columns[LANES - ROWS :]], 0)
    found = [jnp.dot(columns, w_join[q], preferred_element_type=jnp.float32) for q in range(nz)]
    for v in range(2):
        here = pl.ds(0 if v == 0 else PAD + ny, SUB)
        rows = pl.ds(0 if v == 0 else SUB, SUB)
        for p in range(planes):
            mid[p, here, :] = yin[v, planes + p, rows, :] + yin[v, 2 * planes + p % nz, rows, :] * over[v, p]
    for v, at in enumerate((0, ny - ROWS)):
        here = pl.ds(v * ROWS, ROWS)
        twice(
            at,
            [
                along[p, here, :]
                + found[p // 2][v * ROWS : (v + 1) * ROWS, p % 2 * LANES : (p % 2 + 1) * LANES]
                for p in range(planes)
            ],
            None,
        )
    fixes = []
    for z in range(nz):
        f2, a1 = middle[z], middle[nz + z]
        f1, a2 = near[z], near[nz + z]
        f3 = 2.0 * f2 - f1 + jnp.where(edge_source, amplitude(1, z), 0.0)
        f3 = jnp.where(edge_inside, f3, 0.0) + held[z] * (bent[z] + lack[z * SUB : (z + 1) * SUB])
        a0 = jnp.where(edge_inside, 2.0 * a1 - a2, 0.0)
        a0 = a0 + held[z] * (bent[nz + z] + lack[(nz + z) * SUB : (nz + z + 1) * SUB])
        fixes.append(a0 * (f2 - 2.0 * f1 + prior[z]) + a1 * (f3 - 2.0 * f2 + f1))
    fixes = jnp.concatenate([fixes[2 * k] + fixes[2 * k + 1] for k in range(nz // 2)] + [deep_sums[...]], 0)
    both = jnp.dot(jnp.concatenate(split(fixes), 0), w_pairs[...], preferred_element_type=jnp.float32)
    fixes = both[: nz * SUB] + both[nz * SUB :]
    patch[...] = fixes

    rows = [
        image[k, pl.ds(0, half, stride=2), :] + image[k, pl.ds(1, half, stride=2), :] for k in range(nz // 2)
    ]
    cells = jnp.concatenate([x for k in range(nz // 2) for x in split(rows[k])], 1)
    total = lax.dot_general(
        w_pick[...], cells, (((1,), (1,)), ((), ())), preferred_element_type=jnp.float32
    )
    coarse[...] = total

    def exchange(ref, into, lane_of):
        copies = []
        for step in range(1, shots):
            copy = pltpu.make_async_remote_copy(
                src_ref=ref, dst_ref=into.at[step - 1],
                send_sem=shot_send.at[lane_of, step - 1], recv_sem=shot_recv.at[lane_of, step - 1],
                device_id={"shot": lax.rem(shot + step, shots)}, device_id_type=MESH,
            )
            copy.start()
            copies.append(copy)
        return copies

    sends = exchange(coarse, arrived, 0)

    sends = sends + exchange(patch, patches, 1)

    y_each(False, "wait_send")
    for side in range(2):
        @pl.when(x_sides[side][0])
        def _(side=side):
            for part in range(3):
                x_copy(side, part).wait_send()
    for i in range(4):
        @pl.when(diagonal[i][0])
        def _(i=i):
            corner_copy(i).wait_send()
    for copy in sends:
        copy.wait_recv()
    for step in range(shots - 1):
        total = total + arrived[step]
        fixes = fixes + patches[step]
    depth = top[0].astype(jnp.float32)
    width = LANES // 2
    for k in range(nz // 2):
        factor = (0.25 + (depth + (2.0 * k + 1.0)) / 128.0) * 0.125
        out_ref[k] = total[width * k : width * k + width] * factor
        for i, at in enumerate((width - 2, width - 1, 0, 1, width - 4, width - 3, 2, 3)):
            first = (k + i // 4 * (nz // 2)) * SUB + 2 * (i % 4)
            row = (fixes[first : first + 1] + fixes[first + 1 : first + 2]) * factor
            out_ref[k, pl.ds(at, 1), :] = out_ref[k, pl.ds(at, 1), :] + row
    for copy in sends:
        copy.wait_send()


def per_device(shots, counts, fwd_prev, fwd_cur, adj_late, adj_now, courant, wavelet, boxes, sources, slab_top):
    nz, ny, nx = courant.shape
    f32, b16 = jnp.float32, jnp.bfloat16
    planes = 2 * nz
    others = max(shots - 1, 1)
    hbm = pl.BlockSpec(memory_space=pltpu.HBM)
    dma = pltpu.SemaphoreType.DMA
    smalls = [pltpu.with_memory_space_constraint(x, pltpu.HBM) for x in (wavelet, boxes, sources)]
    out = pl.pallas_call(
        functools.partial(kernel, shots, counts),
        out_shape=jax.ShapeDtypeStruct((nz // 2, nx // 2, ny // 2), f32),
        in_specs=[hbm] * 9,
        out_specs=pl.BlockSpec(memory_space=pltpu.VMEM),
        scratch_shapes=[
            pltpu.SMEM((1, 2), f32),
            pltpu.SMEM((1, 4), jnp.int32),
            pltpu.SMEM((1, 3), jnp.int32),
            pltpu.SMEM((1,), jnp.int32),
            pltpu.VMEM((planes, ny + 2 * PAD, nx), f32),
            pltpu.VMEM((planes, ny + 2 * PAD, nx), f32),
            pltpu.VMEM((planes, ny, nx), f32),
            pltpu.VMEM((nz, ny, nx), f32),
            pltpu.VMEM((nz // 2, ny, nx), f32),
            pltpu.VMEM((ny, nx), f32),
            pltpu.VMEM((2, 2 * planes + nz, ROWS, nx), f32),
            pltpu.VMEM((2, planes, SUB, nx), f32),
            pltpu.VMEM((planes, ny, 2 * nx), b16),
            pltpu.VMEM((planes, ny, nx), f32),
            pltpu.VMEM((planes, SUB, ny), f32),
            pltpu.VMEM((planes, SUB, ny), f32),
            pltpu.VMEM((planes, SUB, ny), f32),
            pltpu.VMEM((planes, SUB, ny), f32),
            pltpu.VMEM((nz, SUB, ny), f32),
            pltpu.VMEM((planes, SUB, ny), f32),
            pltpu.VMEM((nz, SUB, ny), f32),
            pltpu.VMEM((nz, SUB, ny), f32),
            pltpu.VMEM((nz, SUB, ny), f32),
            pltpu.VMEM((nz // 2 * SUB, ny), f32),
            pltpu.VMEM((2, 4 * (2 * planes + nz), ny), f32),
            pltpu.VMEM((2, 4 * (2 * planes + nz), ny), f32),
            pltpu.VMEM((2, SUB, nx), f32),
            pltpu.VMEM((4, SUB, nx), f32),
            pltpu.VMEM((4 * nx, nx), b16),
            pltpu.VMEM((2 * ROWS, 2 * nx), b16),
            pltpu.VMEM((nz, nx, 2 * nx), b16),
            pltpu.VMEM((ny, ny), b16),
            pltpu.VMEM((2 * ROWS, ny), b16),
            pltpu.VMEM((planes * SUB, nx), b16),
            pltpu.VMEM((2 * planes * SUB, nx), b16),
            pltpu.VMEM((ny, ny // 2), b16),
            pltpu.VMEM((nx, nz * nx), b16),
            pltpu.VMEM((nx, ny // 2), f32),
            pltpu.VMEM((others, nx, ny // 2), f32),
            pltpu.VMEM((nz * SUB, ny // 2), f32),
            pltpu.VMEM((others, nz * SUB, ny // 2), f32),
            dma((4,)),
            dma((5,)),
            dma((2, 3)),
            dma((2, 3)),
            dma((2, 3)),
            dma((2, 3)),
            dma((4,)),
            dma((4,)),
            dma((2, others)),
            dma((2, others)),
        ],
        compiler_params=pltpu.CompilerParams(
            collective_id=0, has_side_effects=True, vmem_limit_bytes=54912 * 1024
        ),
    )(*smalls, slab_top, fwd_prev, fwd_cur, adj_late, adj_now, courant)
    return jnp.swapaxes(out, 1, 2)


def solution(mesh):
    shots = mesh.shape["shot"]
    counts = (mesh.shape["gy"], mesh.shape["gx"])
    return jax.shard_map(
        functools.partial(per_device, shots, counts),
        mesh=mesh,
        in_specs=(
            P("shot", None, "gy", "gx"),
            P("shot", None, "gy", "gx"),
            P("shot", None, "gy", "gx"),
            P("shot", None, "gy", "gx"),
            P(None, "gy", "gx"),
            P("shot", None),
            P("shot", None),
            P("shot", None),
            P(),
        ),
        out_specs=P(None, "gy", "gx"),
        check_vma=False,
    )
```
